512 devices in a mesh: grid: 128 (over z, x_hi, y), spec: 4 (over x_lo, core).
Axes of the slice: x: 4 (x_hi: 2, x_lo: 2; x = x_hi * 2 + x_lo), y: 8, z: 8, core: 2. Of those that a mesh axis runs over, the one named last changes fastest.
Arguments:
- energy: float32 [36, 36, 512, 128], P('spec', None, 'grid'), may hold values from 0.05 to 1
- nest_energy: float32 [36, 36, 512, 128], P('spec', None, 'grid'), may hold values from 0.05 to 1
- ocean_mask: int32 [512, 128], P('grid'), may hold values 0 or 1
- wind_field: float32 [2, 512, 128], P(None, 'grid'), may hold values from -6 to 6
- rim_cell: int32 [16384, 2], P('grid'), may hold values from 0 to 511, as said below
- rim_dest: int32 [16384, 1], P('grid'), may hold values from 0 to 127; in each aligned block of 128 rows (0 to 127, 128 to 255, ...) at most 2 rows name the same one
- rim_target: int32 [16384], P('grid'), may hold values from 0 to 511
- rim_weight: float32 [16384, 3], P('grid'), may hold values from 0.1 to 0.9
Outputs:
- global_next: float32 [36, 36, 512, 128], P('spec', None, 'grid')
- nest_next: float32 [36, 36, 512, 128], P('spec', None, 'grid')
The draws below stay inside these ranges and needn't reach their ends.
Inputs may be any that keep to these rules, and one draw needn't show every extreme that they name: `rim_cell`: rows of device g of the grid axis have column 0 between g * 4 and (g + 1) * 4 - 1; column 1 is at most 126. `rim_dest`: the 128 rows of one device name any one nest device at most 2 times, and some device's rows name one exactly 2 times.
All inputs are finite; a program needn't handle non-finite values. No bound on the sum of `ocean_mask` on one device may be relied on, other than what follows from the above.
Results may differ from the reference program's by a relative error of at most 0.003.
Values may be sent and summed in bfloat16 or wider, within the bound.
A program may use at most 64 MiB of HBM per device.

```python
import math
import jax
import jax.numpy as jnp
import numpy as np
from jax import lax

FREQS = 36
ANGLES = 36
LON_DEV = 4
LAT_ROWS = 128
RIM_DEV = 128
LON_ALL = 512
CELL_DEV = 512
RIM_ALL = 16384
SLOT_CAP = 2
N_GRID = 128


def draw_rim_cell(key, part):
    key_lon = jax.random.fold_in(key, 11)
    key_lat = jax.random.fold_in(key, 12)
    row_ids = jnp.arange(RIM_ALL, dtype=jnp.int32)
    local_rank = row_ids % RIM_DEV
    local_col = jnp.minimum(jax.random.randint(key_lon, (RIM_ALL,), 0, 2 * LON_DEV, dtype=jnp.int32), LON_DEV - 1)
    local_col = jnp.where(local_rank == RIM_DEV - 1, LON_DEV - 1, local_col)
    local_col = jnp.where(row_ids == 0, 0, local_col)
    rim_lon = row_ids // RIM_DEV * LON_DEV + local_col
    rim_lat = jax.random.randint(key_lat, (RIM_ALL,), 0, LAT_ROWS - 1, dtype=jnp.int32)
    rim_lat = jnp.where(local_rank == 0, LAT_ROWS - 2, rim_lat)
    return jnp.stack([rim_lon, rim_lat], axis=1).astype(jnp.int32)


def set_ends(entries, key, low, top_value):
    place = [jax.random.randint(jax.random.fold_in(key, axis), (), 0, length) for axis, length in enumerate(entries.shape)]
    longest = entries.shape.index(max(entries.shape))
    neighbour = place[:longest] + [(place[longest] + 1) % entries.shape[longest]] + place[longest + 1:]
    return entries.at[tuple(place)].set(low).at[tuple(neighbour)].set(top_value)


def shard_levels(key, extent, shards, low, largest):
    gain = 1.0
    for dim, blocks in shards:
        steps = jax.random.uniform(jax.random.fold_in(jax.random.fold_in(key, 6), dim), (blocks,), jnp.float32, low / len(shards), largest / len(shards))
        gain = gain * jnp.repeat(jnp.exp(steps), extent[dim] // blocks).reshape((-1,) + (1,) * (len(extent) - 1 - dim))
    return gain


def routed_block(key, own, number, rows, count, top, limit, skew):
    sequence = jax.random.permutation(key, count)
    packed, ordinary = portions_of(count, rows * top, limit, skew, True), portions_of(count, rows * top, limit, skew, False)
    places = jnp.arange(count)

    def named(lengths, turn):
        used = int((lengths > 0).sum())
        fixed = max(1, used // 4)
        moved = fixed + (places - fixed + turn * (used - fixed)) % max(1, count - fixed)
        return jnp.zeros((count,), jnp.int32).at[sequence[jnp.where(places < fixed, places, moved)]].set(jnp.asarray(lengths, jnp.int32))

    lengths = jnp.where(number % 4 == 0, named(packed, number // 4), named(ordinary, number - number // 4 - 1))
    mixed = jax.random.permutation(jax.random.fold_in(own, 3), count)
    donor, receiver = mixed[0:count // 2 * 2:2], mixed[1:count // 2 * 2:2]
    room = jnp.minimum(lengths[donor] - 1, limit - lengths[receiver]) // 2
    room = jnp.where((donor == sequence[0]) | (receiver == sequence[0]) | (lengths[receiver] == 0), 0, jnp.maximum(room, 0))
    moved = jax.random.randint(jax.random.fold_in(own, 4), (count // 2,), 0, 1 << 20) % (room + 1)
    lengths = lengths.at[donor].add(-moved).at[receiver].add(moved)
    members = jnp.searchsorted(jnp.cumsum(lengths), jnp.arange(rows * top), side="right").astype(jnp.int32)
    grid = members.reshape(top, rows).T
    grid = grid[jax.random.permutation(jax.random.fold_in(own, 1), rows)]
    turn = jax.random.randint(jax.random.fold_in(own, 2), (rows, 1), 0, top)
    return jnp.take_along_axis(grid, (jnp.arange(top)[None, :] + turn) % top, axis=1)


def portions_of(count, total, most, slope, full):
    loads = [(1 << 20) // math.isqrt(grade ** slope) + 1 for grade in range(1, count + 1)]
    largest = most if full else min(most, max(-(-total // count), total * loads[0] // sum(loads)))
    least = 1 if total - largest >= count - 1 else 0
    counts, spare = [largest] + [least] * (count - 1), total - largest - least * (count - 1)
    while spare > 0:
        free = [i for i in range(1, count) if counts[i] < largest] or [i for i in range(1, count) if counts[i] < most]
        whole, remaining = sum([loads[i] for i in free]), spare
        for i in free:
            more = min(most - counts[i], max(1, remaining * loads[i] // whole), spare)
            counts[i] = counts[i] + more
            spare = spare - more
    return np.array(counts)


def scatter_about(stream_key, dims, deviation, most, pieces=(), kind=jnp.bfloat16):
    entries = jax.random.normal(stream_key, dims, jnp.float32) * deviation
    if len(pieces) > 0:
        entries = shard_levels(stream_key, dims, pieces, -0.22, 0.18) * entries
    return jnp.clip(entries, min=-most, max=most).astype(kind)


def setup_inputs(seed: int = 0) -> dict:
    streams_of = jax.random.split(jax.random.key(seed), 9)
    energy = jnp.clip(jnp.exp(math.log(1.0) - 2.9957323 * jax.random.uniform(streams_of[0], (FREQS, ANGLES, LON_ALL, LAT_ROWS), jnp.float32) ** shard_levels(streams_of[0], (FREQS, ANGLES, LON_ALL, LAT_ROWS), ((0, 4), (2, 128)), -0.2, 0.2)), 0.05, 1.0)
    nest_energy = jnp.clip(jnp.exp(math.log(1.0) - 2.9957323 * jax.random.uniform(streams_of[1], (FREQS, ANGLES, LON_ALL, LAT_ROWS), jnp.float32) ** shard_levels(streams_of[1], (FREQS, ANGLES, LON_ALL, LAT_ROWS), ((0, 4), (2, 128)), -0.2, 0.2)), 0.05, 1.0)
    ocean_mask = set_ends((jax.random.randint(streams_of[2], (LON_ALL, LAT_ROWS), 0, 4) < 3).astype(jnp.int32), jax.random.fold_in(streams_of[2], 1), 0, 1)
    wind_field = scatter_about(streams_of[3], (2, LON_ALL, LAT_ROWS), 1.0, 6.0, ((1, 128),), jnp.float32)
    rim_cell = draw_rim_cell(jax.random.fold_in(streams_of[8], 71), 0)
    rim_dest_keys = jax.random.split(jax.random.fold_in(streams_of[5], 1), RIM_ALL // RIM_DEV)
    rim_dest_turns = jax.random.permutation(jax.random.fold_in(streams_of[5], 3), RIM_ALL // RIM_DEV)
    rim_dest = jax.vmap(lambda own, number: routed_block(jax.random.fold_in(streams_of[5], 2), own, number, RIM_DEV, N_GRID, 1, SLOT_CAP, 2))(rim_dest_keys, rim_dest_turns).reshape((RIM_ALL, 1))
    rim_target = set_ends(jax.random.randint(streams_of[6], (RIM_ALL,), 0, CELL_DEV), jax.random.fold_in(streams_of[6], 1), 0, CELL_DEV - 1).astype(jnp.int32)
    rim_weight = jnp.clip(0.1 + 0.79999997 * jax.random.uniform(streams_of[7], (RIM_ALL, 3), jnp.float32) ** shard_levels(streams_of[7], (RIM_ALL, 3), ((0, 128),), -0.2, 0.2), 0.1, 0.9)
    return {"energy": energy, "nest_energy": nest_energy, "ocean_mask": ocean_mask, "wind_field": wind_field, "rim_cell": rim_cell, "rim_dest": rim_dest, "rim_target": rim_target, "rim_weight": rim_weight}


ratio_step = 1.1
speed_coef = 0.054
wind_coef = 0.05
dissip_coef = 0.2
nonlin_coef = 0.12
nest_speedup = 2.0
band_reach = 5


def freq_ratio(first_band, band_count):
    band_ranks = jnp.asarray(first_band).astype(jnp.float32) + jnp.arange(band_count).astype(jnp.float32)
    return jnp.power(jnp.float32(ratio_step), band_ranks - FREQS // 2)


def lat_secant(lat_rows):
    lat_degrees = -60.0 + 120.0 * (jnp.arange(lat_rows).astype(jnp.float32) + 0.5) / lat_rows
    return 1.0 / jnp.cos(lat_degrees * (jnp.pi / 180.0))


def headings():
    return 2.0 * jnp.pi * jnp.arange(ANGLES).astype(jnp.float32) / ANGLES


def courant_pair(ratios, lat_scale, speedup):
    group_speed = speedup * speed_coef / ratios
    heading = headings()
    along_lon = group_speed[:, None, None, None] * jnp.cos(heading)[None, :, None, None] * lat_scale[None, None, None, :]
    along_lat = group_speed[:, None, None, None] * jnp.sin(heading)[None, :, None, None]
    return along_lon, along_lat


def advect(padded, along_lon, along_lat):
    center = padded[:, :, 1:-1]
    west_cells = padded[:, :, :-2]
    east_cells = padded[:, :, 2:]
    zeros_row = jnp.zeros_like(center[..., :1])
    south_cells = jnp.concatenate([zeros_row, center[..., :-1]], axis=3)
    north_cells = jnp.concatenate([center[..., 1:], zeros_row], axis=3)
    flux_lon = jnp.maximum(along_lon, 0.0) * (center - west_cells) + jnp.minimum(along_lon, 0.0) * (east_cells - center)
    flux_lat = jnp.maximum(along_lat, 0.0) * (center - south_cells) + jnp.minimum(along_lat, 0.0) * (north_cells - center)
    return center - flux_lon - flux_lat


def nonlinear(banded, ratios_padded):
    band_count = banded.shape[0] - 2 * band_reach
    centre = banded[3:band_count + 8]
    strength = nonlin_coef * ratios_padded[3:band_count + 8][:, None, None, None]
    result = jnp.zeros_like(banded[band_reach:band_reach + band_count])
    for mirror in (1, -1):
        upper_pair = jnp.roll(banded[5:band_count + 10], -3 * mirror, axis=1)
        lower_pair = jnp.roll(banded[0:band_count + 5], mirror, axis=1)
        transfer = strength * (centre * centre * (upper_pair + lower_pair) - 2.0 * centre * upper_pair * lower_pair)
        result = result - 2.0 * transfer[2:band_count + 2] + jnp.roll(transfer[0:band_count], 3 * mirror, axis=1) + jnp.roll(transfer[5:band_count + 5], -mirror, axis=1)
    return result


def step_sources(advected, banded, ratios, ratios_padded, wind_block, mean_energy):
    heading = headings()
    along_wind = jnp.maximum(wind_block[0][None, None] * jnp.cos(heading)[None, :, None, None] + wind_block[1][None, None] * jnp.sin(heading)[None, :, None, None], 0.0)
    wind_gain = wind_coef * ratios[:, None, None, None] * along_wind * advected
    transfer = nonlinear(banded, ratios_padded)
    return (advected + wind_gain + transfer) / (1.0 + dissip_coef * (ratios * ratios)[:, None, None, None] * mean_energy[None, None])


def interpolate(spectra_flat, base_cell, east_cell, rim_weight):
    east_share = rim_weight[:, 0]
    north_share = rim_weight[:, 1]
    corner_sw = jnp.take(spectra_flat, base_cell, axis=1)
    corner_nw = jnp.take(spectra_flat, base_cell + 1, axis=1)
    corner_se = jnp.take(spectra_flat, east_cell, axis=1)
    corner_ne = jnp.take(spectra_flat, east_cell + 1, axis=1)
    mixed = (1.0 - east_share) * (1.0 - north_share) * corner_sw + (1.0 - east_share) * north_share * corner_nw
    mixed = mixed + east_share * (1.0 - north_share) * corner_se + east_share * north_share * corner_ne
    return mixed.astype(jnp.bfloat16)


def global_tile(tile_block, mask_block, wind_block):
    ratios = freq_ratio(0, FREQS)
    along_lon, along_lat = courant_pair(ratios, lat_secant(LAT_ROWS), 1.0)
    advected = advect(tile_block, along_lon, along_lat) * mask_block.astype(jnp.float32)
    band_weight = 0.1 * ratios
    partial_value = jnp.sum(band_weight[:, None, None, None] * advected, axis=(0, 1))
    mean_energy = partial_value / (ANGLES * (0.1 * jnp.sum(freq_ratio(0, FREQS))))
    banded = jnp.pad(advected, ((band_reach, band_reach), (0, 0), (0, 0), (0, 0)))
    ratios_padded = freq_ratio(-band_reach, FREQS + 2 * band_reach)
    return step_sources(advected, banded, ratios, ratios_padded, wind_block, mean_energy)


def reference(energy, nest_energy, ocean_mask, wind_field, rim_cell, rim_dest, rim_target, rim_weight):
    padded = jnp.concatenate([energy[:, :, -1:], energy, energy[:, :, :1]], axis=2)

    def one_tile(tile_index):
        offset = tile_index * LON_DEV
        tile_block = lax.dynamic_slice_in_dim(padded, offset, LON_DEV + 2, 2)
        mask_block = lax.dynamic_slice_in_dim(ocean_mask, offset, LON_DEV, 0)
        wind_block = lax.dynamic_slice_in_dim(wind_field, offset, LON_DEV, 1)
        return global_tile(tile_block, mask_block, wind_block)

    tile_stack = lax.map(one_tile, jnp.arange(N_GRID, dtype=jnp.int32))
    global_next = jnp.moveaxis(tile_stack, 0, 2).reshape(FREQS, ANGLES, LON_ALL, LAT_ROWS)

    spectra_flat = global_next.reshape(FREQS * ANGLES, LON_ALL * LAT_ROWS)
    rim_lon = rim_cell[:, 0]
    rim_lat = rim_cell[:, 1]
    base_cell = rim_lon * LAT_ROWS + rim_lat
    east_cell = ((rim_lon + 1) % LON_ALL) * LAT_ROWS + rim_lat
    boundary = interpolate(spectra_flat, base_cell, east_cell, rim_weight)

    ratios = freq_ratio(0, FREQS)
    nest_lon, nest_lat = courant_pair(ratios, jnp.ones((LAT_ROWS,), jnp.float32), nest_speedup)
    half_cols = LON_ALL // 2
    quarter_cols = LON_ALL // 4
    rolled = jnp.roll(nest_energy, -quarter_cols, axis=2)
    halves = []
    for half_index in range(2):
        piece_cols = rolled[:, :, half_index * half_cols:(half_index + 1) * half_cols]
        piece_padded = jnp.pad(piece_cols, ((0, 0), (0, 0), (1, 1), (0, 0)))
        halves.append(advect(piece_padded, nest_lon, nest_lat))
    nest_cols = jnp.roll(jnp.concatenate(halves, axis=2), quarter_cols, axis=2)
    nest_flat = nest_cols.reshape(FREQS * ANGLES, LON_ALL * LAT_ROWS)
    nest_cell = rim_dest[:, 0] * CELL_DEV + rim_target
    picked = jnp.take(nest_flat, nest_cell, axis=1)
    increment = rim_weight[:, 2][None, :] * (boundary.astype(jnp.float32) - picked)
    nest_next = nest_flat.at[:, nest_cell].add(increment).reshape(FREQS, ANGLES, LON_ALL, LAT_ROWS)
    return global_next, nest_next
```

```python
import functools

import jax
import jax.numpy as jnp
from jax import lax
from jax.experimental import pallas as pl
from jax.experimental.pallas import tpu as pltpu
from jax.sharding import PartitionSpec as P

FREQS = 36
ANGLES = 36


ratio_step = 1.1
speed_coef = 0.054
wind_coef = 0.05
dissip_coef = 0.2
nonlin_coef = 0.12
nest_speedup = 2.0
band_reach = 5
SLOTS = 2
MESH = pl.DeviceIdType.MESH


def extended_2(x, sides, width, wrap):
    for axis, dim in sides:
        peers, length = (lax.axis_size(axis), x.shape[dim])
        up = [(i, (i + 1) % peers) for i in range(peers if wrap else peers - 1)]
        down = [(j, i) for i, j in up]
        last = lax.slice_in_dim(x, length - width, length, axis=dim)
        leading = lax.slice_in_dim(x, 0, width, axis=dim)
        before = lax.ppermute(last, axis, up)
        after = lax.ppermute(leading, axis, down)
        x = jnp.concatenate([before, x, after], axis=dim)
    return x


def passed_along(block, axis, distance):
    devices = range(lax.axis_size(axis))
    route = [((i - distance) % len(devices), i) for i in devices]
    return lax.ppermute(block, axis, route)


def freq_ratio(first_band, band_count):
    band_ranks = jnp.asarray(first_band).astype(jnp.float32) + jnp.arange(band_count).astype(
        jnp.float32
    )
    return jnp.power(jnp.float32(ratio_step), band_ranks - FREQS // 2)


def lat_secant(lat_rows):
    lat_degrees = -60.0 + 120.0 * (jnp.arange(lat_rows).astype(jnp.float32) + 0.5) / lat_rows
    return 1.0 / jnp.cos(lat_degrees * (jnp.pi / 180.0))


def headings():
    return 2.0 * jnp.pi * jnp.arange(ANGLES).astype(jnp.float32) / ANGLES


def courant_pair(ratios, lat_scale, speedup):
    group_speed = speedup * speed_coef / ratios
    heading = headings()
    along_lon = (
        group_speed[:, None, None, None]
        * jnp.cos(heading)[None, :, None, None]
        * lat_scale[None, None, None, :]
    )
    along_lat = group_speed[:, None, None, None] * jnp.sin(heading)[None, :, None, None]
    return (along_lon, along_lat)


def advect(padded, along_lon, along_lat):
    center = padded[:, :, 1:-1]
    west_cells = padded[:, :, :-2]
    east_cells = padded[:, :, 2:]
    zeros_row = jnp.zeros_like(center[..., :1])
    south_cells = jnp.concatenate([zeros_row, center[..., :-1]], axis=3)
    north_cells = jnp.concatenate([center[..., 1:], zeros_row], axis=3)
    flux_lon = jnp.maximum(along_lon, 0.0) * (center - west_cells) + jnp.minimum(along_lon, 0.0) * (
        east_cells - center
    )
    flux_lat = jnp.maximum(along_lat, 0.0) * (center - south_cells) + jnp.minimum(
        along_lat, 0.0
    ) * (north_cells - center)
    return center - flux_lon - flux_lat


def nonlinear(banded, ratios_padded):
    band_count = banded.shape[0] - 2 * band_reach
    centre = banded[3 : band_count + 8]
    strength = nonlin_coef * ratios_padded[3 : band_count + 8][:, None, None, None]
    result = jnp.zeros_like(banded[band_reach : band_reach + band_count])
    for mirror in (1, -1):
        upper_pair = jnp.roll(banded[5 : band_count + 10], -3 * mirror, axis=1)
        lower_pair = jnp.roll(banded[0 : band_count + 5], mirror, axis=1)
        transfer = strength * (
            centre * centre * (upper_pair + lower_pair) - 2.0 * centre * upper_pair * lower_pair
        )
        result = (
            result
            - 2.0 * transfer[2 : band_count + 2]
            + jnp.roll(transfer[0:band_count], 3 * mirror, axis=1)
            + jnp.roll(transfer[5 : band_count + 5], -mirror, axis=1)
        )
    return result


def step_sources(advected, banded, ratios, ratios_padded, wind_block, mean_energy):
    heading = headings()
    along_wind = jnp.maximum(
        wind_block[0][None, None] * jnp.cos(heading)[None, :, None, None]
        + wind_block[1][None, None] * jnp.sin(heading)[None, :, None, None],
        0.0,
    )
    wind_gain = wind_coef * ratios[:, None, None, None] * along_wind * advected
    transfer = nonlinear(banded, ratios_padded)
    return (advected + wind_gain + transfer) / (
        1.0 + dissip_coef * (ratios * ratios)[:, None, None, None] * mean_energy[None, None]
    )


def exchange_kernel(count, send_ref, recv_ref, send_sem, recv_sem):
    me = lax.axis_index("grid")
    barrier = pltpu.get_barrier_semaphore()

    def peer(i):
        return lax.rem(me + i, count)

    def greet(i, carry):
        pl.semaphore_signal(barrier, inc=1, device_id={"grid": peer(i)}, device_id_type=MESH)
        return carry

    lax.fori_loop(1, count, greet, 0)
    pl.semaphore_wait(barrier, count - 1)
    own = pltpu.make_async_copy(send_ref.at[me], recv_ref.at[me], recv_sem)
    own.start()

    def post(i, carry):
        dest = peer(i)
        pltpu.make_async_remote_copy(
            src_ref=send_ref.at[dest],
            dst_ref=recv_ref.at[me],
            send_sem=send_sem,
            recv_sem=recv_sem,
            device_id={"grid": dest},
            device_id_type=MESH,
        ).start()
        return carry

    lax.fori_loop(1, count, post, 0)
    others = send_ref.at[pl.ds(0, count - 1)]
    pltpu.make_async_copy(others, others, send_sem).wait()
    pltpu.make_async_copy(recv_ref, recv_ref, recv_sem).wait()


def exchange(blocks):
    count = blocks.shape[0]
    return pl.pallas_call(
        functools.partial(exchange_kernel, count),
        out_shape=jax.ShapeDtypeStruct(blocks.shape, blocks.dtype),
        in_specs=[pl.BlockSpec(memory_space=pltpu.VMEM)],
        out_specs=pl.BlockSpec(memory_space=pltpu.VMEM),
        scratch_shapes=[pltpu.SemaphoreType.DMA, pltpu.SemaphoreType.DMA],
        compiler_params=pltpu.CompilerParams(collective_id=0, has_side_effects=True),
        name="rim_exchange",
    )(blocks)


def split_16(x):
    high = lax.reduce_precision(x, 8, 7)
    return high, x - high


def per_device(
    energy, nest_energy, ocean_mask, wind_field, rim_cell, rim_dest, rim_target, rim_weight
):
    grid_rank = lax.axis_index("grid")
    grid_count = lax.axis_size("grid")
    quarter_count = grid_count // 4
    bands_dev = energy.shape[0]
    lon_dev = energy.shape[2]
    lat_rows = energy.shape[3]
    bin_count = bands_dev * ANGLES
    first_band = lax.axis_index("spec") * bands_dev
    ratios = freq_ratio(first_band, bands_dev)
    global_padded = extended_2(energy, (("grid", 2),), 1, True)
    nest_padded = extended_2(nest_energy, (("grid", 2),), 1, True)
    lower_keep = jnp.logical_and(grid_rank != quarter_count, grid_rank != 3 * quarter_count)
    upper_keep = jnp.logical_and(grid_rank != quarter_count - 1, grid_rank != 3 * quarter_count - 1)
    nest_padded = jnp.concatenate(
        [
            nest_padded[:, :, :1] * lower_keep.astype(jnp.float32),
            nest_padded[:, :, 1:-1],
            nest_padded[:, :, -1:] * upper_keep.astype(jnp.float32),
        ],
        axis=2,
    )
    along_lon, along_lat = courant_pair(ratios, lat_secant(lat_rows), 1.0)
    advected = advect(global_padded, along_lon, along_lat) * ocean_mask.astype(jnp.float32)
    band_weight = 0.1 * ratios
    partial_value = jnp.sum(band_weight[:, None, None, None] * advected, axis=(0, 1))
    total_energy = lax.psum(partial_value, "spec")
    mean_energy = total_energy / (ANGLES * (0.1 * jnp.sum(freq_ratio(0, FREQS))))
    banded = extended_2(advected, (("spec", 0),), band_reach, False)
    ratios_padded = freq_ratio(first_band - band_reach, bands_dev + 2 * band_reach)
    global_next = step_sources(advected, banded, ratios, ratios_padded, wind_field, mean_energy)
    east_column = passed_along(global_next[:, :, :1], "grid", -1)
    extended = jnp.concatenate([global_next, east_column], axis=2).reshape(
        bin_count, (lon_dev + 1) * lat_rows
    )
    local_col = rim_cell[:, 0] - grid_rank * lon_dev
    cols = jnp.arange(lon_dev + 1)[None, :]
    rows = jnp.arange(lat_rows)[None, :]
    ex = rim_weight[:, 0:1]
    ny = rim_weight[:, 1:2]
    col_share = jnp.where(cols == local_col[:, None], 1.0 - ex, 0.0) + jnp.where(
        cols == local_col[:, None] + 1, ex, 0.0
    )
    row_share = jnp.where(rows == rim_cell[:, 1:2], 1.0 - ny, 0.0) + jnp.where(
        rows == rim_cell[:, 1:2] + 1, ny, 0.0
    )
    corners = (col_share[:, :, None] * row_share[:, None, :]).reshape(rim_cell.shape[0], -1)
    boundary = lax.dot_general(
        corners, extended, (((1,), (1,)), ((), ())), precision=lax.Precision.HIGHEST
    )
    dest = rim_dest[:, 0]
    points = dest.shape[0]
    order = jnp.arange(points)
    earlier = (dest[:, None] == dest[None, :]) & (order[None, :] < order[:, None])
    slot = jnp.sum(earlier.astype(jnp.int32), axis=1)
    relax_high, relax_low = split_16(rim_weight[:, 2:3])
    target = rim_target[:, None]
    lanes = 128
    width = -(-(bin_count + 4) // lanes) * lanes
    payload = jnp.concatenate(
        [
            boundary,
            (target // lat_rows).astype(jnp.float32),
            (target % lat_rows).astype(jnp.float32),
            relax_high,
            relax_low,
            jnp.zeros((points, width - bin_count - 4), jnp.float32),
        ],
        axis=1,
    ).astype(jnp.bfloat16)
    slot_ids = jnp.arange(SLOTS)[:, None, None]
    names = jnp.arange(grid_count)[None, :, None]
    chosen = ((slot[None, None, :] == slot_ids) & (dest[None, None, :] == names)).astype(
        jnp.bfloat16
    )
    packed = lax.dot_general(
        chosen, payload, (((2,), (0,)), ((), ())), preferred_element_type=jnp.float32
    ).astype(jnp.bfloat16)
    per_slot = width // lanes
    blocks = jnp.transpose(packed.reshape(SLOTS, grid_count, per_slot, lanes), (1, 0, 2, 3))
    blocks = blocks.reshape(grid_count, SLOTS * per_slot, lanes)
    blocks = jnp.pad(blocks, ((0, 0), (0, 8 - SLOTS * per_slot), (0, 0)))
    arrived = exchange(blocks)
    nest_lon, nest_lat = courant_pair(ratios, jnp.ones((lat_rows,), jnp.float32), nest_speedup)
    nest_flat = advect(nest_padded, nest_lon, nest_lat).reshape(bin_count, lon_dev * lat_rows)
    arrived = arrived[:, : SLOTS * per_slot].reshape(grid_count * SLOTS, width)
    facts = arrived[:, bin_count : bin_count + 4].astype(jnp.float32)
    cell = facts[:, 0:1] * lat_rows + facts[:, 1:2]
    hit = cell == jnp.arange(lon_dev * lat_rows)[None, :].astype(jnp.float32)
    share_high = jnp.where(hit, facts[:, 2:3], 0.0)
    share_low = jnp.where(hit, facts[:, 3:4], 0.0)
    total_share = jnp.sum(share_high + share_low, axis=0)
    spectra = arrived[:, :bin_count]
    gained = lax.dot_general(
        jnp.concatenate([spectra, spectra], axis=0),
        jnp.concatenate([share_high, share_low], axis=0).astype(jnp.bfloat16),
        (((0,), (0,)), ((), ())),
        preferred_element_type=jnp.float32,
    )
    nest_next = (nest_flat * (1.0 - total_share)[None, :] + gained).reshape(
        bands_dev, ANGLES, lon_dev, lat_rows
    )
    return (global_next, nest_next)


def solution(mesh):
    in_specs = (
        P("spec", None, "grid", None),
        P("spec", None, "grid", None),
        P("grid", None),
        P(None, "grid", None),
        P("grid", None),
        P("grid", None),
        P("grid"),
        P("grid", None),
    )
    out_specs = (P("spec", None, "grid", None), P("spec", None, "grid", None))
    return jax.shard_map(
        per_device, mesh=mesh, in_specs=in_specs, out_specs=out_specs, check_vma=False
    )
```

```python
import jax
import jax.numpy as jnp
import numpy as np
from jax import lax
from jax.experimental import pallas as pl
from jax.experimental.pallas import tpu as pltpu
from jax.sharding import PartitionSpec as P

FREQS = 36
ANGLES = 36
LON = 4
LAT = 128
RIM = 128
BANDS = 9
REACH = 5
BINS = BANDS * ANGLES
ROWS = BINS * LON
BAND_ROWS = ANGLES * LON
PAIRS = BAND_ROWS // 8
PACKET = 352
EAST = 336
WIDTH = 384
FACT = BINS - 256
MESH = pl.DeviceIdType.MESH
F32 = jnp.float32
BF16 = jnp.bfloat16

ratio_step = 1.1
speed_coef = 0.054
wind_coef = 0.05
dissip_coef = 0.2
nonlin_coef = 0.12
nest_speedup = 2.0


def tables():
    heading = 2.0 * np.pi * np.arange(ANGLES) / ANGLES
    cosine, sine = np.cos(heading), np.sin(heading)
    cosine[[9, 27]] = 0.0
    sine[[0, 18]] = 0.0

    def spread(x):
        rows = np.repeat(x, LON)
        return np.broadcast_to(rows[:, None], (BAND_ROWS, LAT)).astype(np.float32)

    degrees = -60.0 + 120.0 * (np.arange(LAT) + 0.5) / LAT
    secant = np.broadcast_to(1.0 / np.cos(degrees * np.pi / 180.0), (8, LAT)).astype(np.float32)
    bands = np.arange(-REACH, FREQS + REACH)
    ratio = ratio_step ** (bands - FREQS // 2).astype(np.float64)
    scalars = np.concatenate([ratio, 1.0 / ratio]).astype(np.float32)
    return spread(cosine), spread(sine), secant, scalars


RATIO_COUNT = FREQS + 2 * REACH
MEAN_SCALE = float(
    1.0 / (ANGLES * 0.1 * np.sum(ratio_step ** (np.arange(FREQS) - FREQS // 2.0)))
)


def dot_nt(a, b):
    return lax.dot_general(a, b, (((1,), (1,)), ((), ())), preferred_element_type=F32)


def split_16(x):
    high = x.astype(BF16)
    return high, (x - high.astype(F32)).astype(BF16)


def kernel(
    count,
    e_ref,
    n_ref,
    mask_ref,
    wind_ref,
    cell_ref,
    dest_ref,
    target_ref,
    weight_ref,
    cos_ref,
    sin_ref,
    sec_ref,
    scalar_ref,
    g_out,
    n_out,
    stage_a,
    stage_b,
    east_send,
    west_send,
    from_west,
    from_east,
    halo_e,
    halo_n,
    even,
    odd,
    bands_16,
    low_halo,
    high_halo,
    gain,
    nest,
    g_buf,
    n_buf,
    part,
    parts,
    col_send,
    col_recv,
    share_high,
    share_low,
    hot,
    facts,
    slot_rows,
    blocks,
    arrived,
    lon_send,
    lon_recv,
    band_send,
    band_recv,
    sum_send,
    sum_recv,
    col_ssem,
    col_rsem,
    rim_send,
    rim_recv,
    out_sem,
):
    me = lax.axis_index("grid")
    spec = lax.axis_index("spec")
    specs = FREQS // BANDS
    first = spec * BANDS
    west = lax.rem(me + count - 1, count)
    east = lax.rem(me + 1, count)
    barrier = pltpu.get_barrier_semaphore()

    def ratio(band):
        return scalar_ref[first + band]

    def inverse(band):
        return scalar_ref[first + band + RATIO_COUNT]

    def greet(i, carry):
        pl.semaphore_signal(
            barrier, inc=1, device_id={"grid": lax.rem(me + i, count)}, device_id_type=MESH
        )
        return carry

    lax.fori_loop(1, count, greet, 0)
    for i in range(1, specs):
        pl.semaphore_signal(
            barrier, inc=1, device_id={"spec": lax.rem(spec + i, specs)}, device_id_type=MESH
        )

    packet_rows = lax.broadcasted_iota(jnp.int32, (PACKET, LAT), 0)
    angle = lax.rem(packet_rows, ANGLES)
    eastward = (angle < 10) | (angle >= 28)
    stage_a[...] = jnp.zeros_like(stage_a)
    stage_b[...] = jnp.zeros_like(stage_b)
    for lon, picked, send in ((LON - 1, eastward, east_send), (0, ~eastward, west_send)):
        stage_a[pl.ds(0, BINS), :] = e_ref[pl.ds(lon, BINS, stride=LON), :]
        stage_b[pl.ds(18, BINS), :] = n_ref[pl.ds(lon, BINS, stride=LON), :]
        send[...] = jnp.where(picked, stage_a[...], stage_b[...]).astype(BF16)

    pl.semaphore_wait(barrier, count - 1 + specs - 1)

    def lon_copy(send, recv, index, to):
        return pltpu.make_async_remote_copy(
            src_ref=send,
            dst_ref=recv,
            send_sem=lon_send.at[index],
            recv_sem=lon_recv.at[index],
            device_id={"grid": to},
            device_id_type=MESH,
        )

    eastbound = lon_copy(east_send, from_west, 0, east)
    westbound = lon_copy(west_send, from_east, 1, west)
    eastbound.start()
    westbound.start()

    lane = lax.broadcasted_iota(jnp.int32, (RIM, LAT), 1)
    sub = lax.broadcasted_iota(jnp.int32, (RIM, LAT), 0)
    local_col = cell_ref[:, 0:1] - me * LON
    row = cell_ref[:, 1:2]
    ex = weight_ref[:, 0:1]
    ny = weight_ref[:, 1:2]
    relax = weight_ref[:, 2:3]
    row_share = jnp.where(lane == row, 1.0 - ny, jnp.where(lane == row + 1, ny, 0.0))
    for lon in range(LON + 1):
        col_share = jnp.where(
            local_col == lon, 1.0 - ex, jnp.where(local_col == lon - 1, ex, 0.0)
        )
        high, low = split_16(col_share * row_share)
        share_high[lon] = high
        share_low[lon] = low
    diagonal = lane == sub
    dest_col = dest_ref[...].astype(F32)
    dest_row = jnp.sum(jnp.where(diagonal, dest_col, 0.0), axis=0, keepdims=True)
    target_f = target_ref[...].astype(F32)
    target_col = jnp.sum(jnp.where(diagonal, target_f, 0.0), axis=1, keepdims=True).astype(jnp.int32)
    same = dest_col == dest_row
    slot_row = jnp.sum(jnp.where(same & (sub < lane), 1.0, 0.0), axis=0, keepdims=True)
    named = dest_row == sub.astype(F32)
    for j in range(2):
        hot[pl.ds(j * RIM, RIM), :] = jnp.where(named & (slot_row == float(j)), 1.0, 0.0).astype(BF16)
    relax_high = relax.astype(BF16).astype(F32)
    fact = jnp.where(lane == FACT, (target_col >> 7).astype(F32), 0.0)
    fact = jnp.where(lane == FACT + 1, (target_col & 127).astype(F32), fact)
    fact = jnp.where(lane == FACT + 2, relax_high, fact)
    fact = jnp.where(lane == FACT + 3, relax - relax_high, fact)
    facts[...] = fact
    slot_rows[...] = jnp.zeros_like(slot_rows)

    pair_shape = (PAIRS, 8, LAT)
    cosine = cos_ref[...].reshape(pair_shape)
    sine = sin_ref[...].reshape(pair_shape)
    wind = wind_ref[...]
    wind_x = jnp.concatenate([wind[0], wind[0]], axis=0)[None]
    wind_y = jnp.concatenate([wind[1], wind[1]], axis=0)[None]
    gain[...] = wind_coef * jnp.maximum(wind_x * cosine + wind_y * sine, 0.0)
    mask_half = mask_ref[...].astype(F32)
    mask = jnp.concatenate([mask_half, mask_half], axis=0)[None]
    secant = sec_ref[...][None]

    vreg_sub = lax.broadcasted_iota(jnp.int32, (1, 8, LAT), 1)
    vreg_lane = lax.broadcasted_iota(jnp.int32, (1, 8, LAT), 2)
    lon_of = vreg_sub & 3

    def upwind(block, halo):
        before = jnp.where(lon_of == 0, halo, pltpu.roll(block, 1, axis=1))
        after = jnp.where(lon_of == LON - 1, halo, pltpu.roll(block, 7, axis=1))
        along_lon = jnp.concatenate([before[:5], after[5:14], before[14:]], axis=0)
        south = jnp.where(vreg_lane == 0, 0.0, pltpu.roll(block, 1, axis=2))
        north = jnp.where(vreg_lane == LAT - 1, 0.0, pltpu.roll(block, LAT - 1, axis=2))
        along_lat = jnp.concatenate([south[:9], north[9:]], axis=0)
        return block - along_lon, block - along_lat

    def rows_of(ref, band):
        return ref[pl.ds(pl.multiple_of(band * BAND_ROWS, 8), BAND_ROWS), :].reshape(pair_shape)

    def cyclic(ref, band, value):
        ref[band, pl.ds(2, PAIRS)] = value
        ref[band, pl.ds(0, 2)] = value[PAIRS - 2 :]
        ref[band, pl.ds(PAIRS + 2, 2)] = value[:2]

    def keep(band, value):
        cyclic(even, band, value)
        turned = pltpu.roll(value, 4, axis=1)
        following = jnp.concatenate([turned[1:], turned[:1]], axis=0)
        cyclic(odd, band, jnp.where(vreg_sub < 4, turned, following))

    eastbound.wait()
    westbound.wait()
    stage_a[...] = from_west[...].astype(F32)
    stage_b[...] = from_east[...].astype(F32)
    quarter = count // 4
    lower_keep = jnp.where((me != quarter) & (me != 3 * quarter), 1.0, 0.0)
    upper_keep = jnp.where((me != quarter - 1) & (me != 3 * quarter - 1), 1.0, 0.0)
    halo_e[pl.ds(0, BINS, stride=LON), :] = stage_a[pl.ds(0, BINS), :]
    halo_e[pl.ds(LON - 1, BINS, stride=LON), :] = stage_b[pl.ds(0, BINS), :]
    halo_n[pl.ds(0, BINS, stride=LON), :] = stage_a[pl.ds(18, BINS), :] * lower_keep
    halo_n[pl.ds(LON - 1, BINS, stride=LON), :] = stage_b[pl.ds(18, BINS), :] * upper_keep

    def advect_band(band, total):
        block = rows_of(e_ref, band)
        lon_step, lat_step = upwind(block, rows_of(halo_e, band))
        speed = speed_coef * inverse(band + REACH)
        along_x = jnp.abs(rows_of(cos_ref, 0)) * secant
        along_y = jnp.abs(rows_of(sin_ref, 0))
        moved = (block - speed * (along_x * lon_step + along_y * lat_step)) * mask
        keep(band + REACH, moved)
        bands_16[band] = moved.reshape(BAND_ROWS, LAT).astype(BF16)
        return total + 0.1 * ratio(band + REACH) * jnp.sum(moved, axis=0)

    part[...] = lax.fori_loop(0, BANDS, advect_band, jnp.zeros((8, LAT), F32))

    def band_copy(start, recv, index, to):
        return pltpu.make_async_remote_copy(
            src_ref=bands_16.at[pl.ds(start, REACH)],
            dst_ref=recv,
            send_sem=band_send.at[index],
            recv_sem=band_recv.at[index],
            device_id={"spec": to},
            device_id_type=MESH,
        )

    upward = band_copy(BANDS - REACH, low_halo, 0, lax.rem(spec + 1, specs))
    downward = band_copy(0, high_halo, 1, lax.rem(spec + specs - 1, specs))

    @pl.when(spec < specs - 1)
    def _():
        upward.start()

    @pl.when(spec > 0)
    def _():
        downward.start()

    sums = []
    for i in range(1, specs):
        sums.append(
            pltpu.make_async_remote_copy(
                src_ref=part,
                dst_ref=parts.at[i],
                send_sem=sum_send.at[i],
                recv_sem=sum_recv.at[i],
                device_id={"spec": lax.rem(spec + i, specs)},
                device_id_type=MESH,
            )
        )
    for copy in sums:
        copy.start()

    def advect_nest(band, carry):
        block = rows_of(n_ref, band)
        lon_step, lat_step = upwind(block, rows_of(halo_n, band))
        speed = nest_speedup * speed_coef * inverse(band + REACH)
        along_x = jnp.abs(rows_of(cos_ref, 0))
        along_y = jnp.abs(rows_of(sin_ref, 0))
        moved = block - speed * (along_x * lon_step + along_y * lat_step)
        nest[pl.ds(pl.multiple_of(band * BAND_ROWS, 8), BAND_ROWS), :] = moved.reshape(BAND_ROWS, LAT)
        return carry

    lax.fori_loop(0, BANDS, advect_nest, 0)

    @pl.when(spec < specs - 1)
    def _():
        upward.wait_send()
        downward.wait_recv()

    @pl.when(spec > 0)
    def _():
        upward.wait_recv()
        downward.wait_send()

    def halo_bands(band, carry):
        low = low_halo[band].astype(F32).reshape(pair_shape)
        keep(band, jnp.where(spec > 0, low, 0.0))
        high = high_halo[band].astype(F32).reshape(pair_shape)
        keep(band + BANDS + REACH, jnp.where(spec < specs - 1, high, 0.0))
        return carry

    lax.fori_loop(0, REACH, halo_bands, 0)

    chunk = 6

    def nonlinear_band(band, carry):
        for piece in range(PAIRS // chunk):
            base = 2 + piece * chunk

            def at(ref, offset, turn):
                return ref[band + REACH + offset, pl.ds(base + turn, chunk)]

            here = at(even, 0, 0)
            total = here * (1.0 + ratio(band + REACH) * gain[pl.ds(piece * chunk, chunk)])

            def product(centre, upper, lower):
                return centre * (centre * (upper + lower) - 2.0 * upper * lower)

            own = 0.0
            below = 0.0
            above = 0.0
            for s in (1, -1):
                own += product(
                    here, at(odd, 2, (3 * s - 1) // 2), at(odd, -3, (-s - 1) // 2)
                )
                below += product(at(odd, -2, (-3 * s - 1) // 2), here, at(even, -5, -2 * s))
                above += product(at(odd, 3, (s - 1) // 2), at(even, 5, 2 * s), here)
            total += nonlin_coef * (
                ratio(band + REACH - 2) * below
                + ratio(band + REACH + 3) * above
                - 2.0 * ratio(band + REACH) * own
            )
            start = pl.multiple_of(band * BAND_ROWS + piece * chunk * 8, 8)
            g_buf[pl.ds(start, chunk * 8), :] = total.reshape(chunk * 8, LAT)
        return carry

    lax.fori_loop(0, BANDS, nonlinear_band, 0)

    for copy in sums:
        copy.wait()
    whole = part[...] + parts[1] + parts[2] + parts[3]
    mean = (whole + pltpu.roll(whole, 4, axis=0)) * MEAN_SCALE

    def damp_band(band, carry):
        value = ratio(band + REACH)
        inverse_loss = 1.0 / (1.0 + dissip_coef * value * value * mean)
        start = pl.multiple_of(band * BAND_ROWS, 8)
        result = rows_of(g_buf, band) * inverse_loss[None]
        g_buf[pl.ds(start, BAND_ROWS), :] = result.reshape(BAND_ROWS, LAT)
        return carry

    lax.fori_loop(0, BANDS, damp_band, 0)
    g_buf[pl.ds(ROWS, WIDTH * LON - ROWS), :] = jnp.zeros((WIDTH * LON - ROWS, LAT), F32)

    col_send[...] = g_buf[pl.ds(0, WIDTH, stride=LON), :].astype(BF16)
    column = pltpu.make_async_remote_copy(
        src_ref=col_send,
        dst_ref=col_recv,
        send_sem=col_ssem,
        recv_sem=col_rsem,
        device_id={"grid": west},
        device_id_type=MESH,
    )
    column.start()
    g_copy = pltpu.make_async_copy(g_buf.at[pl.ds(0, ROWS)], g_out, out_sem.at[0])
    g_copy.start()

    boundary = jnp.zeros((RIM, WIDTH), F32)
    for lon in range(LON):
        high, low = split_16(g_buf[pl.ds(lon, WIDTH, stride=LON), :])
        boundary += dot_nt(share_high[lon], high)
        boundary += dot_nt(share_high[lon], low)
        boundary += dot_nt(share_low[lon], high)
    column.wait()
    boundary += dot_nt(share_high[LON], col_recv[...])
    boundary += dot_nt(share_low[LON], col_recv[...])
    boundary = jnp.concatenate([boundary[:, :256], boundary[:, 256:] + facts[...]], axis=1)
    packed = jnp.dot(hot[...], boundary.astype(BF16), preferred_element_type=F32)
    for j in range(2):
        for c in range(3):
            slot_rows[pl.ds(j * 3 + c, RIM, stride=8), :] = packed[
                j * RIM : (j + 1) * RIM, c * LAT : (c + 1) * LAT
            ]
    blocks[...] = slot_rows[...].reshape(count, 8, LAT).astype(BF16)

    own_block = pltpu.make_async_copy(blocks.at[me], arrived.at[me], rim_recv)
    own_block.start()

    def post(i, carry):
        dest = lax.rem(me + i, count)
        pltpu.make_async_remote_copy(
            src_ref=blocks.at[dest],
            dst_ref=arrived.at[me],
            send_sem=rim_send,
            recv_sem=rim_recv,
            device_id={"grid": dest},
            device_id_type=MESH,
        ).start()
        return carry

    lax.fori_loop(1, count, post, 0)
    others = blocks.at[pl.ds(0, count - 1)]
    pltpu.make_async_copy(others, others, rim_send).wait()
    pltpu.make_async_copy(arrived, arrived, rim_recv).wait()

    slot_rows[...] = arrived[...].astype(F32).reshape(count * 8, LAT)
    halves = []
    for j in range(2):
        halves.append(
            jnp.concatenate(
                [slot_rows[pl.ds(j * 3 + c, RIM, stride=8), :] for c in range(3)], axis=1
            )
        )
    spectra = jnp.concatenate(halves, axis=0)
    told = spectra[:, 256:]
    cell = told[:, FACT : FACT + 1] * float(LAT) + told[:, FACT + 1 : FACT + 2]
    cells = lax.broadcasted_iota(jnp.int32, (2 * RIM, LON * LAT), 1).astype(F32)
    hit = cell == cells
    rate_high = jnp.where(hit, told[:, FACT + 2 : FACT + 3], 0.0)
    rate_low = jnp.where(hit, told[:, FACT + 3 : FACT + 4], 0.0)
    remains = 1.0 - jnp.sum(rate_high + rate_low, axis=0, keepdims=True)
    turned = spectra.T.astype(BF16)
    gained = jnp.dot(turned, rate_high.astype(BF16), preferred_element_type=F32)
    gained += jnp.dot(turned, rate_low.astype(BF16), preferred_element_type=F32)
    for lon in range(LON):
        lanes = slice(lon * LAT, (lon + 1) * LAT)
        held = nest[pl.ds(lon, BINS, stride=LON), :]
        n_buf[pl.ds(lon, BINS, stride=LON), :] = held * remains[:, lanes] + gained[:BINS, lanes]
    n_copy = pltpu.make_async_copy(n_buf, n_out, out_sem.at[1])
    n_copy.start()
    g_copy.wait()
    n_copy.wait()


def per_device(
    energy, nest_energy, ocean_mask, wind_field, rim_cell, rim_dest, rim_target, rim_weight
):
    count = lax.axis_size("grid")
    cosine, sine, secant, scalars = tables()
    vmem = pl.BlockSpec(memory_space=pltpu.VMEM)
    flat = jax.ShapeDtypeStruct((ROWS, LAT), F32)
    dma = pltpu.SemaphoreType.DMA

    def body(*refs):
        kernel(count, *refs)

    global_next, nest_next = pl.pallas_call(
        body,
        out_shape=(flat, flat),
        in_specs=[vmem] * 11 + [pl.BlockSpec(memory_space=pltpu.SMEM)],
        out_specs=(pl.BlockSpec(memory_space=pl.ANY), pl.BlockSpec(memory_space=pl.ANY)),
        scratch_shapes=[
            pltpu.VMEM((PACKET, LAT), F32),
            pltpu.VMEM((PACKET, LAT), F32),
            pltpu.VMEM((PACKET, LAT), BF16),
            pltpu.VMEM((PACKET, LAT), BF16),
            pltpu.VMEM((PACKET, LAT), BF16),
            pltpu.VMEM((PACKET, LAT), BF16),
            pltpu.VMEM((ROWS, LAT), F32),
            pltpu.VMEM((ROWS, LAT), F32),
            pltpu.VMEM((BANDS + 2 * REACH, PAIRS + 4, 8, LAT), F32),
            pltpu.VMEM((BANDS + 2 * REACH, PAIRS + 4, 8, LAT), F32),
            pltpu.VMEM((BANDS, BAND_ROWS, LAT), BF16),
            pltpu.VMEM((REACH, BAND_ROWS, LAT), BF16),
            pltpu.VMEM((REACH, BAND_ROWS, LAT), BF16),
            pltpu.VMEM((PAIRS, 8, LAT), F32),
            pltpu.VMEM((ROWS, LAT), F32),
            pltpu.VMEM((WIDTH * LON, LAT), F32),
            pltpu.VMEM((ROWS, LAT), F32),
            pltpu.VMEM((8, LAT), F32),
            pltpu.VMEM((4, 8, LAT), F32),
            pltpu.VMEM((WIDTH, LAT), BF16),
            pltpu.VMEM((WIDTH, LAT), BF16),
            pltpu.VMEM((LON + 1, RIM, LAT), BF16),
            pltpu.VMEM((LON + 1, RIM, LAT), BF16),
            pltpu.VMEM((2 * RIM, RIM), BF16),
            pltpu.VMEM((RIM, LAT), F32),
            pltpu.VMEM((count * 8, LAT), F32),
            pltpu.VMEM((count, 8, LAT), BF16),
            pltpu.VMEM((count, 8, LAT), BF16),
            dma((2,)),
            dma((2,)),
            dma((2,)),
            dma((2,)),
            dma((4,)),
            dma((4,)),
            dma,
            dma,
            dma,
            dma,
            dma((2,)),
        ],
        compiler_params=pltpu.CompilerParams(
            collective_id=0, has_side_effects=True, vmem_limit_bytes=40 << 20
        ),
        name="wave_step",
    )(
        energy.reshape(ROWS, LAT),
        nest_energy.reshape(ROWS, LAT),
        ocean_mask,
        wind_field,
        rim_cell,
        rim_dest,
        rim_target.reshape(1, RIM),
        rim_weight,
        jnp.asarray(cosine),
        jnp.asarray(sine),
        jnp.asarray(secant),
        jnp.asarray(scalars),
    )
    shape = energy.shape
    return (global_next.reshape(shape), nest_next.reshape(shape))


def solution(mesh):
    in_specs = (
        P("spec", None, "grid", None),
        P("spec", None, "grid", None),
        P("grid", None),
        P(None, "grid", None),
        P("grid", None),
        P("grid", None),
        P("grid"),
        P("grid", None),
    )
    out_specs = (P("spec", None, "grid", None), P("spec", None, "grid", None))
    return jax.shard_map(
        per_device, mesh=mesh, in_specs=in_specs, out_specs=out_specs, check_vma=False
    )
```

```python
import jax
import jax.numpy as jnp
import numpy as np
from jax import lax
from jax.experimental import pallas as pl
from jax.experimental.pallas import tpu as pltpu
from jax.sharding import PartitionSpec as P

FREQS = 36
ANGLES = 36
LON = 4
LAT = 128
RIM = 128
BANDS = 9
REACH = 5
BINS = BANDS * ANGLES
ROWS = BINS * LON
BAND_ROWS = ANGLES * LON
PAIRS = BAND_ROWS // 8
PACKET = 208
FIRST_ROWS = 144
EAST = 336
RING = 8
WIDTH = 384
FACT = BINS - 256
MESH = pl.DeviceIdType.MESH
F32 = jnp.float32
BF16 = jnp.bfloat16

ratio_step = 1.1
speed_coef = 0.054
wind_coef = 0.05
dissip_coef = 0.2
nonlin_coef = 0.12
nest_speedup = 2.0


def tables():
    heading = 2.0 * np.pi * np.arange(ANGLES) / ANGLES
    cosine, sine = np.cos(heading), np.sin(heading)
    cosine[[9, 27]] = 0.0
    sine[[0, 18]] = 0.0

    def spread(x):
        rows = np.repeat(x, LON)
        return np.broadcast_to(rows[:, None], (BAND_ROWS, LAT)).astype(np.float32)

    degrees = -60.0 + 120.0 * (np.arange(LAT) + 0.5) / LAT
    secant = np.broadcast_to(1.0 / np.cos(degrees * np.pi / 180.0), (8, LAT)).astype(np.float32)
    bands = np.arange(-REACH, FREQS + REACH)
    ratio = ratio_step ** (bands - FREQS // 2).astype(np.float64)
    scalars = np.zeros((128,), np.float32)
    scalars[: 2 * ratio.size] = np.concatenate([ratio, 1.0 / ratio])
    return spread(cosine), spread(sine), secant, scalars


RATIO_COUNT = FREQS + 2 * REACH
MEAN_SCALE = float(
    1.0 / (ANGLES * 0.1 * np.sum(ratio_step ** (np.arange(FREQS) - FREQS // 2.0)))
)


def dot_nt(a, b):
    return lax.dot_general(a, b, (((1,), (1,)), ((), ())), preferred_element_type=F32)


def split_16(x):
    high = x.astype(BF16)
    return high, (x - high.astype(F32)).astype(BF16)


def far_first():
    def hops(step):
        z, x, y = step
        return min(z, RING - z) + 2 * x + min(y, RING - y)

    steps = [(z, x, y) for z in range(RING) for x in range(2) for y in range(RING)]
    return sorted(steps[1:], key=lambda step: -hops(step))


def kernel(
    count,
    e_hbm,
    n_hbm,
    mask_hbm,
    wind_hbm,
    cell_hbm,
    dest_hbm,
    target_hbm,
    weight_hbm,
    cos_hbm,
    sin_hbm,
    sec_hbm,
    scalar_hbm,
    g_out,
    n_out,
    e_ref,
    n_ref,
    mask_ref,
    wind_ref,
    cell_ref,
    dest_ref,
    target_ref,
    weight_ref,
    cos_ref,
    sin_ref,
    sec_ref,
    scalar_ref,
    rim_rows,
    stage_a,
    stage_b,
    e_send,
    n_send,
    e_recv,
    n_recv,
    halo_e,
    halo_n,
    even,
    odd,
    bands_16,
    low_halo,
    high_halo,
    gain,
    nest,
    g_buf,
    part,
    parts,
    col_send,
    col_recv,
    share_high,
    share_low,
    hot,
    facts,
    slot_rows,
    blocks,
    arrived,
    in_sem,
    lon_send,
    lon_recv,
    band_send,
    band_recv,
    sum_send,
    sum_recv,
    col_ssem,
    col_rsem,
    rim_send,
    rim_recv,
    ring_sem,
    half_sem,
):
    sources = (
        e_hbm, n_hbm, scalar_hbm, mask_hbm, cos_hbm, sin_hbm, sec_hbm, wind_hbm,
        cell_hbm, dest_hbm, target_hbm, weight_hbm,
    )
    places = (
        e_ref, n_ref, scalar_ref, mask_ref, cos_ref, sin_ref, sec_ref, wind_ref,
        cell_ref, dest_ref, target_ref, weight_ref,
    )
    loads = [
        pltpu.make_async_copy(source, place, in_sem.at[i])
        for i, (source, place) in enumerate(zip(sources, places))
    ]
    loads[0].start()
    loads[1].start()
    me = lax.axis_index("grid")
    spec = lax.axis_index("spec")
    specs = FREQS // BANDS
    first = spec * BANDS
    west = lax.rem(me + count - 1, count)
    east = lax.rem(me + 1, count)
    barrier = pltpu.get_barrier_semaphore()

    def ratio(band):
        return scalar_ref[first + band]

    def inverse(band):
        return scalar_ref[first + band + RATIO_COUNT]

    z_part = me // (2 * RING)
    x_part = lax.rem(me // RING, 2)
    y_part = lax.rem(me, RING)

    def place_of(z, x, y):
        return (z * 2 + x) * RING + y

    def turned_by(part, step, size):
        return lax.rem(part + step, size) if step else part

    def tell(sem, to):
        pl.semaphore_signal(sem, inc=1, device_id=to, device_id_type=MESH)

    tell(barrier, {"grid": west})
    tell(barrier, {"grid": east})
    for i in range(1, specs):
        tell(barrier, {"spec": lax.rem(spec + i, specs)})
    z_peers = [place_of(turned_by(z_part, i, RING), x_part, y_part) for i in range(1, RING)]
    x_peer = place_of(z_part, 1 - x_part, y_part)
    for i in range(1, RING):
        tell(barrier, {"grid": place_of(z_part, x_part, turned_by(y_part, i, RING))})
    for peer in z_peers:
        tell(barrier, {"grid": peer})
    tell(barrier, {"grid": x_peer})
    for load in loads[2:]:
        load.start()

    packet_rows = lax.broadcasted_iota(jnp.int32, (PACKET, LAT), 0)
    angle = lax.rem(packet_rows, ANGLES)
    eastward = (angle < 10) | (angle >= 28)
    stage_a[...] = jnp.zeros_like(stage_a)
    stage_b[...] = jnp.zeros_like(stage_b)
    direct = 5 * ANGLES
    folded = BINS - direct

    def pack(source, send):
        for index, lon, picked in ((0, LON - 1, eastward), (1, 0, ~eastward)):
            stage_a[pl.ds(0, direct), :] = source[pl.ds(lon, direct, stride=LON), :]
            stage_b[pl.ds(18, folded), :] = source[pl.ds(direct * LON + lon, folded, stride=LON), :]
            send[index] = jnp.where(picked, stage_a[...], stage_b[...]).astype(BF16)

    loads[0].wait()
    pack(e_ref, e_send)
    pl.semaphore_wait(barrier, 2 + specs - 1 + 2 * (RING - 1) + 1)

    def lon_copies(send, recv, base):
        return [
            pltpu.make_async_remote_copy(
                src_ref=send.at[index],
                dst_ref=recv.at[index],
                send_sem=lon_send.at[base + index],
                recv_sem=lon_recv.at[base + index],
                device_id={"grid": to},
                device_id_type=MESH,
            )
            for index, to in ((0, east), (1, west))
        ]

    e_lon = lon_copies(e_send, e_recv, 0)
    n_lon = lon_copies(n_send, n_recv, 2)
    for copy in e_lon:
        copy.start()
    for peer in z_peers:
        tell(ring_sem, {"grid": peer})
    loads[1].wait()
    pack(n_ref, n_send)
    for copy in n_lon:
        copy.start()
    for load in loads[2:]:
        load.wait()

    lane = lax.broadcasted_iota(jnp.int32, (RIM, LAT), 1)
    sub = lax.broadcasted_iota(jnp.int32, (RIM, LAT), 0)
    rim_rows[...] = jnp.zeros_like(rim_rows)
    rim_rows[pl.ds(0, 2), :] = cell_ref[...].astype(F32)
    rim_rows[pl.ds(2, 1), :] = dest_ref[...].astype(F32)
    rim_rows[pl.ds(3, 1), :] = target_ref[...].astype(F32)
    rim_rows[pl.ds(4, 3), :] = weight_ref[...]
    rim_cols = rim_rows[...].T
    local_col = rim_cols[:, 0:1].astype(jnp.int32) - me * LON
    row = rim_cols[:, 1:2].astype(jnp.int32)
    dest_col = rim_cols[:, 2:3]
    target_col = rim_cols[:, 3:4].astype(jnp.int32)
    ex = rim_cols[:, 4:5]
    ny = rim_cols[:, 5:6]
    relax = rim_cols[:, 6:7]
    row_share = jnp.where(lane == row, 1.0 - ny, jnp.where(lane == row + 1, ny, 0.0))
    for lon in range(LON + 1):
        col_share = jnp.where(
            local_col == lon, 1.0 - ex, jnp.where(local_col == lon - 1, ex, 0.0)
        )
        high, low = split_16(col_share * row_share)
        share_high[lon] = high
        share_low[lon] = low
    dest_row = dest_ref[...].astype(F32)
    same = dest_col == dest_row
    slot_row = jnp.sum(jnp.where(same & (sub < lane), 1.0, 0.0), axis=0, keepdims=True)
    named = dest_row == sub.astype(F32)
    for j in range(2):
        hot[pl.ds(j * RIM, RIM), :] = jnp.where(named & (slot_row == float(j)), 1.0, 0.0).astype(BF16)
    relax_high = relax.astype(BF16).astype(F32)
    fact = jnp.where(lane == FACT, (target_col >> 7).astype(F32), 0.0)
    fact = jnp.where(lane == FACT + 1, (target_col & 127).astype(F32), fact)
    fact = jnp.where(lane == FACT + 2, relax_high, fact)
    fact = jnp.where(lane == FACT + 3, relax - relax_high, fact)
    facts[...] = fact
    slot_rows[...] = jnp.zeros_like(slot_rows)

    pair_shape = (PAIRS, 8, LAT)
    cosine = cos_ref[...].reshape(pair_shape)
    sine = sin_ref[...].reshape(pair_shape)
    wind = wind_ref[...]
    wind_x = jnp.concatenate([wind[0], wind[0]], axis=0)[None]
    wind_y = jnp.concatenate([wind[1], wind[1]], axis=0)[None]
    gain[...] = wind_coef * jnp.maximum(wind_x * cosine + wind_y * sine, 0.0)
    mask_half = mask_ref[...].astype(F32)
    mask = jnp.concatenate([mask_half, mask_half], axis=0)[None]
    secant = sec_ref[...][None]

    vreg_sub = lax.broadcasted_iota(jnp.int32, (1, 8, LAT), 1)
    vreg_lane = lax.broadcasted_iota(jnp.int32, (1, 8, LAT), 2)
    lon_of = vreg_sub & 3

    def upwind(block, halo):
        before = jnp.where(lon_of == 0, halo, pltpu.roll(block, 1, axis=1))
        after = jnp.where(lon_of == LON - 1, halo, pltpu.roll(block, 7, axis=1))
        along_lon = jnp.concatenate([before[:5], after[5:14], before[14:]], axis=0)
        south = jnp.where(vreg_lane == 0, 0.0, pltpu.roll(block, 1, axis=2))
        north = jnp.where(vreg_lane == LAT - 1, 0.0, pltpu.roll(block, LAT - 1, axis=2))
        along_lat = jnp.concatenate([south[:9], north[9:]], axis=0)
        return block - along_lon, block - along_lat

    def rows_of(ref, band):
        return ref[pl.ds(pl.multiple_of(band * BAND_ROWS, 8), BAND_ROWS), :].reshape(pair_shape)

    def cyclic(ref, band, value):
        ref[band, pl.ds(2, PAIRS)] = value
        ref[band, pl.ds(0, 2)] = value[PAIRS - 2 :]
        ref[band, pl.ds(PAIRS + 2, 2)] = value[:2]

    def keep(band, value):
        cyclic(even, band, value)
        turned = pltpu.roll(value, 4, axis=1)
        following = jnp.concatenate([turned[1:], turned[:1]], axis=0)
        cyclic(odd, band, jnp.where(vreg_sub < 4, turned, following))

    def unpack(recv, halo, lower, upper):
        for index, lon, factor in ((0, 0, lower), (1, LON - 1, upper)):
            stage_a[...] = recv[index].astype(F32)
            front = stage_a[pl.ds(0, direct), :]
            rest = stage_a[pl.ds(18, folded), :]
            if factor is not None:
                front, rest = front * factor, rest * factor
            halo[pl.ds(lon, direct, stride=LON), :] = front
            halo[pl.ds(direct * LON + lon, folded, stride=LON), :] = rest

    for copy in e_lon:
        copy.wait()
    unpack(e_recv, halo_e, None, None)

    def advect_band(band, total):
        block = rows_of(e_ref, band)
        lon_step, lat_step = upwind(block, rows_of(halo_e, band))
        speed = speed_coef * inverse(band + REACH)
        along_x = jnp.abs(rows_of(cos_ref, 0)) * secant
        along_y = jnp.abs(rows_of(sin_ref, 0))
        moved = (block - speed * (along_x * lon_step + along_y * lat_step)) * mask
        keep(band + REACH, moved)
        bands_16[band] = moved.reshape(BAND_ROWS, LAT).astype(BF16)
        return total + 0.1 * ratio(band + REACH) * jnp.sum(moved, axis=0)

    def band_copy(start, recv, index, to):
        return pltpu.make_async_remote_copy(
            src_ref=bands_16.at[pl.ds(start, REACH)],
            dst_ref=recv,
            send_sem=band_send.at[index],
            recv_sem=band_recv.at[index],
            device_id={"spec": to},
            device_id_type=MESH,
        )

    upward = band_copy(BANDS - REACH, low_halo, 0, lax.rem(spec + 1, specs))
    downward = band_copy(0, high_halo, 1, lax.rem(spec + specs - 1, specs))
    total = lax.fori_loop(0, REACH, advect_band, jnp.zeros((8, LAT), F32))

    @pl.when(spec > 0)
    def _():
        downward.start()

    part[...] = lax.fori_loop(REACH, BANDS, advect_band, total)

    @pl.when(spec < specs - 1)
    def _():
        upward.start()

    sums = []
    for i in range(1, specs):
        sums.append(
            pltpu.make_async_remote_copy(
                src_ref=part,
                dst_ref=parts.at[i],
                send_sem=sum_send.at[i],
                recv_sem=sum_recv.at[i],
                device_id={"spec": lax.rem(spec + i, specs)},
                device_id_type=MESH,
            )
        )
    for copy in sums:
        copy.start()

    pl.semaphore_wait(ring_sem, RING - 1)
    tell(half_sem, {"grid": x_peer})

    quarter = count // 4
    lower_keep = jnp.where((me != quarter) & (me != 3 * quarter), 1.0, 0.0)
    upper_keep = jnp.where((me != quarter - 1) & (me != 3 * quarter - 1), 1.0, 0.0)
    for copy in n_lon:
        copy.wait()
    unpack(n_recv, halo_n, lower_keep, upper_keep)

    def advect_nest(band, carry):
        block = rows_of(n_ref, band)
        lon_step, lat_step = upwind(block, rows_of(halo_n, band))
        speed = nest_speedup * speed_coef * inverse(band + REACH)
        along_x = jnp.abs(rows_of(cos_ref, 0))
        along_y = jnp.abs(rows_of(sin_ref, 0))
        moved = block - speed * (along_x * lon_step + along_y * lat_step)
        nest[pl.ds(pl.multiple_of(band * BAND_ROWS, 8), BAND_ROWS), :] = moved.reshape(BAND_ROWS, LAT)
        return carry

    lax.fori_loop(0, BANDS, advect_nest, 0)

    for copy in sums:
        copy.wait()
    whole = part[...] + parts[1] + parts[2] + parts[3]
    mean = (whole + pltpu.roll(whole, 4, axis=0)) * MEAN_SCALE

    @pl.when(spec < specs - 1)
    def _():
        upward.wait_send()
        downward.wait_recv()

    @pl.when(spec > 0)
    def _():
        upward.wait_recv()
        downward.wait_send()

    def halo_bands(band, carry):
        low = low_halo[band].astype(F32).reshape(pair_shape)
        keep(band, jnp.where(spec > 0, low, 0.0))
        high = high_halo[band].astype(F32).reshape(pair_shape)
        keep(band + BANDS + REACH, jnp.where(spec < specs - 1, high, 0.0))
        return carry

    lax.fori_loop(0, REACH, halo_bands, 0)

    chunk = 6

    def nonlinear_band(band, carry):
        loss = ratio(band + REACH)
        inverse_loss = (1.0 / (1.0 + dissip_coef * loss * loss * mean))[None]
        for piece in range(PAIRS // chunk):
            base = 2 + piece * chunk

            def at(ref, offset, turn):
                return ref[band + REACH + offset, pl.ds(base + turn, chunk)]

            here = at(even, 0, 0)
            total = here * (1.0 + ratio(band + REACH) * gain[pl.ds(piece * chunk, chunk)])

            def product(centre, upper, lower):
                return centre * (centre * (upper + lower) - 2.0 * upper * lower)

            own = 0.0
            below = 0.0
            above = 0.0
            for s in (1, -1):
                own += product(
                    here, at(odd, 2, (3 * s - 1) // 2), at(odd, -3, (-s - 1) // 2)
                )
                below += product(at(odd, -2, (-3 * s - 1) // 2), here, at(even, -5, -2 * s))
                above += product(at(odd, 3, (s - 1) // 2), at(even, 5, 2 * s), here)
            total += nonlin_coef * (
                ratio(band + REACH - 2) * below
                + ratio(band + REACH + 3) * above
                - 2.0 * ratio(band + REACH) * own
            )
            start = pl.multiple_of(band * BAND_ROWS + piece * chunk * 8, 8)
            g_buf[pl.ds(start, chunk * 8), :] = (total * inverse_loss).reshape(chunk * 8, LAT)
        return carry

    def column_copy(start, rows, index):
        return pltpu.make_async_remote_copy(
            src_ref=col_send.at[pl.ds(start, rows)],
            dst_ref=col_recv.at[pl.ds(start, rows)],
            send_sem=col_ssem.at[index],
            recv_sem=col_rsem.at[index],
            device_id={"grid": west},
            device_id_type=MESH,
        )

    columns = [column_copy(0, FIRST_ROWS, 0), column_copy(FIRST_ROWS, EAST - FIRST_ROWS, 1)]
    first_bands = FIRST_ROWS // ANGLES
    g_buf[pl.ds(ROWS, WIDTH * LON - ROWS), :] = jnp.zeros((WIDTH * LON - ROWS, LAT), F32)
    col_recv[pl.ds(EAST, WIDTH - EAST), :] = jnp.zeros((WIDTH - EAST, LAT), BF16)
    lax.fori_loop(0, first_bands, nonlinear_band, 0)
    col_send[pl.ds(0, FIRST_ROWS), :] = g_buf[pl.ds(0, FIRST_ROWS, stride=LON), :].astype(BF16)
    columns[0].start()
    lax.fori_loop(first_bands, BANDS, nonlinear_band, 0)
    col_send[pl.ds(FIRST_ROWS, EAST - FIRST_ROWS), :] = g_buf[
        pl.ds(FIRST_ROWS * LON, EAST - FIRST_ROWS, stride=LON), :
    ].astype(BF16)
    columns[1].start()

    boundary = jnp.zeros((RIM, WIDTH), F32)
    for lon in range(LON):
        high, low = split_16(g_buf[pl.ds(lon, WIDTH, stride=LON), :])
        boundary += dot_nt(share_high[lon], high)
        boundary += dot_nt(share_high[lon], low)
        boundary += dot_nt(share_low[lon], high)
    for copy in columns:
        copy.wait()
    boundary += dot_nt(share_high[LON], col_recv[...])
    boundary += dot_nt(share_low[LON], col_recv[...])
    boundary = jnp.concatenate([boundary[:, :256], boundary[:, 256:] + facts[...]], axis=1)
    packed = jnp.dot(hot[...], boundary.astype(BF16), preferred_element_type=F32)
    for j in range(2):
        for c in range(3):
            slot_rows[pl.ds(j * 3 + c, RIM, stride=8), :] = packed[
                j * RIM : (j + 1) * RIM, c * LAT : (c + 1) * LAT
            ]
    blocks[...] = slot_rows[...].reshape(count, 8, LAT).astype(BF16)

    own_block = pltpu.make_async_copy(blocks.at[me], arrived.at[me], rim_recv)
    own_block.start()

    pl.semaphore_wait(half_sem, 1)
    for z, x, y in far_first():
        dest = place_of(
            turned_by(z_part, z, RING), 1 - x_part if x else x_part, turned_by(y_part, y, RING)
        )
        pltpu.make_async_remote_copy(
            src_ref=blocks.at[dest],
            dst_ref=arrived.at[me],
            send_sem=rim_send,
            recv_sem=rim_recv,
            device_id={"grid": dest},
            device_id_type=MESH,
        ).start()
    g_out[...] = g_buf[pl.ds(0, ROWS), :]
    others = blocks.at[pl.ds(0, count - 1)]
    pltpu.make_async_copy(others, others, rim_send).wait()
    pltpu.make_async_copy(arrived, arrived, rim_recv).wait()

    slot_rows[...] = arrived[...].astype(F32).reshape(count * 8, LAT)
    halves = []
    for j in range(2):
        halves.append(
            jnp.concatenate(
                [slot_rows[pl.ds(j * 3 + c, RIM, stride=8), :] for c in range(3)], axis=1
            )
        )
    spectra = jnp.concatenate(halves, axis=0)
    told = spectra[:, 256:]
    cell = told[:, FACT : FACT + 1] * float(LAT) + told[:, FACT + 1 : FACT + 2]
    cells = lax.broadcasted_iota(jnp.int32, (2 * RIM, LON * LAT), 1).astype(F32)
    hit = cell == cells
    rate_high = jnp.where(hit, told[:, FACT + 2 : FACT + 3], 0.0)
    rate_low = jnp.where(hit, told[:, FACT + 3 : FACT + 4], 0.0)
    remains = 1.0 - jnp.sum(rate_high + rate_low, axis=0, keepdims=True)
    turned = spectra.T.astype(BF16)
    gained = jnp.dot(turned, rate_high.astype(BF16), preferred_element_type=F32)
    gained += jnp.dot(turned, rate_low.astype(BF16), preferred_element_type=F32)
    for lon in range(LON):
        lanes = slice(lon * LAT, (lon + 1) * LAT)
        held = nest[pl.ds(lon, BINS, stride=LON), :]
        n_out[pl.ds(lon, BINS, stride=LON), :] = held * remains[:, lanes] + gained[:BINS, lanes]


def per_device(
    energy, nest_energy, ocean_mask, wind_field, rim_cell, rim_dest, rim_target, rim_weight
):
    count = lax.axis_size("grid")
    cosine, sine, secant, scalars = tables()
    vmem = pl.BlockSpec(memory_space=pltpu.VMEM)
    flat = jax.ShapeDtypeStruct((ROWS, LAT), F32)
    dma = pltpu.SemaphoreType.DMA

    def body(*refs):
        kernel(count, *refs)

    global_next, nest_next = pl.pallas_call(
        body,
        out_shape=(flat, flat),
        in_specs=[pl.BlockSpec(memory_space=pltpu.HBM)] * 12,
        out_specs=(vmem, vmem),
        scratch_shapes=[
            pltpu.VMEM((ROWS, LAT), F32),
            pltpu.VMEM((ROWS, LAT), F32),
            pltpu.VMEM((LON, LAT), jnp.int32),
            pltpu.VMEM((2, LON, LAT), F32),
            pltpu.VMEM((2, RIM), jnp.int32),
            pltpu.VMEM((1, RIM), jnp.int32),
            pltpu.VMEM((1, RIM), jnp.int32),
            pltpu.VMEM((3, RIM), F32),
            pltpu.VMEM((BAND_ROWS, LAT), F32),
            pltpu.VMEM((BAND_ROWS, LAT), F32),
            pltpu.VMEM((8, LAT), F32),
            pltpu.SMEM((128,), F32),
            pltpu.VMEM((RIM, RIM), F32),
            pltpu.VMEM((PACKET, LAT), F32),
            pltpu.VMEM((PACKET, LAT), F32),
            pltpu.VMEM((2, PACKET, LAT), BF16),
            pltpu.VMEM((2, PACKET, LAT), BF16),
            pltpu.VMEM((2, PACKET, LAT), BF16),
            pltpu.VMEM((2, PACKET, LAT), BF16),
            pltpu.VMEM((ROWS, LAT), F32),
            pltpu.VMEM((ROWS, LAT), F32),
            pltpu.VMEM((BANDS + 2 * REACH, PAIRS + 4, 8, LAT), F32),
            pltpu.VMEM((BANDS + 2 * REACH, PAIRS + 4, 8, LAT), F32),
            pltpu.VMEM((BANDS, BAND_ROWS, LAT), BF16),
            pltpu.VMEM((REACH, BAND_ROWS, LAT), BF16),
            pltpu.VMEM((REACH, BAND_ROWS, LAT), BF16),
            pltpu.VMEM((PAIRS, 8, LAT), F32),
            pltpu.VMEM((ROWS, LAT), F32),
            pltpu.VMEM((WIDTH * LON, LAT), F32),
            pltpu.VMEM((8, LAT), F32),
            pltpu.VMEM((4, 8, LAT), F32),
            pltpu.VMEM((WIDTH, LAT), BF16),
            pltpu.VMEM((WIDTH, LAT), BF16),
            pltpu.VMEM((LON + 1, RIM, LAT), BF16),
            pltpu.VMEM((LON + 1, RIM, LAT), BF16),
            pltpu.VMEM((2 * RIM, RIM), BF16),
            pltpu.VMEM((RIM, LAT), F32),
            pltpu.VMEM((count * 8, LAT), F32),
            pltpu.VMEM((count, 8, LAT), BF16),
            pltpu.VMEM((count, 8, LAT), BF16),
            dma((12,)),
            dma((4,)),
            dma((4,)),
            dma((2,)),
            dma((2,)),
            dma((4,)),
            dma((4,)),
            dma((2,)),
            dma((2,)),
            dma,
            dma,
            pltpu.SemaphoreType.REGULAR,
            pltpu.SemaphoreType.REGULAR,
        ],
        compiler_params=pltpu.CompilerParams(
            collective_id=0, has_side_effects=True, vmem_limit_bytes=40 << 20
        ),
        name="wave_step",
    )(
        *(
            pltpu.with_memory_space_constraint(x, pltpu.HBM)
            for x in (
                energy.reshape(ROWS, LAT),
                nest_energy.reshape(ROWS, LAT),
                ocean_mask,
                wind_field,
                rim_cell.T,
                rim_dest.T,
                rim_target.reshape(1, RIM),
                rim_weight.T,
                jnp.asarray(cosine),
                jnp.asarray(sine),
                jnp.asarray(secant),
                jnp.asarray(scalars),
            )
        )
    )
    shape = energy.shape
    return (global_next.reshape(shape), nest_next.reshape(shape))


def solution(mesh):
    in_specs = (
        P("spec", None, "grid", None),
        P("spec", None, "grid", None),
        P("grid", None),
        P(None, "grid", None),
        P("grid", None),
        P("grid", None),
        P("grid"),
        P("grid", None),
    )
    out_specs = (P("spec", None, "grid", None), P("spec", None, "grid", None))
    return jax.shard_map(
        per_device, mesh=mesh, in_specs=in_specs, out_specs=out_specs, check_vma=False
    )
```

```python
import jax
import jax.numpy as jnp
import numpy as np
from jax import lax
from jax.experimental import pallas as pl
from jax.experimental.pallas import tpu as pltpu
from jax.sharding import PartitionSpec as P

FREQS = 36
ANGLES = 36
LON = 4
LAT = 128
RIM = 128
BANDS = 9
REACH = 5
BINS = BANDS * ANGLES
ROWS = BINS * LON
BAND_ROWS = ANGLES * LON
PAIRS = BAND_ROWS // 8
PACKET = 192
FIRST_ROWS = 144
EAST = 336
RING = 8
SETTLE_LIMIT = 16 << 20
WIDTH = 384
FACT = BINS - 256
MESH = pl.DeviceIdType.MESH
F32 = jnp.float32
BF16 = jnp.bfloat16

ratio_step = 1.1
speed_coef = 0.054
wind_coef = 0.05
dissip_coef = 0.2
nonlin_coef = 0.12
nest_speedup = 2.0


def tables():
    heading = 2.0 * np.pi * np.arange(ANGLES) / ANGLES
    cosine, sine = np.cos(heading), np.sin(heading)
    cosine[[9, 27]] = 0.0
    sine[[0, 18]] = 0.0

    def spread(x):
        rows = np.repeat(x, LON)
        return np.broadcast_to(rows[:, None], (BAND_ROWS, LAT)).astype(np.float32)

    degrees = -60.0 + 120.0 * (np.arange(LAT) + 0.5) / LAT
    secant = np.broadcast_to(1.0 / np.cos(degrees * np.pi / 180.0), (8, LAT)).astype(np.float32)
    bands = np.arange(-REACH, FREQS + REACH)
    ratio = ratio_step ** (bands - FREQS // 2).astype(np.float64)
    scalars = np.zeros((128,), np.float32)
    scalars[: 2 * ratio.size] = np.concatenate([ratio, 1.0 / ratio])
    return spread(cosine), spread(sine), secant, scalars


RATIO_COUNT = FREQS + 2 * REACH
MEAN_SCALE = float(
    1.0 / (ANGLES * 0.1 * np.sum(ratio_step ** (np.arange(FREQS) - FREQS // 2.0)))
)


def dot_nt(a, b):
    return lax.dot_general(a, b, (((1,), (1,)), ((), ())), preferred_element_type=F32)


def split_16(x):
    high = x.astype(BF16)
    return high, (x - high.astype(F32)).astype(BF16)


def far_first():
    def hops(step):
        z, x, y = step
        return min(z, RING - z) + 2 * x + min(y, RING - y)

    steps = [(z, x, y) for z in range(RING) for x in range(2) for y in range(RING)]
    return sorted(steps[1:], key=lambda step: -hops(step))


def kernel(
    count,
    e_hbm,
    n_hbm,
    mask_hbm,
    wind_hbm,
    cell_hbm,
    dest_hbm,
    target_hbm,
    weight_hbm,
    cos_hbm,
    sin_hbm,
    sec_hbm,
    scalar_hbm,
    g_out,
    nest,
    arrived,
    e_ref,
    n_ref,
    mask_ref,
    wind_ref,
    cell_ref,
    dest_ref,
    target_ref,
    weight_ref,
    cos_ref,
    sin_ref,
    sec_ref,
    scalar_ref,
    rim_rows,
    stage_a,
    stage_b,
    e_send,
    n_send,
    e_recv,
    n_recv,
    halo_e,
    halo_n,
    even,
    odd,
    bands_16,
    low_halo,
    high_halo,
    gain,
    g_buf,
    part,
    parts,
    col_send,
    col_recv,
    share_high,
    share_low,
    hot,
    facts,
    blocks,
    in_sem,
    lon_send,
    lon_recv,
    band_send,
    band_recv,
    sum_send,
    sum_recv,
    col_ssem,
    col_rsem,
    rim_send,
    rim_recv,
    ring_sem,
    half_sem,
):
    sources = (
        e_hbm, n_hbm, scalar_hbm, mask_hbm, cos_hbm, sin_hbm, sec_hbm, wind_hbm,
        cell_hbm, dest_hbm, target_hbm, weight_hbm,
    )
    places = (
        e_ref, n_ref, scalar_ref, mask_ref, cos_ref, sin_ref, sec_ref, wind_ref,
        cell_ref, dest_ref, target_ref, weight_ref,
    )
    loads = [
        pltpu.make_async_copy(source, place, in_sem.at[i])
        for i, (source, place) in enumerate(zip(sources, places))
    ]
    loads[0].start()
    loads[1].start()
    me = lax.axis_index("grid")
    spec = lax.axis_index("spec")
    specs = FREQS // BANDS
    first = spec * BANDS
    west = lax.rem(me + count - 1, count)
    east = lax.rem(me + 1, count)
    barrier = pltpu.get_barrier_semaphore()

    def ratio(band):
        return scalar_ref[first + band]

    def inverse(band):
        return scalar_ref[first + band + RATIO_COUNT]

    z_part = me // (2 * RING)
    x_part = lax.rem(me // RING, 2)
    y_part = lax.rem(me, RING)

    def place_of(z, x, y):
        return (z * 2 + x) * RING + y

    def turned_by(part, step, size):
        return lax.rem(part + step, size) if step else part

    def tell(sem, to):
        pl.semaphore_signal(sem, inc=1, device_id=to, device_id_type=MESH)

    tell(barrier, {"grid": west})
    tell(barrier, {"grid": east})
    for i in range(1, specs):
        tell(barrier, {"spec": lax.rem(spec + i, specs)})
    z_peers = [place_of(turned_by(z_part, i, RING), x_part, y_part) for i in range(1, RING)]
    x_peer = place_of(z_part, 1 - x_part, y_part)
    for i in range(1, RING):
        tell(barrier, {"grid": place_of(z_part, x_part, turned_by(y_part, i, RING))})
    for peer in z_peers:
        tell(barrier, {"grid": peer})
    tell(barrier, {"grid": x_peer})
    for load in loads[2:]:
        load.start()

    packet_rows = lax.broadcasted_iota(jnp.int32, (PACKET, LAT), 0)
    angle = lax.rem(packet_rows, ANGLES)
    eastward = (angle < 10) | (angle >= 28)
    stage_a[...] = jnp.zeros_like(stage_a)
    stage_b[...] = jnp.zeros_like(stage_b)
    direct = 5 * ANGLES
    folded = BINS - direct

    def pack(source, send):
        for index, lon, picked in ((0, LON - 1, eastward), (1, 0, ~eastward)):
            stage_a[pl.ds(0, direct), :] = source[pl.ds(lon, direct, stride=LON), :]
            stage_b[pl.ds(18, folded), :] = source[pl.ds(direct * LON + lon, folded, stride=LON), :]
            send[index] = jnp.where(picked, stage_a[...], stage_b[...]).astype(BF16)

    loads[0].wait()
    pack(e_ref, e_send)
    pl.semaphore_wait(barrier, 2 + specs - 1 + 2 * (RING - 1) + 1)

    def lon_copies(send, recv, base):
        return [
            pltpu.make_async_remote_copy(
                src_ref=send.at[index],
                dst_ref=recv.at[index],
                send_sem=lon_send.at[base + index],
                recv_sem=lon_recv.at[base + index],
                device_id={"grid": to},
                device_id_type=MESH,
            )
            for index, to in ((0, east), (1, west))
        ]

    e_lon = lon_copies(e_send, e_recv, 0)
    n_lon = lon_copies(n_send, n_recv, 2)
    for copy in e_lon:
        copy.start()
    for peer in z_peers:
        tell(ring_sem, {"grid": peer})
    for load in loads[2:]:
        load.wait()
    loads[1].wait()
    pack(n_ref, n_send)

    lane = lax.broadcasted_iota(jnp.int32, (RIM, LAT), 1)
    sub = lax.broadcasted_iota(jnp.int32, (RIM, LAT), 0)
    rim_rows[...] = jnp.zeros_like(rim_rows)
    rim_rows[pl.ds(0, 2), :] = cell_ref[...].astype(F32)
    rim_rows[pl.ds(2, 1), :] = dest_ref[...].astype(F32)
    rim_rows[pl.ds(3, 1), :] = target_ref[...].astype(F32)
    rim_rows[pl.ds(4, 3), :] = weight_ref[...]
    rim_cols = rim_rows[...].T
    local_col = rim_cols[:, 0:1].astype(jnp.int32) - me * LON
    row = rim_cols[:, 1:2].astype(jnp.int32)
    dest_col = rim_cols[:, 2:3]
    target_col = rim_cols[:, 3:4].astype(jnp.int32)
    ex = rim_cols[:, 4:5]
    ny = rim_cols[:, 5:6]
    relax = rim_cols[:, 6:7]
    row_share = jnp.where(lane == row, 1.0 - ny, jnp.where(lane == row + 1, ny, 0.0))
    for lon in range(LON + 1):
        col_share = jnp.where(
            local_col == lon, 1.0 - ex, jnp.where(local_col == lon - 1, ex, 0.0)
        )
        high, low = split_16(col_share * row_share)
        share_high[lon] = high
        share_low[lon] = low
    dest_row = dest_ref[...].astype(F32)
    same = dest_col == dest_row
    slot_row = jnp.sum(jnp.where(same & (sub < lane), 1.0, 0.0), axis=0, keepdims=True)
    places = lax.broadcasted_iota(jnp.int32, (2 * RIM, LAT), 0)
    named = (dest_row == (places >> 1).astype(F32)) & (slot_row == (places & 1).astype(F32))
    hot[...] = jnp.where(named, 1.0, 0.0).astype(BF16)
    relax_high = relax.astype(BF16).astype(F32)
    fact = jnp.where(lane == FACT, (target_col >> 7).astype(F32), 0.0)
    fact = jnp.where(lane == FACT + 1, (target_col & 127).astype(F32), fact)
    fact = jnp.where(lane == FACT + 2, relax_high, fact)
    fact = jnp.where(lane == FACT + 3, relax - relax_high, fact)
    facts[...] = fact
    pair_shape = (PAIRS, 8, LAT)
    cosine = cos_ref[...].reshape(pair_shape)
    sine = sin_ref[...].reshape(pair_shape)
    wind = wind_ref[...]
    wind_x = jnp.concatenate([wind[0], wind[0]], axis=0)[None]
    wind_y = jnp.concatenate([wind[1], wind[1]], axis=0)[None]
    gain[...] = wind_coef * jnp.maximum(wind_x * cosine + wind_y * sine, 0.0)
    mask_half = mask_ref[...].astype(F32)
    mask = jnp.concatenate([mask_half, mask_half], axis=0)[None]
    secant = sec_ref[...][None]

    vreg_sub = lax.broadcasted_iota(jnp.int32, (1, 8, LAT), 1)
    vreg_lane = lax.broadcasted_iota(jnp.int32, (1, 8, LAT), 2)
    lon_of = vreg_sub & 3

    def upwind(block, halo):
        before = jnp.where(lon_of == 0, halo, pltpu.roll(block, 1, axis=1))
        after = jnp.where(lon_of == LON - 1, halo, pltpu.roll(block, 7, axis=1))
        along_lon = jnp.concatenate([before[:5], after[5:14], before[14:]], axis=0)
        south = jnp.where(vreg_lane == 0, 0.0, pltpu.roll(block, 1, axis=2))
        north = jnp.where(vreg_lane == LAT - 1, 0.0, pltpu.roll(block, LAT - 1, axis=2))
        along_lat = jnp.concatenate([south[:9], north[9:]], axis=0)
        return block - along_lon, block - along_lat

    def rows_of(ref, band):
        return ref[pl.ds(pl.multiple_of(band * BAND_ROWS, 8), BAND_ROWS), :].reshape(pair_shape)

    def cyclic(ref, band, value):
        ref[band, pl.ds(2, PAIRS)] = value
        ref[band, pl.ds(0, 2)] = value[PAIRS - 2 :]
        ref[band, pl.ds(PAIRS + 2, 2)] = value[:2]

    def keep(band, value):
        cyclic(even, band, value)
        turned = pltpu.roll(value, 4, axis=1)
        following = jnp.concatenate([turned[1:], turned[:1]], axis=0)
        cyclic(odd, band, jnp.where(vreg_sub < 4, turned, following))

    def unpack(recv, halo, lower, upper):
        for index, lon, factor in ((0, 0, lower), (1, LON - 1, upper)):
            stage_a[...] = recv[index].astype(F32)
            front = stage_a[pl.ds(0, direct), :]
            rest = stage_a[pl.ds(18, folded), :]
            if factor is not None:
                front, rest = front * factor, rest * factor
            halo[pl.ds(lon, direct, stride=LON), :] = front
            halo[pl.ds(direct * LON + lon, folded, stride=LON), :] = rest

    for copy in e_lon:
        copy.wait()
    unpack(e_recv, halo_e, None, None)

    backward = lax.rem(spec, 2) == 1

    def advect_band(index, total):
        band = jnp.where(backward, BANDS - 1 - index, index)
        block = rows_of(e_ref, band)
        lon_step, lat_step = upwind(block, rows_of(halo_e, band))
        speed = speed_coef * inverse(band + REACH)
        along_x = jnp.abs(rows_of(cos_ref, 0)) * secant
        along_y = jnp.abs(rows_of(sin_ref, 0))
        moved = (block - speed * (along_x * lon_step + along_y * lat_step)) * mask
        keep(band + REACH, moved)
        bands_16[band] = moved.reshape(BAND_ROWS, LAT).astype(BF16)
        return total + 0.1 * ratio(band + REACH) * jnp.sum(moved, axis=0)

    def band_copy(start, recv, index, to):
        return pltpu.make_async_remote_copy(
            src_ref=bands_16.at[pl.ds(start, REACH)],
            dst_ref=recv,
            send_sem=band_send.at[index],
            recv_sem=band_recv.at[index],
            device_id={"spec": to},
            device_id_type=MESH,
        )

    upward = band_copy(BANDS - REACH, low_halo, 0, lax.rem(spec + 1, specs))
    downward = band_copy(0, high_halo, 1, lax.rem(spec + specs - 1, specs))
    total = lax.fori_loop(0, REACH, advect_band, jnp.zeros((8, LAT), F32))

    @pl.when((spec > 0) & ~backward)
    def _():
        downward.start()

    @pl.when((spec < specs - 1) & backward)
    def _():
        upward.start()

    part[...] = lax.fori_loop(REACH, BANDS, advect_band, total)

    @pl.when((spec > 0) & backward)
    def _():
        downward.start()

    @pl.when((spec < specs - 1) & ~backward)
    def _():
        upward.start()

    sums = []
    for i in range(1, specs):
        sums.append(
            pltpu.make_async_remote_copy(
                src_ref=part,
                dst_ref=parts.at[i],
                send_sem=sum_send.at[i],
                recv_sem=sum_recv.at[i],
                device_id={"spec": lax.rem(spec + i, specs)},
                device_id_type=MESH,
            )
        )
    for copy in sums:
        copy.start()

    pl.semaphore_wait(ring_sem, RING - 1)
    tell(half_sem, {"grid": x_peer})

    for copy in n_lon:
        copy.start()

    chunk = 6

    def product(centre, upper, lower):
        return centre * (centre * (upper + lower) - 2.0 * upper * lower)

    def own_terms(here, at, band):
        terms = [product(here, at(odd, 2, (3 * s - 1) // 2), at(odd, -3, (-s - 1) // 2)) for s in (1, -1)]
        return (-2.0 * nonlin_coef * ratio(band + REACH)) * (terms[0] + terms[1])

    def below_terms(here, at, band):
        terms = [product(at(odd, -2, (-3 * s - 1) // 2), here, at(even, -5, -2 * s)) for s in (1, -1)]
        return (nonlin_coef * ratio(band + REACH - 2)) * (terms[0] + terms[1])

    def above_terms(here, at, band):
        terms = [product(at(odd, 3, (s - 1) // 2), at(even, 5, 2 * s), here) for s in (1, -1)]
        return (nonlin_coef * ratio(band + REACH + 3)) * (terms[0] + terms[1])

    def add_terms(begin, end, kinds, opening, damped):
        def step(band, carry):
            if damped:
                loss = ratio(band + REACH)
                inverse_loss = (1.0 / (1.0 + dissip_coef * loss * loss * damped[0]))[None]
            for piece in range(PAIRS // chunk):
                base = 2 + piece * chunk

                def at(ref, offset, turn):
                    return ref[band + REACH + offset, pl.ds(base + turn, chunk)]

                here = at(even, 0, 0)
                rows = pl.ds(pl.multiple_of(band * BAND_ROWS + piece * chunk * 8, 8), chunk * 8)
                if opening:
                    total = here * (1.0 + ratio(band + REACH) * gain[pl.ds(piece * chunk, chunk)])
                else:
                    total = g_buf[rows, :].reshape(chunk, 8, LAT)
                for kind in kinds:
                    total += kind(here, at, band)
                if damped:
                    total *= inverse_loss
                g_buf[rows, :] = total.reshape(chunk * 8, LAT)
            return carry

        lax.fori_loop(begin, end, step, 0)

    add_terms(0, 3, (above_terms,), True, ())
    add_terms(3, 4, (own_terms, above_terms), True, ())
    add_terms(4, 5, (own_terms,), True, ())
    add_terms(5, 7, (own_terms, below_terms), True, ())
    add_terms(7, 9, (below_terms,), True, ())

    for copy in sums:
        copy.wait()
    whole = part[...] + parts[1] + parts[2] + parts[3]
    mean = (whole + pltpu.roll(whole, 4, axis=0)) * MEAN_SCALE

    @pl.when(spec < specs - 1)
    def _():
        upward.wait_send()
        downward.wait_recv()

    @pl.when(spec > 0)
    def _():
        upward.wait_recv()
        downward.wait_send()

    def halo_bands(band, carry):
        low = low_halo[band].astype(F32).reshape(pair_shape)
        keep(band, jnp.where(spec > 0, low, 0.0))
        high = high_halo[band].astype(F32).reshape(pair_shape)
        keep(band + BANDS + REACH, jnp.where(spec < specs - 1, high, 0.0))
        return carry

    lax.fori_loop(0, REACH, halo_bands, 0)

    def column_copy(start, rows, index):
        return pltpu.make_async_remote_copy(
            src_ref=col_send.at[pl.ds(start, rows)],
            dst_ref=col_recv.at[pl.ds(start, rows)],
            send_sem=col_ssem.at[index],
            recv_sem=col_rsem.at[index],
            device_id={"grid": west},
            device_id_type=MESH,
        )

    columns = [column_copy(0, FIRST_ROWS, 0), column_copy(FIRST_ROWS, EAST - FIRST_ROWS, 1)]
    g_buf[pl.ds(ROWS, WIDTH * LON - ROWS), :] = jnp.zeros((WIDTH * LON - ROWS, LAT), F32)
    col_recv[pl.ds(EAST, WIDTH - EAST), :] = jnp.zeros((WIDTH - EAST, LAT), BF16)
    add_terms(0, 3, (own_terms, below_terms), False, (mean,))
    add_terms(3, 4, (below_terms,), False, (mean,))
    col_send[pl.ds(0, FIRST_ROWS), :] = g_buf[pl.ds(0, FIRST_ROWS, stride=LON), :].astype(BF16)
    columns[0].start()
    add_terms(4, 5, (below_terms, above_terms), False, (mean,))
    add_terms(5, 7, (above_terms,), False, (mean,))
    add_terms(7, 9, (own_terms, above_terms), False, (mean,))
    col_send[pl.ds(FIRST_ROWS, EAST - FIRST_ROWS), :] = g_buf[
        pl.ds(FIRST_ROWS * LON, EAST - FIRST_ROWS, stride=LON), :
    ].astype(BF16)
    columns[1].start()

    boundary = jnp.zeros((RIM, WIDTH), F32)
    for lon in range(LON):
        high, low = split_16(g_buf[pl.ds(lon, WIDTH, stride=LON), :])
        boundary += dot_nt(share_high[lon], high)
        boundary += dot_nt(share_high[lon], low)
        boundary += dot_nt(share_low[lon], high)
    for copy in columns:
        copy.wait()
    boundary += dot_nt(share_high[LON], col_recv[...])
    boundary += dot_nt(share_low[LON], col_recv[...])
    boundary = jnp.concatenate([boundary[:, :256], boundary[:, 256:] + facts[...]], axis=1)
    packed = jnp.dot(hot[...], boundary.astype(BF16), preferred_element_type=F32)
    for c in range(3):
        lanes = packed[:, c * LAT : (c + 1) * LAT].astype(BF16)
        blocks[c] = lanes.reshape(count, 2, LAT)

    own_block = pltpu.make_async_copy(blocks.at[:, me], arrived.at[:, me], rim_recv)
    own_block.start()

    pl.semaphore_wait(half_sem, 1)
    for z, x, y in far_first():
        dest = place_of(
            turned_by(z_part, z, RING), 1 - x_part if x else x_part, turned_by(y_part, y, RING)
        )
        pltpu.make_async_remote_copy(
            src_ref=blocks.at[:, dest],
            dst_ref=arrived.at[:, me],
            send_sem=rim_send,
            recv_sem=rim_recv,
            device_id={"grid": dest},
            device_id_type=MESH,
        ).start()
    g_out[...] = g_buf[pl.ds(0, ROWS), :]
    quarter = count // 4
    lower_keep = jnp.where((me != quarter) & (me != 3 * quarter), 1.0, 0.0)
    upper_keep = jnp.where((me != quarter - 1) & (me != 3 * quarter - 1), 1.0, 0.0)
    for copy in n_lon:
        copy.wait()
    unpack(n_recv, halo_n, lower_keep, upper_keep)

    def advect_nest(band, carry):
        block = rows_of(n_ref, band)
        lon_step, lat_step = upwind(block, rows_of(halo_n, band))
        speed = nest_speedup * speed_coef * inverse(band + REACH)
        along_x = jnp.abs(rows_of(cos_ref, 0))
        along_y = jnp.abs(rows_of(sin_ref, 0))
        moved = block - speed * (along_x * lon_step + along_y * lat_step)
        nest[pl.ds(pl.multiple_of(band * BAND_ROWS, 8), BAND_ROWS), :] = moved.reshape(BAND_ROWS, LAT)
        return carry

    lax.fori_loop(0, BANDS, advect_nest, 0)

    others = blocks.at[:, pl.ds(0, count - 1)]
    pltpu.make_async_copy(others, others, rim_send).wait()
    pltpu.make_async_copy(arrived, arrived, rim_recv).wait()


def settle(arrived, nest, g_next, g_out, n_out, n_buf, out_sem):
    g_copy = pltpu.make_async_copy(g_next, g_out, out_sem.at[0])
    g_copy.start()
    spectra = jnp.concatenate(
        [arrived[c].reshape(2 * RIM, LAT).astype(F32) for c in range(3)], axis=1
    )
    told = spectra[:, 256:]
    cell = told[:, FACT : FACT + 1] * float(LAT) + told[:, FACT + 1 : FACT + 2]
    cells = lax.broadcasted_iota(jnp.int32, (2 * RIM, LON * LAT), 1).astype(F32)
    hit = cell == cells
    rate_high = jnp.where(hit, told[:, FACT + 2 : FACT + 3], 0.0)
    rate_low = jnp.where(hit, told[:, FACT + 3 : FACT + 4], 0.0)
    remains = 1.0 - jnp.sum(rate_high + rate_low, axis=0, keepdims=True)
    turned = spectra.T.astype(BF16)
    gained = jnp.dot(turned, rate_high.astype(BF16), preferred_element_type=F32)
    gained += jnp.dot(turned, rate_low.astype(BF16), preferred_element_type=F32)
    for lon in range(LON):
        lanes = slice(lon * LAT, (lon + 1) * LAT)
        held = nest[pl.ds(lon, BINS, stride=LON), :]
        n_buf[pl.ds(lon, BINS, stride=LON), :] = held * remains[:, lanes] + gained[:BINS, lanes]
    n_copy = pltpu.make_async_copy(n_buf, n_out, out_sem.at[1])
    n_copy.start()
    g_copy.wait()
    n_copy.wait()


def per_device(
    energy, nest_energy, ocean_mask, wind_field, rim_cell, rim_dest, rim_target, rim_weight
):
    count = lax.axis_size("grid")
    cosine, sine, secant, scalars = tables()
    vmem = pl.BlockSpec(memory_space=pltpu.VMEM)
    flat = jax.ShapeDtypeStruct((ROWS, LAT), F32)
    dma = pltpu.SemaphoreType.DMA

    def body(*refs):
        kernel(count, *refs)

    global_rows, nest_rows, arrived = pl.pallas_call(
        body,
        out_shape=(flat, flat, jax.ShapeDtypeStruct((3, count, 2, LAT), BF16)),
        in_specs=[pl.BlockSpec(memory_space=pltpu.HBM)] * 12,
        out_specs=(vmem, vmem, vmem),
        scratch_shapes=[
            pltpu.VMEM((ROWS, LAT), F32),
            pltpu.VMEM((ROWS, LAT), F32),
            pltpu.VMEM((LON, LAT), jnp.int32),
            pltpu.VMEM((2, LON, LAT), F32),
            pltpu.VMEM((2, RIM), jnp.int32),
            pltpu.VMEM((1, RIM), jnp.int32),
            pltpu.VMEM((1, RIM), jnp.int32),
            pltpu.VMEM((3, RIM), F32),
            pltpu.VMEM((BAND_ROWS, LAT), F32),
            pltpu.VMEM((BAND_ROWS, LAT), F32),
            pltpu.VMEM((8, LAT), F32),
            pltpu.SMEM((128,), F32),
            pltpu.VMEM((RIM, RIM), F32),
            pltpu.VMEM((PACKET, LAT), F32),
            pltpu.VMEM((PACKET, LAT), F32),
            pltpu.VMEM((2, PACKET, LAT), BF16),
            pltpu.VMEM((2, PACKET, LAT), BF16),
            pltpu.VMEM((2, PACKET, LAT), BF16),
            pltpu.VMEM((2, PACKET, LAT), BF16),
            pltpu.VMEM((ROWS, LAT), F32),
            pltpu.VMEM((ROWS, LAT), F32),
            pltpu.VMEM((BANDS + 2 * REACH, PAIRS + 4, 8, LAT), F32),
            pltpu.VMEM((BANDS + 2 * REACH, PAIRS + 4, 8, LAT), F32),
            pltpu.VMEM((BANDS, BAND_ROWS, LAT), BF16),
            pltpu.VMEM((REACH, BAND_ROWS, LAT), BF16),
            pltpu.VMEM((REACH, BAND_ROWS, LAT), BF16),
            pltpu.VMEM((PAIRS, 8, LAT), F32),
            pltpu.VMEM((WIDTH * LON, LAT), F32),
            pltpu.VMEM((8, LAT), F32),
            pltpu.VMEM((4, 8, LAT), F32),
            pltpu.VMEM((WIDTH, LAT), BF16),
            pltpu.VMEM((WIDTH, LAT), BF16),
            pltpu.VMEM((LON + 1, RIM, LAT), BF16),
            pltpu.VMEM((LON + 1, RIM, LAT), BF16),
            pltpu.VMEM((2 * RIM, RIM), BF16),
            pltpu.VMEM((RIM, LAT), F32),
            pltpu.VMEM((3, count, 2, LAT), BF16),
            dma((12,)),
            dma((4,)),
            dma((4,)),
            dma((2,)),
            dma((2,)),
            dma((4,)),
            dma((4,)),
            dma((2,)),
            dma((2,)),
            dma,
            dma,
            pltpu.SemaphoreType.REGULAR,
            pltpu.SemaphoreType.REGULAR,
        ],
        compiler_params=pltpu.CompilerParams(
            collective_id=0, has_side_effects=True, vmem_limit_bytes=40 << 20
        ),
        name="wave_step",
    )(
        *(
            pltpu.with_memory_space_constraint(x, pltpu.HBM)
            for x in (
                energy.reshape(ROWS, LAT),
                nest_energy.reshape(ROWS, LAT),
                ocean_mask,
                wind_field,
                rim_cell.T,
                rim_dest.T,
                rim_target.reshape(1, RIM),
                rim_weight.T,
                jnp.asarray(cosine),
                jnp.asarray(sine),
                jnp.asarray(secant),
                jnp.asarray(scalars),
            )
        )
    )
    hbm = pl.BlockSpec(memory_space=pl.ANY)
    global_next, nest_next = pl.pallas_call(
        settle,
        out_shape=(flat, flat),
        in_specs=[vmem] * 3,
        out_specs=(hbm, hbm),
        scratch_shapes=[
            pltpu.VMEM((ROWS, LAT), F32),
            dma((2,)),
        ],
        compiler_params=pltpu.CompilerParams(vmem_limit_bytes=SETTLE_LIMIT),
        name="settle",
    )(arrived, nest_rows, global_rows)
    shape = energy.shape
    return (global_next.reshape(shape), nest_next.reshape(shape))


def solution(mesh):
    in_specs = (
        P("spec", None, "grid", None),
        P("spec", None, "grid", None),
        P("grid", None),
        P(None, "grid", None),
        P("grid", None),
        P("grid", None),
        P("grid"),
        P("grid", None),
    )
    out_specs = (P("spec", None, "grid", None), P("spec", None, "grid", None))
    return jax.shard_map(
        per_device, mesh=mesh, in_specs=in_specs, out_specs=out_specs, check_vma=False
    )
```

```python
import jax
import jax.numpy as jnp
import numpy as np
from jax import lax
from jax.experimental import pallas as pl
from jax.experimental.pallas import tpu as pltpu
from jax.sharding import PartitionSpec as P

FREQS = 36
ANGLES = 36
LON = 4
LAT = 128
RIM = 128
BANDS = 9
REACH = 5
BINS = BANDS * ANGLES
ROWS = BINS * LON
BAND_ROWS = ANGLES * LON
PAIRS = BAND_ROWS // 8
PACKET = 192
FIRST_ROWS = 144
EAST = 336
RING = 8
SETTLE_LIMIT = 16 << 20
WIDTH = 384
FACT = BINS - 256
MESH = pl.DeviceIdType.MESH
F32 = jnp.float32
BF16 = jnp.bfloat16

ratio_step = 1.1
speed_coef = 0.054
wind_coef = 0.05
dissip_coef = 0.2
nonlin_coef = 0.12
nest_speedup = 2.0


def tables():
    heading = 2.0 * np.pi * np.arange(ANGLES) / ANGLES
    cosine, sine = np.cos(heading), np.sin(heading)
    cosine[[9, 27]] = 0.0
    sine[[0, 18]] = 0.0

    def spread(x):
        rows = np.repeat(x, LON)
        return np.broadcast_to(rows[:, None], (BAND_ROWS, LAT)).astype(np.float32)

    degrees = -60.0 + 120.0 * (np.arange(LAT) + 0.5) / LAT
    secant = np.broadcast_to(1.0 / np.cos(degrees * np.pi / 180.0), (8, LAT)).astype(np.float32)
    bands = np.arange(-REACH, FREQS + REACH)
    ratio = ratio_step ** (bands - FREQS // 2).astype(np.float64)
    scalars = np.zeros((128,), np.float32)
    scalars[: 2 * ratio.size] = np.concatenate([ratio, 1.0 / ratio])
    return spread(cosine), spread(sine), secant, scalars


RATIO_COUNT = FREQS + 2 * REACH
MEAN_SCALE = float(
    1.0 / (ANGLES * 0.1 * np.sum(ratio_step ** (np.arange(FREQS) - FREQS // 2.0)))
)


def dot_nt(a, b):
    return lax.dot_general(a, b, (((1,), (1,)), ((), ())), preferred_element_type=F32)


def split_16(x):
    high = x.astype(BF16)
    return high, (x - high.astype(F32)).astype(BF16)


def far_first():
    def hops(step):
        z, x, y = step
        return min(z, RING - z) + 2 * x + min(y, RING - y)

    steps = [(z, x, y) for z in range(RING) for x in range(2) for y in range(RING)]
    return sorted(steps[1:], key=lambda step: -hops(step))


def kernel(
    count,
    e_hbm,
    n_hbm,
    mask_hbm,
    wind_hbm,
    cell_hbm,
    dest_hbm,
    target_hbm,
    weight_hbm,
    cos_hbm,
    sin_hbm,
    sec_hbm,
    scalar_hbm,
    g_out,
    nest,
    arrived,
    e_ref,
    n_ref,
    mask_ref,
    wind_ref,
    cell_ref,
    dest_ref,
    target_ref,
    weight_ref,
    cos_ref,
    sin_ref,
    sec_ref,
    scalar_ref,
    rim_rows,
    stage_a,
    stage_b,
    e_send,
    n_send,
    e_recv,
    n_recv,
    halo_e,
    halo_n,
    even,
    odd,
    bands_16,
    low_halo,
    high_halo,
    gain,
    g_buf,
    part,
    parts,
    col_send,
    col_recv,
    share_high,
    share_low,
    hot,
    facts,
    blocks,
    in_sem,
    lon_send,
    lon_recv,
    band_send,
    band_recv,
    sum_send,
    sum_recv,
    col_ssem,
    col_rsem,
    rim_send,
    rim_recv,
    near_sem,
    ring_sem,
    half_sem,
):
    sources = (
        e_hbm, n_hbm, scalar_hbm, mask_hbm, cos_hbm, sin_hbm, sec_hbm, wind_hbm,
        cell_hbm, dest_hbm, target_hbm, weight_hbm,
    )
    places = (
        e_ref, n_ref, scalar_ref, mask_ref, cos_ref, sin_ref, sec_ref, wind_ref,
        cell_ref, dest_ref, target_ref, weight_ref,
    )
    loads = [
        pltpu.make_async_copy(source, place, in_sem.at[i])
        for i, (source, place) in enumerate(zip(sources, places))
    ]
    loads[0].start()
    loads[1].start()
    me = lax.axis_index("grid")
    spec = lax.axis_index("spec")
    specs = FREQS // BANDS
    first = spec * BANDS
    west = lax.rem(me + count - 1, count)
    east = lax.rem(me + 1, count)
    barrier = pltpu.get_barrier_semaphore()

    def ratio(band):
        return scalar_ref[first + band]

    def inverse(band):
        return scalar_ref[first + band + RATIO_COUNT]

    z_part = me // (2 * RING)
    x_part = lax.rem(me // RING, 2)
    y_part = lax.rem(me, RING)

    def place_of(z, x, y):
        return (z * 2 + x) * RING + y

    def turned_by(part, step, size):
        return lax.rem(part + step, size) if step else part

    def tell(sem, to):
        pl.semaphore_signal(sem, inc=1, device_id=to, device_id_type=MESH)

    tell(barrier, {"grid": west})
    tell(barrier, {"grid": east})
    for i in range(1, specs):
        tell(barrier, {"spec": lax.rem(spec + i, specs)})
    z_peers = [place_of(turned_by(z_part, i, RING), x_part, y_part) for i in range(1, RING)]
    x_peer = place_of(z_part, 1 - x_part, y_part)
    near = (1, RING - 1, 2, RING - 2)
    y_near = [place_of(z_part, x_part, turned_by(y_part, i, RING)) for i in near]
    z_near = [z_peers[i - 1] for i in near]
    for peer in y_near + z_near:
        tell(barrier, {"grid": peer})
    tell(barrier, {"grid": x_peer})
    for load in loads[2:]:
        load.start()

    packet_rows = lax.broadcasted_iota(jnp.int32, (PACKET, LAT), 0)
    angle = lax.rem(packet_rows, ANGLES)
    eastward = (angle < 10) | (angle >= 28)
    stage_a[...] = jnp.zeros_like(stage_a)
    stage_b[...] = jnp.zeros_like(stage_b)
    direct = 5 * ANGLES
    folded = BINS - direct

    def pack(source, send):
        for index, lon, picked in ((0, LON - 1, eastward), (1, 0, ~eastward)):
            stage_a[pl.ds(0, direct), :] = source[pl.ds(lon, direct, stride=LON), :]
            stage_b[pl.ds(18, folded), :] = source[pl.ds(direct * LON + lon, folded, stride=LON), :]
            send[index] = jnp.where(picked, stage_a[...], stage_b[...]).astype(BF16)

    loads[0].wait()
    pack(e_ref, e_send)
    pl.semaphore_wait(barrier, 2 + specs - 1 + 2 * len(near) + 1)

    def lon_copies(send, recv, base):
        return [
            pltpu.make_async_remote_copy(
                src_ref=send.at[index],
                dst_ref=recv.at[index],
                send_sem=lon_send.at[base + index],
                recv_sem=lon_recv.at[base + index],
                device_id={"grid": to},
                device_id_type=MESH,
            )
            for index, to in ((0, east), (1, west))
        ]

    e_lon = lon_copies(e_send, e_recv, 0)
    n_lon = lon_copies(n_send, n_recv, 2)
    for copy in e_lon:
        copy.start()
    for peer in y_near[2:] + z_near[2:]:
        tell(near_sem, {"grid": peer})
    for load in loads[2:]:
        load.wait()
    loads[1].wait()
    pack(n_ref, n_send)

    lane = lax.broadcasted_iota(jnp.int32, (RIM, LAT), 1)
    sub = lax.broadcasted_iota(jnp.int32, (RIM, LAT), 0)
    rim_rows[...] = jnp.zeros_like(rim_rows)
    rim_rows[pl.ds(0, 2), :] = cell_ref[...].astype(F32)
    rim_rows[pl.ds(2, 1), :] = dest_ref[...].astype(F32)
    rim_rows[pl.ds(3, 1), :] = target_ref[...].astype(F32)
    rim_rows[pl.ds(4, 3), :] = weight_ref[...]
    rim_cols = rim_rows[...].T
    local_col = rim_cols[:, 0:1].astype(jnp.int32) - me * LON
    row = rim_cols[:, 1:2].astype(jnp.int32)
    dest_col = rim_cols[:, 2:3]
    target_col = rim_cols[:, 3:4].astype(jnp.int32)
    ex = rim_cols[:, 4:5]
    ny = rim_cols[:, 5:6]
    relax = rim_cols[:, 6:7]
    row_share = jnp.where(lane == row, 1.0 - ny, jnp.where(lane == row + 1, ny, 0.0))
    for lon in range(LON + 1):
        col_share = jnp.where(
            local_col == lon, 1.0 - ex, jnp.where(local_col == lon - 1, ex, 0.0)
        )
        high, low = split_16(col_share * row_share)
        share_high[lon] = high
        share_low[lon] = low
    dest_row = dest_ref[...].astype(F32)
    same = dest_col == dest_row
    slot_row = jnp.sum(jnp.where(same & (sub < lane), 1.0, 0.0), axis=0, keepdims=True)
    places = lax.broadcasted_iota(jnp.int32, (2 * RIM, LAT), 0)
    named = (dest_row == (places >> 1).astype(F32)) & (slot_row == (places & 1).astype(F32))
    hot[...] = jnp.where(named, 1.0, 0.0).astype(BF16)
    relax_high = relax.astype(BF16).astype(F32)
    fact = jnp.where(lane == FACT, (target_col >> 7).astype(F32), 0.0)
    fact = jnp.where(lane == FACT + 1, (target_col & 127).astype(F32), fact)
    fact = jnp.where(lane == FACT + 2, relax_high, fact)
    fact = jnp.where(lane == FACT + 3, relax - relax_high, fact)
    facts[...] = fact
    pair_shape = (PAIRS, 8, LAT)
    cosine = cos_ref[...].reshape(pair_shape)
    sine = sin_ref[...].reshape(pair_shape)
    wind = wind_ref[...]
    wind_x = jnp.concatenate([wind[0], wind[0]], axis=0)[None]
    wind_y = jnp.concatenate([wind[1], wind[1]], axis=0)[None]
    gain[...] = wind_coef * jnp.maximum(wind_x * cosine + wind_y * sine, 0.0)
    mask_half = mask_ref[...].astype(F32)
    mask = jnp.concatenate([mask_half, mask_half], axis=0)[None]
    secant = sec_ref[...][None]

    vreg_sub = lax.broadcasted_iota(jnp.int32, (1, 8, LAT), 1)
    vreg_lane = lax.broadcasted_iota(jnp.int32, (1, 8, LAT), 2)
    lon_of = vreg_sub & 3

    def upwind(block, halo):
        before = jnp.where(lon_of == 0, halo, pltpu.roll(block, 1, axis=1))
        after = jnp.where(lon_of == LON - 1, halo, pltpu.roll(block, 7, axis=1))
        along_lon = jnp.concatenate([before[:5], after[5:14], before[14:]], axis=0)
        south = jnp.where(vreg_lane == 0, 0.0, pltpu.roll(block, 1, axis=2))
        north = jnp.where(vreg_lane == LAT - 1, 0.0, pltpu.roll(block, LAT - 1, axis=2))
        along_lat = jnp.concatenate([south[:9], north[9:]], axis=0)
        return block - along_lon, block - along_lat

    def rows_of(ref, band):
        return ref[pl.ds(pl.multiple_of(band * BAND_ROWS, 8), BAND_ROWS), :].reshape(pair_shape)

    def cyclic(ref, band, value):
        ref[band, pl.ds(2, PAIRS)] = value
        ref[band, pl.ds(0, 2)] = value[PAIRS - 2 :]
        ref[band, pl.ds(PAIRS + 2, 2)] = value[:2]

    def keep(band, value):
        cyclic(even, band, value)
        turned = pltpu.roll(value, 4, axis=1)
        following = jnp.concatenate([turned[1:], turned[:1]], axis=0)
        cyclic(odd, band, jnp.where(vreg_sub < 4, turned, following))

    def unpack(recv, halo, lower, upper):
        for index, lon, factor in ((0, 0, lower), (1, LON - 1, upper)):
            stage_a[...] = recv[index].astype(F32)
            front = stage_a[pl.ds(0, direct), :]
            rest = stage_a[pl.ds(18, folded), :]
            if factor is not None:
                front, rest = front * factor, rest * factor
            halo[pl.ds(lon, direct, stride=LON), :] = front
            halo[pl.ds(direct * LON + lon, folded, stride=LON), :] = rest

    for copy in e_lon:
        copy.wait_recv()
    unpack(e_recv, halo_e, None, None)

    backward = lax.rem(spec, 2) == 1

    def advect_band(index, total):
        band = jnp.where(backward, BANDS - 1 - index, index)
        block = rows_of(e_ref, band)
        lon_step, lat_step = upwind(block, rows_of(halo_e, band))
        speed = speed_coef * inverse(band + REACH)
        along_x = jnp.abs(rows_of(cos_ref, 0)) * secant
        along_y = jnp.abs(rows_of(sin_ref, 0))
        moved = (block - speed * (along_x * lon_step + along_y * lat_step)) * mask
        keep(band + REACH, moved)
        bands_16[band] = moved.reshape(BAND_ROWS, LAT).astype(BF16)
        return total + 0.1 * ratio(band + REACH) * jnp.sum(moved, axis=0)

    def band_copy(start, recv, index, to):
        return pltpu.make_async_remote_copy(
            src_ref=bands_16.at[pl.ds(start, REACH)],
            dst_ref=recv,
            send_sem=band_send.at[index],
            recv_sem=band_recv.at[index],
            device_id={"spec": to},
            device_id_type=MESH,
        )

    upward = band_copy(BANDS - REACH, low_halo, 0, lax.rem(spec + 1, specs))
    downward = band_copy(0, high_halo, 1, lax.rem(spec + specs - 1, specs))
    total = lax.fori_loop(0, REACH, advect_band, jnp.zeros((8, LAT), F32))

    @pl.when((spec > 0) & ~backward)
    def _():
        downward.start()

    @pl.when((spec < specs - 1) & backward)
    def _():
        upward.start()

    part[...] = lax.fori_loop(REACH, BANDS, advect_band, total)

    @pl.when((spec > 0) & backward)
    def _():
        downward.start()

    @pl.when((spec < specs - 1) & ~backward)
    def _():
        upward.start()

    sums = []
    for i in range(1, specs):
        sums.append(
            pltpu.make_async_remote_copy(
                src_ref=part,
                dst_ref=parts.at[i],
                send_sem=sum_send.at[i],
                recv_sem=sum_recv.at[i],
                device_id={"spec": lax.rem(spec + i, specs)},
                device_id_type=MESH,
            )
        )
    for copy in sums:
        copy.start()

    pl.semaphore_wait(near_sem, 4)
    for peer in z_peers:
        tell(ring_sem, {"grid": peer})

    for copy in n_lon:
        copy.start()

    chunk = 6

    def product(centre, upper, lower):
        return centre * (centre * (upper + lower) - 2.0 * upper * lower)

    def own_terms(here, at, band):
        terms = [product(here, at(odd, 2, (3 * s - 1) // 2), at(odd, -3, (-s - 1) // 2)) for s in (1, -1)]
        return (-2.0 * nonlin_coef * ratio(band + REACH)) * (terms[0] + terms[1])

    def below_terms(here, at, band):
        terms = [product(at(odd, -2, (-3 * s - 1) // 2), here, at(even, -5, -2 * s)) for s in (1, -1)]
        return (nonlin_coef * ratio(band + REACH - 2)) * (terms[0] + terms[1])

    def above_terms(here, at, band):
        terms = [product(at(odd, 3, (s - 1) // 2), at(even, 5, 2 * s), here) for s in (1, -1)]
        return (nonlin_coef * ratio(band + REACH + 3)) * (terms[0] + terms[1])

    def add_terms(begin, end, kinds, opening, damped):
        def step(band, carry):
            if damped:
                loss = ratio(band + REACH)
                inverse_loss = (1.0 / (1.0 + dissip_coef * loss * loss * damped[0]))[None]
            for piece in range(PAIRS // chunk):
                base = 2 + piece * chunk

                def at(ref, offset, turn):
                    return ref[band + REACH + offset, pl.ds(base + turn, chunk)]

                here = at(even, 0, 0)
                rows = pl.ds(pl.multiple_of(band * BAND_ROWS + piece * chunk * 8, 8), chunk * 8)
                if opening:
                    total = here * (1.0 + ratio(band + REACH) * gain[pl.ds(piece * chunk, chunk)])
                else:
                    total = g_buf[rows, :].reshape(chunk, 8, LAT)
                for kind in kinds:
                    total += kind(here, at, band)
                if damped:
                    total *= inverse_loss
                g_buf[rows, :] = total.reshape(chunk * 8, LAT)
            return carry

        lax.fori_loop(begin, end, step, 0)

    add_terms(0, 3, (above_terms,), True, ())
    add_terms(3, 4, (own_terms, above_terms), True, ())
    add_terms(4, 5, (own_terms,), True, ())
    add_terms(5, 7, (own_terms, below_terms), True, ())
    add_terms(7, 9, (below_terms,), True, ())

    for copy in sums:
        copy.wait_recv()
    whole = part[...] + parts[1] + parts[2] + parts[3]
    mean = (whole + pltpu.roll(whole, 4, axis=0)) * MEAN_SCALE

    @pl.when(spec < specs - 1)
    def _():
        downward.wait_recv()

    @pl.when(spec > 0)
    def _():
        upward.wait_recv()

    def halo_bands(band, carry):
        low = low_halo[band].astype(F32).reshape(pair_shape)
        keep(band, jnp.where(spec > 0, low, 0.0))
        high = high_halo[band].astype(F32).reshape(pair_shape)
        keep(band + BANDS + REACH, jnp.where(spec < specs - 1, high, 0.0))
        return carry

    lax.fori_loop(0, REACH, halo_bands, 0)

    def column_copy(start, rows, index):
        return pltpu.make_async_remote_copy(
            src_ref=col_send.at[pl.ds(start, rows)],
            dst_ref=col_recv.at[pl.ds(start, rows)],
            send_sem=col_ssem.at[index],
            recv_sem=col_rsem.at[index],
            device_id={"grid": west},
            device_id_type=MESH,
        )

    columns = [column_copy(0, FIRST_ROWS, 0), column_copy(FIRST_ROWS, EAST - FIRST_ROWS, 1)]
    g_buf[pl.ds(ROWS, WIDTH * LON - ROWS), :] = jnp.zeros((WIDTH * LON - ROWS, LAT), F32)
    col_recv[pl.ds(EAST, WIDTH - EAST), :] = jnp.zeros((WIDTH - EAST, LAT), BF16)
    add_terms(0, 3, (own_terms, below_terms), False, (mean,))
    add_terms(3, 4, (below_terms,), False, (mean,))
    col_send[pl.ds(0, FIRST_ROWS), :] = g_buf[pl.ds(0, FIRST_ROWS, stride=LON), :].astype(BF16)
    columns[0].start()
    pl.semaphore_wait(ring_sem, RING - 1)
    tell(half_sem, {"grid": x_peer})
    add_terms(4, 5, (below_terms, above_terms), False, (mean,))
    add_terms(5, 7, (above_terms,), False, (mean,))
    add_terms(7, 9, (own_terms, above_terms), False, (mean,))
    col_send[pl.ds(FIRST_ROWS, EAST - FIRST_ROWS), :] = g_buf[
        pl.ds(FIRST_ROWS * LON, EAST - FIRST_ROWS, stride=LON), :
    ].astype(BF16)
    columns[1].start()

    boundary = jnp.zeros((RIM, WIDTH), F32)
    for lon in range(LON):
        high, low = split_16(g_buf[pl.ds(lon, WIDTH, stride=LON), :])
        boundary += dot_nt(share_high[lon], high)
        boundary += dot_nt(share_high[lon], low)
        boundary += dot_nt(share_low[lon], high)
    for copy in columns:
        copy.wait_recv()
    boundary += dot_nt(share_high[LON], col_recv[...])
    boundary += dot_nt(share_low[LON], col_recv[...])
    boundary = jnp.concatenate([boundary[:, :256], boundary[:, 256:] + facts[...]], axis=1)
    packed = jnp.dot(hot[...], boundary.astype(BF16), preferred_element_type=F32)
    for c in range(3):
        lanes = packed[:, c * LAT : (c + 1) * LAT].astype(BF16)
        blocks[c] = lanes.reshape(count, 2, LAT)

    own_block = pltpu.make_async_copy(blocks.at[:, me], arrived.at[:, me], rim_recv)
    own_block.start()

    pl.semaphore_wait(half_sem, 1)
    for z, x, y in far_first():
        dest = place_of(
            turned_by(z_part, z, RING), 1 - x_part if x else x_part, turned_by(y_part, y, RING)
        )
        pltpu.make_async_remote_copy(
            src_ref=blocks.at[:, dest],
            dst_ref=arrived.at[:, me],
            send_sem=rim_send,
            recv_sem=rim_recv,
            device_id={"grid": dest},
            device_id_type=MESH,
        ).start()
    g_out[...] = g_buf[pl.ds(0, ROWS), :]
    quarter = count // 4
    lower_keep = jnp.where((me != quarter) & (me != 3 * quarter), 1.0, 0.0)
    upper_keep = jnp.where((me != quarter - 1) & (me != 3 * quarter - 1), 1.0, 0.0)
    for copy in n_lon:
        copy.wait_recv()
    unpack(n_recv, halo_n, lower_keep, upper_keep)

    def advect_nest(band, carry):
        block = rows_of(n_ref, band)
        lon_step, lat_step = upwind(block, rows_of(halo_n, band))
        speed = nest_speedup * speed_coef * inverse(band + REACH)
        along_x = jnp.abs(rows_of(cos_ref, 0))
        along_y = jnp.abs(rows_of(sin_ref, 0))
        moved = block - speed * (along_x * lon_step + along_y * lat_step)
        nest[pl.ds(pl.multiple_of(band * BAND_ROWS, 8), BAND_ROWS), :] = moved.reshape(BAND_ROWS, LAT)
        return carry

    lax.fori_loop(0, BANDS, advect_nest, 0)

    for copy in e_lon + n_lon + sums + columns:
        copy.wait_send()

    @pl.when(spec < specs - 1)
    def _():
        upward.wait_send()

    @pl.when(spec > 0)
    def _():
        downward.wait_send()

    others = blocks.at[:, pl.ds(0, count - 1)]
    pltpu.make_async_copy(others, others, rim_send).wait()
    pltpu.make_async_copy(arrived, arrived, rim_recv).wait()


def settle(arrived, nest, g_next, g_out, n_out, n_buf, out_sem):
    g_copy = pltpu.make_async_copy(g_next, g_out, out_sem.at[0])
    g_copy.start()
    spectra = jnp.concatenate(
        [arrived[c].reshape(2 * RIM, LAT).astype(F32) for c in range(3)], axis=1
    )
    told = spectra[:, 256:]
    cell = told[:, FACT : FACT + 1] * float(LAT) + told[:, FACT + 1 : FACT + 2]
    cells = lax.broadcasted_iota(jnp.int32, (2 * RIM, LON * LAT), 1).astype(F32)
    hit = cell == cells
    rate_high = jnp.where(hit, told[:, FACT + 2 : FACT + 3], 0.0)
    rate_low = jnp.where(hit, told[:, FACT + 3 : FACT + 4], 0.0)
    remains = 1.0 - jnp.sum(rate_high + rate_low, axis=0, keepdims=True)
    turned = spectra.T.astype(BF16)
    gained = jnp.dot(turned, rate_high.astype(BF16), preferred_element_type=F32)
    gained += jnp.dot(turned, rate_low.astype(BF16), preferred_element_type=F32)
    for lon in range(LON):
        lanes = slice(lon * LAT, (lon + 1) * LAT)
        held = nest[pl.ds(lon, BINS, stride=LON), :]
        n_buf[pl.ds(lon, BINS, stride=LON), :] = held * remains[:, lanes] + gained[:BINS, lanes]
    n_copy = pltpu.make_async_copy(n_buf, n_out, out_sem.at[1])
    n_copy.start()
    g_copy.wait()
    n_copy.wait()


def per_device(
    energy, nest_energy, ocean_mask, wind_field, rim_cell, rim_dest, rim_target, rim_weight
):
    count = lax.axis_size("grid")
    cosine, sine, secant, scalars = tables()
    vmem = pl.BlockSpec(memory_space=pltpu.VMEM)
    flat = jax.ShapeDtypeStruct((ROWS, LAT), F32)
    dma = pltpu.SemaphoreType.DMA

    def body(*refs):
        kernel(count, *refs)

    global_rows, nest_rows, arrived = pl.pallas_call(
        body,
        out_shape=(flat, flat, jax.ShapeDtypeStruct((3, count, 2, LAT), BF16)),
        in_specs=[pl.BlockSpec(memory_space=pltpu.HBM)] * 12,
        out_specs=(vmem, vmem, vmem),
        scratch_shapes=[
            pltpu.VMEM((ROWS, LAT), F32),
            pltpu.VMEM((ROWS, LAT), F32),
            pltpu.VMEM((LON, LAT), jnp.int32),
            pltpu.VMEM((2, LON, LAT), F32),
            pltpu.VMEM((2, RIM), jnp.int32),
            pltpu.VMEM((1, RIM), jnp.int32),
            pltpu.VMEM((1, RIM), jnp.int32),
            pltpu.VMEM((3, RIM), F32),
            pltpu.VMEM((BAND_ROWS, LAT), F32),
            pltpu.VMEM((BAND_ROWS, LAT), F32),
            pltpu.VMEM((8, LAT), F32),
            pltpu.SMEM((128,), F32),
            pltpu.VMEM((RIM, RIM), F32),
            pltpu.VMEM((PACKET, LAT), F32),
            pltpu.VMEM((PACKET, LAT), F32),
            pltpu.VMEM((2, PACKET, LAT), BF16),
            pltpu.VMEM((2, PACKET, LAT), BF16),
            pltpu.VMEM((2, PACKET, LAT), BF16),
            pltpu.VMEM((2, PACKET, LAT), BF16),
            pltpu.VMEM((ROWS, LAT), F32),
            pltpu.VMEM((ROWS, LAT), F32),
            pltpu.VMEM((BANDS + 2 * REACH, PAIRS + 4, 8, LAT), F32),
            pltpu.VMEM((BANDS + 2 * REACH, PAIRS + 4, 8, LAT), F32),
            pltpu.VMEM((BANDS, BAND_ROWS, LAT), BF16),
            pltpu.VMEM((REACH, BAND_ROWS, LAT), BF16),
            pltpu.VMEM((REACH, BAND_ROWS, LAT), BF16),
            pltpu.VMEM((PAIRS, 8, LAT), F32),
            pltpu.VMEM((WIDTH * LON, LAT), F32),
            pltpu.VMEM((8, LAT), F32),
            pltpu.VMEM((4, 8, LAT), F32),
            pltpu.VMEM((WIDTH, LAT), BF16),
            pltpu.VMEM((WIDTH, LAT), BF16),
            pltpu.VMEM((LON + 1, RIM, LAT), BF16),
            pltpu.VMEM((LON + 1, RIM, LAT), BF16),
            pltpu.VMEM((2 * RIM, RIM), BF16),
            pltpu.VMEM((RIM, LAT), F32),
            pltpu.VMEM((3, count, 2, LAT), BF16),
            dma((12,)),
            dma((4,)),
            dma((4,)),
            dma((2,)),
            dma((2,)),
            dma((4,)),
            dma((4,)),
            dma((2,)),
            dma((2,)),
            dma,
            dma,
            pltpu.SemaphoreType.REGULAR,
            pltpu.SemaphoreType.REGULAR,
            pltpu.SemaphoreType.REGULAR,
        ],
        compiler_params=pltpu.CompilerParams(
            collective_id=0, has_side_effects=True, vmem_limit_bytes=40 << 20
        ),
        name="wave_step",
    )(
        *(
            pltpu.with_memory_space_constraint(x, pltpu.HBM)
            for x in (
                energy.reshape(ROWS, LAT),
                nest_energy.reshape(ROWS, LAT),
                ocean_mask,
                wind_field,
                rim_cell.T,
                rim_dest.T,
                rim_target.reshape(1, RIM),
                rim_weight.T,
                jnp.asarray(cosine),
                jnp.asarray(sine),
                jnp.asarray(secant),
                jnp.asarray(scalars),
            )
        )
    )
    hbm = pl.BlockSpec(memory_space=pl.ANY)
    global_next, nest_next = pl.pallas_call(
        settle,
        out_shape=(flat, flat),
        in_specs=[vmem] * 3,
        out_specs=(hbm, hbm),
        scratch_shapes=[
            pltpu.VMEM((ROWS, LAT), F32),
            dma((2,)),
        ],
        compiler_params=pltpu.CompilerParams(vmem_limit_bytes=SETTLE_LIMIT),
        name="settle",
    )(arrived, nest_rows, global_rows)
    shape = energy.shape
    return (global_next.reshape(shape), nest_next.reshape(shape))


def solution(mesh):
    in_specs = (
        P("spec", None, "grid", None),
        P("spec", None, "grid", None),
        P("grid", None),
        P(None, "grid", None),
        P("grid", None),
        P("grid", None),
        P("grid"),
        P("grid", None),
    )
    out_specs = (P("spec", None, "grid", None), P("spec", None, "grid", None))
    return jax.shard_map(
        per_device, mesh=mesh, in_specs=in_specs, out_specs=out_specs, check_vma=False
    )
```

```python
import jax
import jax.numpy as jnp
import numpy as np
from jax import lax
from jax.experimental import pallas as pl
from jax.experimental.pallas import tpu as pltpu
from jax.sharding import PartitionSpec as P

FREQS = 36
ANGLES = 36
LON = 4
LAT = 128
RIM = 128
BANDS = 9
REACH = 5
BINS = BANDS * ANGLES
ROWS = BINS * LON
BAND_ROWS = ANGLES * LON
PAIRS = BAND_ROWS // 8
PACKET = 192
FIRST_ROWS = 144
EAST = 336
RING = 8
SETTLE_LIMIT = 16 << 20
WIDTH = 384
FACT = BINS - 256
MESH = pl.DeviceIdType.MESH
F32 = jnp.float32
BF16 = jnp.bfloat16

ratio_step = 1.1
speed_coef = 0.054
wind_coef = 0.05
dissip_coef = 0.2
nonlin_coef = 0.12
nest_speedup = 2.0


def tables():
    heading = 2.0 * np.pi * np.arange(ANGLES) / ANGLES
    cosine, sine = np.cos(heading), np.sin(heading)
    cosine[[9, 27]] = 0.0
    sine[[0, 18]] = 0.0

    def spread(x):
        rows = np.repeat(x, LON)
        return np.broadcast_to(rows[:, None], (BAND_ROWS, LAT)).astype(np.float32)

    degrees = -60.0 + 120.0 * (np.arange(LAT) + 0.5) / LAT
    secant = np.broadcast_to(1.0 / np.cos(degrees * np.pi / 180.0), (8, LAT)).astype(np.float32)
    bands = np.arange(-REACH, FREQS + REACH)
    ratio = ratio_step ** (bands - FREQS // 2).astype(np.float64)
    scalars = np.zeros((128,), np.float32)
    scalars[: 2 * ratio.size] = np.concatenate([ratio, 1.0 / ratio])
    return spread(cosine), spread(sine), secant, scalars


RATIO_COUNT = FREQS + 2 * REACH
MEAN_SCALE = float(
    1.0 / (ANGLES * 0.1 * np.sum(ratio_step ** (np.arange(FREQS) - FREQS // 2.0)))
)


def dot_nt(a, b):
    return lax.dot_general(a, b, (((1,), (1,)), ((), ())), preferred_element_type=F32)


def split_16(x):
    high = x.astype(BF16)
    return high, (x - high.astype(F32)).astype(BF16)


def far_first():
    def hops(step):
        z, x, y = step
        return min(z, RING - z) + 2 * x + min(y, RING - y)

    steps = [(z, x, y) for z in range(RING) for x in range(2) for y in range(RING)]
    return sorted(steps[1:], key=lambda step: -hops(step))


def kernel(
    count,
    e_hbm,
    n_hbm,
    mask_hbm,
    wind_hbm,
    cell_hbm,
    dest_hbm,
    target_hbm,
    weight_hbm,
    cos_hbm,
    sin_hbm,
    sec_hbm,
    scalar_hbm,
    g_out,
    nest,
    arrived,
    e_ref,
    n_ref,
    mask_ref,
    wind_ref,
    cell_ref,
    dest_ref,
    target_ref,
    weight_ref,
    cos_ref,
    sin_ref,
    sec_ref,
    scalar_ref,
    rim_rows,
    stage_a,
    stage_b,
    e_send,
    n_send,
    e_recv,
    n_recv,
    halo_e,
    halo_n,
    even,
    odd,
    bands_16,
    low_halo,
    high_halo,
    gain,
    g_buf,
    part,
    parts,
    col_send,
    col_recv,
    share_high,
    share_low,
    facts,
    blocks,
    in_sem,
    lon_send,
    lon_recv,
    band_send,
    band_recv,
    sum_send,
    sum_recv,
    col_ssem,
    col_rsem,
    rim_send,
    rim_recv,
    near_sem,
    ring_sem,
    half_sem,
):
    sources = (
        e_hbm, n_hbm, scalar_hbm, mask_hbm, cos_hbm, sin_hbm, sec_hbm, wind_hbm,
        cell_hbm, dest_hbm, target_hbm, weight_hbm,
    )
    places = (
        e_ref, n_ref, scalar_ref, mask_ref, cos_ref, sin_ref, sec_ref, wind_ref,
        cell_ref, dest_ref, target_ref, weight_ref,
    )
    loads = [
        pltpu.make_async_copy(source, place, in_sem.at[i])
        for i, (source, place) in enumerate(zip(sources, places))
    ]
    loads[0].start()
    loads[1].start()
    me = lax.axis_index("grid")
    spec = lax.axis_index("spec")
    specs = FREQS // BANDS
    first = spec * BANDS
    west = lax.rem(me + count - 1, count)
    east = lax.rem(me + 1, count)
    barrier = pltpu.get_barrier_semaphore()

    def ratio(band):
        return scalar_ref[first + band]

    def inverse(band):
        return scalar_ref[first + band + RATIO_COUNT]

    z_part = me // (2 * RING)
    x_part = lax.rem(me // RING, 2)
    y_part = lax.rem(me, RING)

    def place_of(z, x, y):
        return (z * 2 + x) * RING + y

    def turned_by(part, step, size):
        return lax.rem(part + step, size) if step else part

    def tell(sem, to):
        pl.semaphore_signal(sem, inc=1, device_id=to, device_id_type=MESH)

    tell(barrier, {"grid": west})
    tell(barrier, {"grid": east})
    for i in range(1, specs):
        tell(barrier, {"spec": lax.rem(spec + i, specs)})
    z_peers = [place_of(turned_by(z_part, i, RING), x_part, y_part) for i in range(1, RING)]
    x_peer = place_of(z_part, 1 - x_part, y_part)
    near = (1, RING - 1, 2, RING - 2)
    y_near = [place_of(z_part, x_part, turned_by(y_part, i, RING)) for i in near]
    z_near = [z_peers[i - 1] for i in near]
    for peer in y_near + z_near:
        tell(barrier, {"grid": peer})
    tell(barrier, {"grid": x_peer})
    for load in loads[2:]:
        load.start()

    packet_rows = lax.broadcasted_iota(jnp.int32, (PACKET, LAT), 0)
    angle = lax.rem(packet_rows, ANGLES)
    eastward = (angle < 10) | (angle >= 28)
    stage_a[...] = jnp.zeros_like(stage_a)
    stage_b[...] = jnp.zeros_like(stage_b)
    direct = 5 * ANGLES
    folded = BINS - direct

    def pack(source, send):
        for index, lon, picked in ((0, LON - 1, eastward), (1, 0, ~eastward)):
            stage_a[pl.ds(0, direct), :] = source[pl.ds(lon, direct, stride=LON), :]
            stage_b[pl.ds(18, folded), :] = source[pl.ds(direct * LON + lon, folded, stride=LON), :]
            send[index] = jnp.where(picked, stage_a[...], stage_b[...]).astype(BF16)

    loads[0].wait()
    pack(e_ref, e_send)
    pl.semaphore_wait(barrier, 2 + specs - 1 + 2 * len(near) + 1)

    def lon_copies(send, recv, base):
        return [
            pltpu.make_async_remote_copy(
                src_ref=send.at[index],
                dst_ref=recv.at[index],
                send_sem=lon_send.at[base + index],
                recv_sem=lon_recv.at[base + index],
                device_id={"grid": to},
                device_id_type=MESH,
            )
            for index, to in ((0, east), (1, west))
        ]

    e_lon = lon_copies(e_send, e_recv, 0)
    n_lon = lon_copies(n_send, n_recv, 2)
    for copy in e_lon:
        copy.start()
    for peer in y_near[2:] + z_near[2:]:
        tell(near_sem, {"grid": peer})
    for load in loads[2:]:
        load.wait()
    loads[1].wait()
    pack(n_ref, n_send)

    lane = lax.broadcasted_iota(jnp.int32, (RIM, LAT), 1)
    sub = lax.broadcasted_iota(jnp.int32, (RIM, LAT), 0)
    rim_rows[...] = jnp.zeros_like(rim_rows)
    rim_rows[pl.ds(0, 2), :] = cell_ref[...].astype(F32)
    rim_rows[pl.ds(2, 1), :] = dest_ref[...].astype(F32)
    rim_rows[pl.ds(3, 1), :] = target_ref[...].astype(F32)
    rim_rows[pl.ds(4, 3), :] = weight_ref[...]
    rim_cols = rim_rows[...].T
    local_col = rim_cols[:, 0:1].astype(jnp.int32) - me * LON
    row = rim_cols[:, 1:2].astype(jnp.int32)
    dest_col = rim_cols[:, 2:3]
    target_col = rim_cols[:, 3:4].astype(jnp.int32)
    ex = rim_cols[:, 4:5]
    ny = rim_cols[:, 5:6]
    relax = rim_cols[:, 6:7]
    row_share = jnp.where(lane == row, 1.0 - ny, jnp.where(lane == row + 1, ny, 0.0))
    shares = []
    for lon in range(LON + 1):
        col_share = jnp.where(
            local_col == lon, 1.0 - ex, jnp.where(local_col == lon - 1, ex, 0.0)
        )
        high, low = split_16(col_share * row_share)
        shares.append((high, low))
    dest_row = dest_ref[...].astype(F32)
    same = dest_col == dest_row
    slot_row = jnp.sum(jnp.where(same & (sub < lane), 1.0, 0.0), axis=0, keepdims=True)
    places = lax.broadcasted_iota(jnp.int32, (2 * RIM, LAT), 0)
    named = (dest_row == (places >> 1).astype(F32)) & (slot_row == (places & 1).astype(F32))
    hot = jnp.where(named, 1.0, 0.0).astype(BF16)
    relax_high = relax.astype(BF16).astype(F32)
    fact = jnp.where(lane == FACT, (target_col >> 7).astype(F32), 0.0)
    fact = jnp.where(lane == FACT + 1, (target_col & 127).astype(F32), fact)
    fact = jnp.where(lane == FACT + 2, relax_high, fact)
    fact = jnp.where(lane == FACT + 3, relax - relax_high, fact)
    facts[...] = jnp.dot(hot, fact.astype(BF16), preferred_element_type=F32)
    for lon, (high, low) in enumerate(shares):
        share_high[lon] = jnp.dot(hot, high, preferred_element_type=F32).astype(BF16)
        share_low[lon] = jnp.dot(hot, low, preferred_element_type=F32).astype(BF16)
    pair_shape = (PAIRS, 8, LAT)
    cosine = cos_ref[...].reshape(pair_shape)
    sine = sin_ref[...].reshape(pair_shape)
    wind = wind_ref[...]
    wind_x = jnp.concatenate([wind[0], wind[0]], axis=0)[None]
    wind_y = jnp.concatenate([wind[1], wind[1]], axis=0)[None]
    gain[...] = wind_coef * jnp.maximum(wind_x * cosine + wind_y * sine, 0.0)
    mask_half = mask_ref[...].astype(F32)
    mask = jnp.concatenate([mask_half, mask_half], axis=0)[None]
    secant = sec_ref[...][None]

    vreg_sub = lax.broadcasted_iota(jnp.int32, (1, 8, LAT), 1)
    vreg_lane = lax.broadcasted_iota(jnp.int32, (1, 8, LAT), 2)
    lon_of = vreg_sub & 3

    def upwind(block, halo):
        before = jnp.where(lon_of == 0, halo, pltpu.roll(block, 1, axis=1))
        after = jnp.where(lon_of == LON - 1, halo, pltpu.roll(block, 7, axis=1))
        along_lon = jnp.concatenate([before[:5], after[5:14], before[14:]], axis=0)
        south = jnp.where(vreg_lane == 0, 0.0, pltpu.roll(block, 1, axis=2))
        north = jnp.where(vreg_lane == LAT - 1, 0.0, pltpu.roll(block, LAT - 1, axis=2))
        along_lat = jnp.concatenate([south[:9], north[9:]], axis=0)
        return block - along_lon, block - along_lat

    def rows_of(ref, band):
        return ref[pl.ds(pl.multiple_of(band * BAND_ROWS, 8), BAND_ROWS), :].reshape(pair_shape)

    def cyclic(ref, band, value):
        ref[band, pl.ds(2, PAIRS)] = value
        ref[band, pl.ds(0, 2)] = value[PAIRS - 2 :]
        ref[band, pl.ds(PAIRS + 2, 2)] = value[:2]

    def keep(band, value):
        cyclic(even, band, value)
        turned = pltpu.roll(value, 4, axis=1)
        following = jnp.concatenate([turned[1:], turned[:1]], axis=0)
        cyclic(odd, band, jnp.where(vreg_sub < 4, turned, following))

    def unpack(recv, halo, lower, upper):
        for index, lon, factor in ((0, 0, lower), (1, LON - 1, upper)):
            stage_a[...] = recv[index].astype(F32)
            front = stage_a[pl.ds(0, direct), :]
            rest = stage_a[pl.ds(18, folded), :]
            if factor is not None:
                front, rest = front * factor, rest * factor
            halo[pl.ds(lon, direct, stride=LON), :] = front
            halo[pl.ds(direct * LON + lon, folded, stride=LON), :] = rest

    for copy in e_lon:
        copy.wait_recv()
    unpack(e_recv, halo_e, None, None)
    pl.semaphore_wait(near_sem, 4)
    for peer in z_peers:
        tell(ring_sem, {"grid": peer})

    backward = lax.rem(spec, 2) == 1

    def advect_band(index, total):
        band = jnp.where(backward, BANDS - 1 - index, index)
        block = rows_of(e_ref, band)
        lon_step, lat_step = upwind(block, rows_of(halo_e, band))
        speed = speed_coef * inverse(band + REACH)
        along_x = jnp.abs(rows_of(cos_ref, 0)) * secant
        along_y = jnp.abs(rows_of(sin_ref, 0))
        moved = (block - speed * (along_x * lon_step + along_y * lat_step)) * mask
        keep(band + REACH, moved)
        bands_16[band] = moved.reshape(BAND_ROWS, LAT).astype(BF16)
        return total + 0.1 * ratio(band + REACH) * jnp.sum(moved, axis=0)

    def band_copy(start, recv, index, to):
        return pltpu.make_async_remote_copy(
            src_ref=bands_16.at[pl.ds(start, REACH)],
            dst_ref=recv,
            send_sem=band_send.at[index],
            recv_sem=band_recv.at[index],
            device_id={"spec": to},
            device_id_type=MESH,
        )

    upward = band_copy(BANDS - REACH, low_halo, 0, lax.rem(spec + 1, specs))
    downward = band_copy(0, high_halo, 1, lax.rem(spec + specs - 1, specs))
    total = lax.fori_loop(0, REACH, advect_band, jnp.zeros((8, LAT), F32))

    @pl.when((spec > 0) & ~backward)
    def _():
        downward.start()

    @pl.when((spec < specs - 1) & backward)
    def _():
        upward.start()

    part[...] = lax.fori_loop(REACH, BANDS, advect_band, total)

    @pl.when((spec > 0) & backward)
    def _():
        downward.start()

    @pl.when((spec < specs - 1) & ~backward)
    def _():
        upward.start()

    sums = []
    for i in range(1, specs):
        sums.append(
            pltpu.make_async_remote_copy(
                src_ref=part,
                dst_ref=parts.at[i],
                send_sem=sum_send.at[i],
                recv_sem=sum_recv.at[i],
                device_id={"spec": lax.rem(spec + i, specs)},
                device_id_type=MESH,
            )
        )
    for copy in sums:
        copy.start()


    for copy in n_lon:
        copy.start()

    chunk = 6

    def product(centre, upper, lower):
        return centre * (centre * (upper + lower) - 2.0 * upper * lower)

    def own_terms(here, at, band):
        terms = [product(here, at(odd, 2, (3 * s - 1) // 2), at(odd, -3, (-s - 1) // 2)) for s in (1, -1)]
        return (-2.0 * nonlin_coef * ratio(band + REACH)) * (terms[0] + terms[1])

    def below_terms(here, at, band):
        terms = [product(at(odd, -2, (-3 * s - 1) // 2), here, at(even, -5, -2 * s)) for s in (1, -1)]
        return (nonlin_coef * ratio(band + REACH - 2)) * (terms[0] + terms[1])

    def above_terms(here, at, band):
        terms = [product(at(odd, 3, (s - 1) // 2), at(even, 5, 2 * s), here) for s in (1, -1)]
        return (nonlin_coef * ratio(band + REACH + 3)) * (terms[0] + terms[1])

    def add_terms(begin, end, kinds, opening, damped):
        def step(band, carry):
            if damped:
                loss = ratio(band + REACH)
                inverse_loss = (1.0 / (1.0 + dissip_coef * loss * loss * damped[0]))[None]
            for piece in range(PAIRS // chunk):
                base = 2 + piece * chunk

                def at(ref, offset, turn):
                    return ref[band + REACH + offset, pl.ds(base + turn, chunk)]

                here = at(even, 0, 0)
                rows = pl.ds(pl.multiple_of(band * BAND_ROWS + piece * chunk * 8, 8), chunk * 8)
                if opening:
                    total = here * (1.0 + ratio(band + REACH) * gain[pl.ds(piece * chunk, chunk)])
                else:
                    total = g_buf[rows, :].reshape(chunk, 8, LAT)
                for kind in kinds:
                    total += kind(here, at, band)
                if damped:
                    total *= inverse_loss
                g_buf[rows, :] = total.reshape(chunk * 8, LAT)
            return carry

        lax.fori_loop(begin, end, step, 0)

    add_terms(0, 3, (above_terms,), True, ())
    add_terms(3, 4, (own_terms, above_terms), True, ())
    add_terms(4, 5, (own_terms,), True, ())
    add_terms(5, 7, (own_terms, below_terms), True, ())
    add_terms(7, 9, (below_terms,), True, ())

    for copy in sums:
        copy.wait_recv()
    whole = part[...] + parts[1] + parts[2] + parts[3]
    mean = (whole + pltpu.roll(whole, 4, axis=0)) * MEAN_SCALE

    @pl.when(spec < specs - 1)
    def _():
        downward.wait_recv()

    @pl.when(spec > 0)
    def _():
        upward.wait_recv()

    def halo_bands(band, carry):
        low = low_halo[band].astype(F32).reshape(pair_shape)
        keep(band, jnp.where(spec > 0, low, 0.0))
        high = high_halo[band].astype(F32).reshape(pair_shape)
        keep(band + BANDS + REACH, jnp.where(spec < specs - 1, high, 0.0))
        return carry

    lax.fori_loop(0, REACH, halo_bands, 0)

    def column_copy(start, rows, index):
        return pltpu.make_async_remote_copy(
            src_ref=col_send.at[pl.ds(start, rows)],
            dst_ref=col_recv.at[pl.ds(start, rows)],
            send_sem=col_ssem.at[index],
            recv_sem=col_rsem.at[index],
            device_id={"grid": west},
            device_id_type=MESH,
        )

    columns = [column_copy(0, FIRST_ROWS, 0), column_copy(FIRST_ROWS, EAST - FIRST_ROWS, 1)]
    g_buf[pl.ds(ROWS, WIDTH * LON - ROWS), :] = jnp.zeros((WIDTH * LON - ROWS, LAT), F32)
    col_recv[pl.ds(EAST, WIDTH - EAST), :] = jnp.zeros((WIDTH - EAST, LAT), BF16)
    add_terms(0, 3, (own_terms, below_terms), False, (mean,))
    add_terms(3, 4, (below_terms,), False, (mean,))
    col_send[pl.ds(0, FIRST_ROWS), :] = g_buf[pl.ds(0, FIRST_ROWS, stride=LON), :].astype(BF16)
    columns[0].start()
    add_terms(4, 5, (below_terms, above_terms), False, (mean,))
    add_terms(5, 7, (above_terms,), False, (mean,))
    add_terms(7, 9, (own_terms, above_terms), False, (mean,))
    col_send[pl.ds(FIRST_ROWS, EAST - FIRST_ROWS), :] = g_buf[
        pl.ds(FIRST_ROWS * LON, EAST - FIRST_ROWS, stride=LON), :
    ].astype(BF16)
    columns[1].start()
    pl.semaphore_wait(ring_sem, RING - 1)
    tell(half_sem, {"grid": x_peer})

    packed = jnp.zeros((2 * RIM, WIDTH), F32)
    for lon in range(LON):
        high, low = split_16(g_buf[pl.ds(lon, WIDTH, stride=LON), :])
        packed += dot_nt(share_high[lon], high)
        packed += dot_nt(share_high[lon], low)
        packed += dot_nt(share_low[lon], high)
    for copy in columns:
        copy.wait_recv()
    packed += dot_nt(share_high[LON], col_recv[...])
    packed += dot_nt(share_low[LON], col_recv[...])
    for c in range(3):
        lanes = packed[:, c * LAT : (c + 1) * LAT]
        if c == 2:
            lanes += facts[...]
        lanes = lanes.astype(BF16)
        blocks[c] = lanes.reshape(count, 2, LAT)

    own_block = pltpu.make_async_copy(blocks.at[:, me], arrived.at[:, me], rim_recv)
    own_block.start()

    pl.semaphore_wait(half_sem, 1)
    for z, x, y in far_first():
        dest = place_of(
            turned_by(z_part, z, RING), 1 - x_part if x else x_part, turned_by(y_part, y, RING)
        )
        pltpu.make_async_remote_copy(
            src_ref=blocks.at[:, dest],
            dst_ref=arrived.at[:, me],
            send_sem=rim_send,
            recv_sem=rim_recv,
            device_id={"grid": dest},
            device_id_type=MESH,
        ).start()
    g_out[...] = g_buf[pl.ds(0, ROWS), :]
    quarter = count // 4
    lower_keep = jnp.where((me != quarter) & (me != 3 * quarter), 1.0, 0.0)
    upper_keep = jnp.where((me != quarter - 1) & (me != 3 * quarter - 1), 1.0, 0.0)
    for copy in n_lon:
        copy.wait_recv()
    unpack(n_recv, halo_n, lower_keep, upper_keep)

    def advect_nest(band, carry):
        block = rows_of(n_ref, band)
        lon_step, lat_step = upwind(block, rows_of(halo_n, band))
        speed = nest_speedup * speed_coef * inverse(band + REACH)
        along_x = jnp.abs(rows_of(cos_ref, 0))
        along_y = jnp.abs(rows_of(sin_ref, 0))
        moved = block - speed * (along_x * lon_step + along_y * lat_step)
        nest[pl.ds(pl.multiple_of(band * BAND_ROWS, 8), BAND_ROWS), :] = moved.reshape(BAND_ROWS, LAT)
        return carry

    lax.fori_loop(0, BANDS, advect_nest, 0)

    for copy in e_lon + n_lon + sums + columns:
        copy.wait_send()

    @pl.when(spec < specs - 1)
    def _():
        upward.wait_send()

    @pl.when(spec > 0)
    def _():
        downward.wait_send()

    others = blocks.at[:, pl.ds(0, count - 1)]
    pltpu.make_async_copy(others, others, rim_send).wait()
    pltpu.make_async_copy(arrived, arrived, rim_recv).wait()


def settle(arrived, nest, g_next, g_out, n_out, n_buf, out_sem):
    g_copy = pltpu.make_async_copy(g_next, g_out, out_sem.at[0])
    g_copy.start()
    spectra = jnp.concatenate([arrived[c].reshape(2 * RIM, LAT) for c in range(3)], axis=1)
    told = spectra[:, 256:].astype(F32)
    cell = told[:, FACT : FACT + 1] * float(LAT) + told[:, FACT + 1 : FACT + 2]
    cells = lax.broadcasted_iota(jnp.int32, (2 * RIM, LON * LAT), 1).astype(F32)
    hit = cell == cells
    rate_high = jnp.where(hit, told[:, FACT + 2 : FACT + 3], 0.0)
    rate_low = jnp.where(hit, told[:, FACT + 3 : FACT + 4], 0.0)
    remains = 1.0 - jnp.sum(rate_high + rate_low, axis=0, keepdims=True)
    turned = spectra.T
    gained = jnp.dot(turned, rate_high.astype(BF16), preferred_element_type=F32)
    gained += jnp.dot(turned, rate_low.astype(BF16), preferred_element_type=F32)
    for lon in range(LON):
        lanes = slice(lon * LAT, (lon + 1) * LAT)
        held = nest[pl.ds(lon, BINS, stride=LON), :]
        n_buf[pl.ds(lon, BINS, stride=LON), :] = held * remains[:, lanes] + gained[:BINS, lanes]
    n_copy = pltpu.make_async_copy(n_buf, n_out, out_sem.at[1])
    n_copy.start()
    g_copy.wait()
    n_copy.wait()


def per_device(
    energy, nest_energy, ocean_mask, wind_field, rim_cell, rim_dest, rim_target, rim_weight
):
    count = lax.axis_size("grid")
    cosine, sine, secant, scalars = tables()
    vmem = pl.BlockSpec(memory_space=pltpu.VMEM)
    flat = jax.ShapeDtypeStruct((ROWS, LAT), F32)
    dma = pltpu.SemaphoreType.DMA

    def body(*refs):
        kernel(count, *refs)

    global_rows, nest_rows, arrived = pl.pallas_call(
        body,
        out_shape=(flat, flat, jax.ShapeDtypeStruct((3, count, 2, LAT), BF16)),
        in_specs=[pl.BlockSpec(memory_space=pltpu.HBM)] * 12,
        out_specs=(vmem, vmem, vmem),
        scratch_shapes=[
            pltpu.VMEM((ROWS, LAT), F32),
            pltpu.VMEM((ROWS, LAT), F32),
            pltpu.VMEM((LON, LAT), jnp.int32),
            pltpu.VMEM((2, LON, LAT), F32),
            pltpu.VMEM((2, RIM), jnp.int32),
            pltpu.VMEM((1, RIM), jnp.int32),
            pltpu.VMEM((1, RIM), jnp.int32),
            pltpu.VMEM((3, RIM), F32),
            pltpu.VMEM((BAND_ROWS, LAT), F32),
            pltpu.VMEM((BAND_ROWS, LAT), F32),
            pltpu.VMEM((8, LAT), F32),
            pltpu.SMEM((128,), F32),
            pltpu.VMEM((RIM, RIM), F32),
            pltpu.VMEM((PACKET, LAT), F32),
            pltpu.VMEM((PACKET, LAT), F32),
            pltpu.VMEM((2, PACKET, LAT), BF16),
            pltpu.VMEM((2, PACKET, LAT), BF16),
            pltpu.VMEM((2, PACKET, LAT), BF16),
            pltpu.VMEM((2, PACKET, LAT), BF16),
            pltpu.VMEM((ROWS, LAT), F32),
            pltpu.VMEM((ROWS, LAT), F32),
            pltpu.VMEM((BANDS + 2 * REACH, PAIRS + 4, 8, LAT), F32),
            pltpu.VMEM((BANDS + 2 * REACH, PAIRS + 4, 8, LAT), F32),
            pltpu.VMEM((BANDS, BAND_ROWS, LAT), BF16),
            pltpu.VMEM((REACH, BAND_ROWS, LAT), BF16),
            pltpu.VMEM((REACH, BAND_ROWS, LAT), BF16),
            pltpu.VMEM((PAIRS, 8, LAT), F32),
            pltpu.VMEM((WIDTH * LON, LAT), F32),
            pltpu.VMEM((8, LAT), F32),
            pltpu.VMEM((4, 8, LAT), F32),
            pltpu.VMEM((WIDTH, LAT), BF16),
            pltpu.VMEM((WIDTH, LAT), BF16),
            pltpu.VMEM((LON + 1, 2 * RIM, LAT), BF16),
            pltpu.VMEM((LON + 1, 2 * RIM, LAT), BF16),
            pltpu.VMEM((2 * RIM, LAT), F32),
            pltpu.VMEM((3, count, 2, LAT), BF16),
            dma((12,)),
            dma((4,)),
            dma((4,)),
            dma((2,)),
            dma((2,)),
            dma((4,)),
            dma((4,)),
            dma((2,)),
            dma((2,)),
            dma,
            dma,
            pltpu.SemaphoreType.REGULAR,
            pltpu.SemaphoreType.REGULAR,
            pltpu.SemaphoreType.REGULAR,
        ],
        compiler_params=pltpu.CompilerParams(
            collective_id=0, has_side_effects=True, vmem_limit_bytes=40 << 20
        ),
        name="wave_step",
    )(
        *(
            pltpu.with_memory_space_constraint(x, pltpu.HBM)
            for x in (
                energy.reshape(ROWS, LAT),
                nest_energy.reshape(ROWS, LAT),
                ocean_mask,
                wind_field,
                rim_cell.T,
                rim_dest.T,
                rim_target.reshape(1, RIM),
                rim_weight.T,
                jnp.asarray(cosine),
                jnp.asarray(sine),
                jnp.asarray(secant),
                jnp.asarray(scalars),
            )
        )
    )
    hbm = pl.BlockSpec(memory_space=pl.ANY)
    global_next, nest_next = pl.pallas_call(
        settle,
        out_shape=(flat, flat),
        in_specs=[vmem] * 3,
        out_specs=(hbm, hbm),
        scratch_shapes=[
            pltpu.VMEM((ROWS, LAT), F32),
            dma((2,)),
        ],
        compiler_params=pltpu.CompilerParams(vmem_limit_bytes=SETTLE_LIMIT),
        name="settle",
    )(arrived, nest_rows, global_rows)
    shape = energy.shape
    return (global_next.reshape(shape), nest_next.reshape(shape))


def solution(mesh):
    in_specs = (
        P("spec", None, "grid", None),
        P("spec", None, "grid", None),
        P("grid", None),
        P(None, "grid", None),
        P("grid", None),
        P("grid", None),
        P("grid"),
        P("grid", None),
    )
    out_specs = (P("spec", None, "grid", None), P("spec", None, "grid", None))
    return jax.shard_map(
        per_device, mesh=mesh, in_specs=in_specs, out_specs=out_specs, check_vma=False
    )
```

```python
import jax
import jax.numpy as jnp
import numpy as np
from jax import lax
from jax.experimental import pallas as pl
from jax.experimental.pallas import tpu as pltpu
from jax.sharding import PartitionSpec as P

FREQS = 36
ANGLES = 36
LON = 4
LAT = 128
RIM = 128
BANDS = 9
REACH = 5
BINS = BANDS * ANGLES
ROWS = BINS * LON
BAND_ROWS = ANGLES * LON
PAIRS = BAND_ROWS // 8
PACKET = 192
FIRST_ROWS = 144
EAST = 336
RING = 8
SETTLE_LIMIT = 16 << 20
WIDTH = 384
ROOM = 8 * -(-BINS // 8) * LON
FACT = BINS - 256
MESH = pl.DeviceIdType.MESH
F32 = jnp.float32
BF16 = jnp.bfloat16

ratio_step = 1.1
speed_coef = 0.054
wind_coef = 0.05
dissip_coef = 0.2
nonlin_coef = 0.12
nest_speedup = 2.0


def tables():
    heading = 2.0 * np.pi * np.arange(ANGLES) / ANGLES
    cosine, sine = np.cos(heading), np.sin(heading)
    cosine[[9, 27]] = 0.0
    sine[[0, 18]] = 0.0

    def spread(x):
        rows = np.repeat(x, LON)
        return np.broadcast_to(rows[:, None], (BAND_ROWS, LAT)).astype(np.float32)

    degrees = -60.0 + 120.0 * (np.arange(LAT) + 0.5) / LAT
    secant = np.broadcast_to(1.0 / np.cos(degrees * np.pi / 180.0), (8, LAT)).astype(np.float32)
    bands = np.arange(-REACH, FREQS + REACH)
    ratio = ratio_step ** (bands - FREQS // 2).astype(np.float64)
    scalars = np.zeros((128,), np.float32)
    scalars[: 2 * ratio.size] = np.concatenate([ratio, 1.0 / ratio])
    return spread(cosine), spread(sine), secant, scalars


RATIO_COUNT = FREQS + 2 * REACH
MEAN_SCALE = float(
    1.0 / (ANGLES * 0.1 * np.sum(ratio_step ** (np.arange(FREQS) - FREQS // 2.0)))
)


def dot_nt(a, b):
    return lax.dot_general(a, b, (((1,), (1,)), ((), ())), preferred_element_type=F32)


def split_16(x):
    high = x.astype(BF16)
    return high, (x - high.astype(F32)).astype(BF16)


def far_first():
    def hops(step):
        z, x, y = step
        return min(z, RING - z) + 2 * x + min(y, RING - y)

    steps = [(z, x, y) for z in range(RING) for x in range(2) for y in range(RING)]
    return sorted(steps[1:], key=lambda step: -hops(step))


def kernel(
    count,
    e_hbm,
    n_hbm,
    mask_hbm,
    wind_hbm,
    cell_hbm,
    dest_hbm,
    target_hbm,
    weight_hbm,
    cos_hbm,
    sin_hbm,
    sec_hbm,
    scalar_hbm,
    g_out,
    nest,
    arrived,
    e_ref,
    n_ref,
    mask_ref,
    wind_ref,
    cell_ref,
    dest_ref,
    target_ref,
    weight_ref,
    cos_ref,
    sin_ref,
    sec_ref,
    scalar_ref,
    rim_rows,
    stage_a,
    stage_b,
    e_send,
    n_send,
    e_recv,
    n_recv,
    halo_e,
    halo_n,
    even,
    odd,
    bands_16,
    low_halo,
    high_halo,
    gain,
    g_buf,
    part,
    parts,
    col_send,
    col_recv,
    share_high,
    share_low,
    facts,
    blocks,
    in_sem,
    lon_send,
    lon_recv,
    band_send,
    band_recv,
    sum_send,
    sum_recv,
    col_ssem,
    col_rsem,
    rim_send,
    rim_recv,
    near_sem,
    ring_sem,
    half_sem,
):
    sources = (
        e_hbm, n_hbm, scalar_hbm, mask_hbm, cos_hbm, sin_hbm, sec_hbm, wind_hbm,
        cell_hbm, dest_hbm, target_hbm, weight_hbm,
    )
    places = (
        e_ref, n_ref, scalar_ref, mask_ref, cos_ref, sin_ref, sec_ref, wind_ref,
        cell_ref, dest_ref, target_ref, weight_ref,
    )
    loads = [
        pltpu.make_async_copy(source, place, in_sem.at[i])
        for i, (source, place) in enumerate(zip(sources, places))
    ]
    loads[0].start()
    loads[1].start()
    me = lax.axis_index("grid")
    spec = lax.axis_index("spec")
    specs = FREQS // BANDS
    first = spec * BANDS
    west = lax.rem(me + count - 1, count)
    east = lax.rem(me + 1, count)
    barrier = pltpu.get_barrier_semaphore()

    def ratio(band):
        return scalar_ref[first + band]

    def inverse(band):
        return scalar_ref[first + band + RATIO_COUNT]

    z_part = me // (2 * RING)
    x_part = lax.rem(me // RING, 2)
    y_part = lax.rem(me, RING)

    def place_of(z, x, y):
        return (z * 2 + x) * RING + y

    def turned_by(part, step, size):
        return lax.rem(part + step, size) if step else part

    def tell(sem, to):
        pl.semaphore_signal(sem, inc=1, device_id=to, device_id_type=MESH)

    tell(barrier, {"grid": west})
    tell(barrier, {"grid": east})
    for i in range(1, specs):
        tell(barrier, {"spec": lax.rem(spec + i, specs)})
    z_peers = [place_of(turned_by(z_part, i, RING), x_part, y_part) for i in range(1, RING)]
    x_peer = place_of(z_part, 1 - x_part, y_part)
    near = (1, RING - 1, 2, RING - 2)
    y_near = [place_of(z_part, x_part, turned_by(y_part, i, RING)) for i in near]
    z_near = [z_peers[i - 1] for i in near]
    for peer in y_near + z_near:
        tell(barrier, {"grid": peer})
    tell(barrier, {"grid": x_peer})
    for load in loads[2:]:
        load.start()

    packet_rows = lax.broadcasted_iota(jnp.int32, (PACKET, LAT), 0)
    angle = lax.rem(packet_rows, ANGLES)
    eastward = (angle < 10) | (angle >= 28)
    stage_a[...] = jnp.zeros_like(stage_a)
    stage_b[...] = jnp.zeros_like(stage_b)
    direct = 5 * ANGLES
    folded = BINS - direct

    def pack(source, send):
        for index, lon, picked in ((0, LON - 1, eastward), (1, 0, ~eastward)):
            stage_a[pl.ds(0, direct), :] = source[pl.ds(lon, direct, stride=LON), :]
            stage_b[pl.ds(18, folded), :] = source[pl.ds(direct * LON + lon, folded, stride=LON), :]
            send[index] = jnp.where(picked, stage_a[...], stage_b[...]).astype(BF16)

    loads[0].wait()
    pack(e_ref, e_send)
    pl.semaphore_wait(barrier, 2 + specs - 1 + 2 * len(near) + 1)

    def lon_copies(send, recv, base):
        return [
            pltpu.make_async_remote_copy(
                src_ref=send.at[index],
                dst_ref=recv.at[index],
                send_sem=lon_send.at[base + index],
                recv_sem=lon_recv.at[base + index],
                device_id={"grid": to},
                device_id_type=MESH,
            )
            for index, to in ((0, east), (1, west))
        ]

    e_lon = lon_copies(e_send, e_recv, 0)
    n_lon = lon_copies(n_send, n_recv, 2)
    for copy in e_lon:
        copy.start()
    for peer in y_near[2:] + z_near[2:]:
        tell(near_sem, {"grid": peer})
    for load in loads[2:]:
        load.wait()
    loads[1].wait()
    pack(n_ref, n_send)

    lane = lax.broadcasted_iota(jnp.int32, (RIM, LAT), 1)
    sub = lax.broadcasted_iota(jnp.int32, (RIM, LAT), 0)
    rim_rows[...] = jnp.zeros_like(rim_rows)
    rim_rows[pl.ds(0, 2), :] = cell_ref[...].astype(F32)
    rim_rows[pl.ds(2, 1), :] = dest_ref[...].astype(F32)
    rim_rows[pl.ds(3, 1), :] = target_ref[...].astype(F32)
    rim_rows[pl.ds(4, 3), :] = weight_ref[...]
    rim_cols = rim_rows[...].T
    local_col = rim_cols[:, 0:1].astype(jnp.int32) - me * LON
    row = rim_cols[:, 1:2].astype(jnp.int32)
    dest_col = rim_cols[:, 2:3]
    target_col = rim_cols[:, 3:4].astype(jnp.int32)
    ex = rim_cols[:, 4:5]
    ny = rim_cols[:, 5:6]
    relax = rim_cols[:, 6:7]
    row_share = jnp.where(lane == row, 1.0 - ny, jnp.where(lane == row + 1, ny, 0.0))
    shares = []
    for lon in range(LON + 1):
        col_share = jnp.where(
            local_col == lon, 1.0 - ex, jnp.where(local_col == lon - 1, ex, 0.0)
        )
        high, low = split_16(col_share * row_share)
        shares.append((high, low))
    dest_row = dest_ref[...].astype(F32)
    same = dest_col == dest_row
    slot_row = jnp.sum(jnp.where(same & (sub < lane), 1.0, 0.0), axis=0, keepdims=True)
    places = lax.broadcasted_iota(jnp.int32, (2 * RIM, LAT), 0)
    named = (dest_row == (places >> 1).astype(F32)) & (slot_row == (places & 1).astype(F32))
    hot = jnp.where(named, 1.0, 0.0).astype(BF16)
    relax_high = relax.astype(BF16).astype(F32)
    fact = jnp.where(lane == FACT, (target_col >> 7).astype(F32), 0.0)
    fact = jnp.where(lane == FACT + 1, (target_col & 127).astype(F32), fact)
    fact = jnp.where(lane == FACT + 2, relax_high, fact)
    fact = jnp.where(lane == FACT + 3, relax - relax_high, fact)
    facts[...] = jnp.dot(hot, fact.astype(BF16), preferred_element_type=F32)
    for lon, (high, low) in enumerate(shares):
        share_high[lon] = jnp.dot(hot, high, preferred_element_type=F32).astype(BF16)
        share_low[lon] = jnp.dot(hot, low, preferred_element_type=F32).astype(BF16)
    pair_shape = (PAIRS, 8, LAT)
    cosine = cos_ref[...].reshape(pair_shape)
    sine = sin_ref[...].reshape(pair_shape)
    wind = wind_ref[...]
    wind_x = jnp.concatenate([wind[0], wind[0]], axis=0)[None]
    wind_y = jnp.concatenate([wind[1], wind[1]], axis=0)[None]
    gain[...] = wind_coef * jnp.maximum(wind_x * cosine + wind_y * sine, 0.0)
    mask_half = mask_ref[...].astype(F32)
    mask = jnp.concatenate([mask_half, mask_half], axis=0)[None]
    secant = sec_ref[...][None]

    vreg_sub = lax.broadcasted_iota(jnp.int32, (1, 8, LAT), 1)
    vreg_lane = lax.broadcasted_iota(jnp.int32, (1, 8, LAT), 2)
    lon_of = vreg_sub & 3

    def upwind(block, halo):
        before = jnp.where(lon_of == 0, halo, pltpu.roll(block, 1, axis=1))
        after = jnp.where(lon_of == LON - 1, halo, pltpu.roll(block, 7, axis=1))
        along_lon = jnp.concatenate([before[:5], after[5:14], before[14:]], axis=0)
        south = jnp.where(vreg_lane == 0, 0.0, pltpu.roll(block, 1, axis=2))
        north = jnp.where(vreg_lane == LAT - 1, 0.0, pltpu.roll(block, LAT - 1, axis=2))
        along_lat = jnp.concatenate([south[:9], north[9:]], axis=0)
        return block - along_lon, block - along_lat

    def rows_of(ref, band):
        return ref[pl.ds(pl.multiple_of(band * BAND_ROWS, 8), BAND_ROWS), :].reshape(pair_shape)

    def cyclic(ref, band, value):
        ref[band, pl.ds(2, PAIRS)] = value
        ref[band, pl.ds(0, 2)] = value[PAIRS - 2 :]
        ref[band, pl.ds(PAIRS + 2, 2)] = value[:2]

    def keep(band, value):
        cyclic(even, band, value)
        turned = pltpu.roll(value, 4, axis=1)
        following = jnp.concatenate([turned[1:], turned[:1]], axis=0)
        cyclic(odd, band, jnp.where(vreg_sub < 4, turned, following))

    def unpack(recv, halo, lower, upper):
        for index, lon, factor in ((0, 0, lower), (1, LON - 1, upper)):
            stage_a[...] = recv[index].astype(F32)
            front = stage_a[pl.ds(0, direct), :]
            rest = stage_a[pl.ds(18, folded), :]
            if factor is not None:
                front, rest = front * factor, rest * factor
            halo[pl.ds(lon, direct, stride=LON), :] = front
            halo[pl.ds(direct * LON + lon, folded, stride=LON), :] = rest

    for copy in e_lon:
        copy.wait_recv()
    unpack(e_recv, halo_e, None, None)
    pl.semaphore_wait(near_sem, 4)
    for peer in z_peers:
        tell(ring_sem, {"grid": peer})

    backward = lax.rem(spec, 2) == 1

    def advect_band(index, total):
        band = jnp.where(backward, BANDS - 1 - index, index)
        block = rows_of(e_ref, band)
        lon_step, lat_step = upwind(block, rows_of(halo_e, band))
        speed = speed_coef * inverse(band + REACH)
        along_x = jnp.abs(rows_of(cos_ref, 0)) * secant
        along_y = jnp.abs(rows_of(sin_ref, 0))
        moved = (block - speed * (along_x * lon_step + along_y * lat_step)) * mask
        keep(band + REACH, moved)
        bands_16[band] = moved.reshape(BAND_ROWS, LAT).astype(BF16)
        return total + 0.1 * ratio(band + REACH) * jnp.sum(moved, axis=0)

    def band_copy(start, recv, index, to):
        return pltpu.make_async_remote_copy(
            src_ref=bands_16.at[pl.ds(start, REACH)],
            dst_ref=recv,
            send_sem=band_send.at[index],
            recv_sem=band_recv.at[index],
            device_id={"spec": to},
            device_id_type=MESH,
        )

    upward = band_copy(BANDS - REACH, low_halo, 0, lax.rem(spec + 1, specs))
    downward = band_copy(0, high_halo, 1, lax.rem(spec + specs - 1, specs))
    total = lax.fori_loop(0, REACH, advect_band, jnp.zeros((8, LAT), F32))

    @pl.when((spec > 0) & ~backward)
    def _():
        downward.start()

    @pl.when((spec < specs - 1) & backward)
    def _():
        upward.start()

    part[...] = lax.fori_loop(REACH, BANDS, advect_band, total)

    @pl.when((spec > 0) & backward)
    def _():
        downward.start()

    @pl.when((spec < specs - 1) & ~backward)
    def _():
        upward.start()

    sums = []
    for i in range(1, specs):
        sums.append(
            pltpu.make_async_remote_copy(
                src_ref=part,
                dst_ref=parts.at[i],
                send_sem=sum_send.at[i],
                recv_sem=sum_recv.at[i],
                device_id={"spec": lax.rem(spec + i, specs)},
                device_id_type=MESH,
            )
        )
    for copy in sums:
        copy.start()


    for copy in n_lon:
        copy.start()

    chunk = 6

    def product(centre, upper, lower):
        return centre * (centre * (upper + lower) - 2.0 * upper * lower)

    def own_terms(here, at, band):
        terms = [product(here, at(odd, 2, (3 * s - 1) // 2), at(odd, -3, (-s - 1) // 2)) for s in (1, -1)]
        return (-2.0 * nonlin_coef * ratio(band + REACH)) * (terms[0] + terms[1])

    def below_terms(here, at, band):
        terms = [product(at(odd, -2, (-3 * s - 1) // 2), here, at(even, -5, -2 * s)) for s in (1, -1)]
        return (nonlin_coef * ratio(band + REACH - 2)) * (terms[0] + terms[1])

    def above_terms(here, at, band):
        terms = [product(at(odd, 3, (s - 1) // 2), at(even, 5, 2 * s), here) for s in (1, -1)]
        return (nonlin_coef * ratio(band + REACH + 3)) * (terms[0] + terms[1])

    def add_terms(begin, end, kinds, opening, damped):
        def step(band, carry):
            if damped:
                loss = ratio(band + REACH)
                inverse_loss = (1.0 / (1.0 + dissip_coef * loss * loss * damped[0]))[None]
            for piece in range(PAIRS // chunk):
                base = 2 + piece * chunk

                def at(ref, offset, turn):
                    return ref[band + REACH + offset, pl.ds(base + turn, chunk)]

                here = at(even, 0, 0)
                rows = pl.ds(pl.multiple_of(band * BAND_ROWS + piece * chunk * 8, 8), chunk * 8)
                if opening:
                    total = here * (1.0 + ratio(band + REACH) * gain[pl.ds(piece * chunk, chunk)])
                else:
                    total = g_buf[rows, :].reshape(chunk, 8, LAT)
                for kind in kinds:
                    total += kind(here, at, band)
                if damped:
                    total *= inverse_loss
                g_buf[rows, :] = total.reshape(chunk * 8, LAT)
            return carry

        lax.fori_loop(begin, end, step, 0)

    add_terms(0, 3, (above_terms,), True, ())
    add_terms(3, 4, (own_terms, above_terms), True, ())
    add_terms(4, 5, (own_terms,), True, ())
    add_terms(5, 7, (own_terms, below_terms), True, ())
    add_terms(7, 9, (below_terms,), True, ())

    for copy in sums:
        copy.wait_recv()
    whole = part[...] + parts[1] + parts[2] + parts[3]
    mean = (whole + pltpu.roll(whole, 4, axis=0)) * MEAN_SCALE

    @pl.when(spec < specs - 1)
    def _():
        downward.wait_recv()

    @pl.when(spec > 0)
    def _():
        upward.wait_recv()

    def halo_bands(band, carry):
        low = low_halo[band].astype(F32).reshape(pair_shape)
        keep(band, jnp.where(spec > 0, low, 0.0))
        high = high_halo[band].astype(F32).reshape(pair_shape)
        keep(band + BANDS + REACH, jnp.where(spec < specs - 1, high, 0.0))
        return carry

    lax.fori_loop(0, REACH, halo_bands, 0)

    def column_copy(start, rows, index):
        return pltpu.make_async_remote_copy(
            src_ref=col_send.at[pl.ds(start, rows)],
            dst_ref=col_recv.at[pl.ds(start, rows)],
            send_sem=col_ssem.at[index],
            recv_sem=col_rsem.at[index],
            device_id={"grid": west},
            device_id_type=MESH,
        )

    columns = [column_copy(0, FIRST_ROWS, 0), column_copy(FIRST_ROWS, EAST - FIRST_ROWS, 1)]
    g_buf[pl.ds(ROWS, WIDTH * LON - ROWS), :] = jnp.zeros((WIDTH * LON - ROWS, LAT), F32)
    col_recv[pl.ds(EAST, WIDTH - EAST), :] = jnp.zeros((WIDTH - EAST, LAT), BF16)
    add_terms(0, 3, (own_terms, below_terms), False, (mean,))
    add_terms(3, 4, (below_terms,), False, (mean,))
    col_send[pl.ds(0, FIRST_ROWS), :] = g_buf[pl.ds(0, FIRST_ROWS, stride=LON), :].astype(BF16)
    columns[0].start()
    add_terms(4, 5, (below_terms, above_terms), False, (mean,))
    add_terms(5, 7, (above_terms,), False, (mean,))
    add_terms(7, 9, (own_terms, above_terms), False, (mean,))
    col_send[pl.ds(FIRST_ROWS, EAST - FIRST_ROWS), :] = g_buf[
        pl.ds(FIRST_ROWS * LON, EAST - FIRST_ROWS, stride=LON), :
    ].astype(BF16)
    columns[1].start()
    pl.semaphore_wait(ring_sem, RING - 1)
    tell(half_sem, {"grid": x_peer})

    packed = jnp.zeros((2 * RIM, WIDTH), F32)
    for lon in range(LON):
        high, low = split_16(g_buf[pl.ds(lon, WIDTH, stride=LON), :])
        packed += dot_nt(share_high[lon], high)
        packed += dot_nt(share_high[lon], low)
        packed += dot_nt(share_low[lon], high)
    for copy in columns:
        copy.wait_recv()
    packed += dot_nt(share_high[LON], col_recv[...])
    packed += dot_nt(share_low[LON], col_recv[...])
    for c in range(3):
        lanes = packed[:, c * LAT : (c + 1) * LAT]
        if c == 2:
            lanes += facts[...]
        lanes = lanes.astype(BF16)
        blocks[c] = lanes.reshape(count, 2, LAT)

    own_block = pltpu.make_async_copy(blocks.at[:, me], arrived.at[:, me], rim_recv)
    own_block.start()

    pl.semaphore_wait(half_sem, 1)
    for z, x, y in far_first():
        dest = place_of(
            turned_by(z_part, z, RING), 1 - x_part if x else x_part, turned_by(y_part, y, RING)
        )
        pltpu.make_async_remote_copy(
            src_ref=blocks.at[:, dest],
            dst_ref=arrived.at[:, me],
            send_sem=rim_send,
            recv_sem=rim_recv,
            device_id={"grid": dest},
            device_id_type=MESH,
        ).start()
    g_out[...] = g_buf[pl.ds(0, ROWS), :]
    quarter = count // 4
    lower_keep = jnp.where((me != quarter) & (me != 3 * quarter), 1.0, 0.0)
    upper_keep = jnp.where((me != quarter - 1) & (me != 3 * quarter - 1), 1.0, 0.0)
    for copy in n_lon:
        copy.wait_recv()
    unpack(n_recv, halo_n, lower_keep, upper_keep)

    def advect_nest(band, carry):
        block = rows_of(n_ref, band)
        lon_step, lat_step = upwind(block, rows_of(halo_n, band))
        speed = nest_speedup * speed_coef * inverse(band + REACH)
        along_x = jnp.abs(rows_of(cos_ref, 0))
        along_y = jnp.abs(rows_of(sin_ref, 0))
        moved = block - speed * (along_x * lon_step + along_y * lat_step)
        nest[pl.ds(pl.multiple_of(band * BAND_ROWS, 8), BAND_ROWS), :] = moved.reshape(BAND_ROWS, LAT)
        return carry

    lax.fori_loop(0, BANDS, advect_nest, 0)

    for copy in e_lon + n_lon + sums + columns:
        copy.wait_send()

    @pl.when(spec < specs - 1)
    def _():
        upward.wait_send()

    @pl.when(spec > 0)
    def _():
        downward.wait_send()

    others = blocks.at[:, pl.ds(0, count - 1)]
    pltpu.make_async_copy(others, others, rim_send).wait()
    pltpu.make_async_copy(arrived, arrived, rim_recv).wait()


def settle(arrived, nest, g_next, g_out, n_out, n_buf, out_sem):
    g_copy = pltpu.make_async_copy(g_next, g_out, out_sem.at[0])
    g_copy.start()
    spectra = jnp.concatenate([arrived[c].reshape(2 * RIM, LAT) for c in range(3)], axis=1)
    told = spectra[:, 256:].astype(F32)
    cell = told[:, FACT : FACT + 1] * float(LAT) + told[:, FACT + 1 : FACT + 2]
    cells = lax.broadcasted_iota(jnp.int32, (2 * RIM, LON * LAT), 1).astype(F32)
    hit = cell == cells
    rate_high = jnp.where(hit, told[:, FACT + 2 : FACT + 3], 0.0)
    rate_low = jnp.where(hit, told[:, FACT + 3 : FACT + 4], 0.0)
    remains = 1.0 - jnp.sum(rate_high + rate_low, axis=0, keepdims=True)
    turned = spectra.T
    gained = jnp.dot(turned, rate_high.astype(BF16), preferred_element_type=F32)
    gained += jnp.dot(turned, rate_low.astype(BF16), preferred_element_type=F32)
    for lon in range(LON):
        lanes = slice(lon * LAT, (lon + 1) * LAT)
        held = nest[pl.ds(lon, BINS, stride=LON), :]
        n_buf[pl.ds(lon, BINS, stride=LON), :] = held * remains[:, lanes] + gained[:BINS, lanes]
    n_copy = pltpu.make_async_copy(n_buf.at[pl.ds(0, ROWS)], n_out, out_sem.at[1])
    n_copy.start()
    g_copy.wait()
    n_copy.wait()


def per_device(
    energy, nest_energy, ocean_mask, wind_field, rim_cell, rim_dest, rim_target, rim_weight
):
    count = lax.axis_size("grid")
    cosine, sine, secant, scalars = tables()
    vmem = pl.BlockSpec(memory_space=pltpu.VMEM)
    flat = jax.ShapeDtypeStruct((ROWS, LAT), F32)
    dma = pltpu.SemaphoreType.DMA

    def body(*refs):
        kernel(count, *refs)

    global_rows, nest_rows, arrived = pl.pallas_call(
        body,
        out_shape=(flat, jax.ShapeDtypeStruct((ROOM, LAT), F32), jax.ShapeDtypeStruct((3, count, 2, LAT), BF16)),
        in_specs=[pl.BlockSpec(memory_space=pltpu.HBM)] * 12,
        out_specs=(vmem, vmem, vmem),
        scratch_shapes=[
            pltpu.VMEM((ROWS, LAT), F32),
            pltpu.VMEM((ROWS, LAT), F32),
            pltpu.VMEM((LON, LAT), jnp.int32),
            pltpu.VMEM((2, LON, LAT), F32),
            pltpu.VMEM((2, RIM), jnp.int32),
            pltpu.VMEM((1, RIM), jnp.int32),
            pltpu.VMEM((1, RIM), jnp.int32),
            pltpu.VMEM((3, RIM), F32),
            pltpu.VMEM((BAND_ROWS, LAT), F32),
            pltpu.VMEM((BAND_ROWS, LAT), F32),
            pltpu.VMEM((8, LAT), F32),
            pltpu.SMEM((128,), F32),
            pltpu.VMEM((RIM, RIM), F32),
            pltpu.VMEM((PACKET, LAT), F32),
            pltpu.VMEM((PACKET, LAT), F32),
            pltpu.VMEM((2, PACKET, LAT), BF16),
            pltpu.VMEM((2, PACKET, LAT), BF16),
            pltpu.VMEM((2, PACKET, LAT), BF16),
            pltpu.VMEM((2, PACKET, LAT), BF16),
            pltpu.VMEM((ROWS, LAT), F32),
            pltpu.VMEM((ROWS, LAT), F32),
            pltpu.VMEM((BANDS + 2 * REACH, PAIRS + 4, 8, LAT), F32),
            pltpu.VMEM((BANDS + 2 * REACH, PAIRS + 4, 8, LAT), F32),
            pltpu.VMEM((BANDS, BAND_ROWS, LAT), BF16),
            pltpu.VMEM((REACH, BAND_ROWS, LAT), BF16),
            pltpu.VMEM((REACH, BAND_ROWS, LAT), BF16),
            pltpu.VMEM((PAIRS, 8, LAT), F32),
            pltpu.VMEM((WIDTH * LON, LAT), F32),
            pltpu.VMEM((8, LAT), F32),
            pltpu.VMEM((4, 8, LAT), F32),
            pltpu.VMEM((WIDTH, LAT), BF16),
            pltpu.VMEM((WIDTH, LAT), BF16),
            pltpu.VMEM((LON + 1, 2 * RIM, LAT), BF16),
            pltpu.VMEM((LON + 1, 2 * RIM, LAT), BF16),
            pltpu.VMEM((2 * RIM, LAT), F32),
            pltpu.VMEM((3, count, 2, LAT), BF16),
            dma((12,)),
            dma((4,)),
            dma((4,)),
            dma((2,)),
            dma((2,)),
            dma((4,)),
            dma((4,)),
            dma((2,)),
            dma((2,)),
            dma,
            dma,
            pltpu.SemaphoreType.REGULAR,
            pltpu.SemaphoreType.REGULAR,
            pltpu.SemaphoreType.REGULAR,
        ],
        compiler_params=pltpu.CompilerParams(
            collective_id=0, has_side_effects=True, vmem_limit_bytes=40 << 20
        ),
        name="wave_step",
    )(
        *(
            pltpu.with_memory_space_constraint(x, pltpu.HBM)
            for x in (
                energy.reshape(ROWS, LAT),
                nest_energy.reshape(ROWS, LAT),
                ocean_mask,
                wind_field,
                rim_cell.T,
                rim_dest.T,
                rim_target.reshape(1, RIM),
                rim_weight.T,
                jnp.asarray(cosine),
                jnp.asarray(sine),
                jnp.asarray(secant),
                jnp.asarray(scalars),
            )
        )
    )
    hbm = pl.BlockSpec(memory_space=pl.ANY)
    global_next, nest_next = pl.pallas_call(
        settle,
        out_shape=(flat, flat),
        in_specs=[vmem] * 3,
        out_specs=(hbm, hbm),
        scratch_shapes=[
            pltpu.VMEM((ROOM, LAT), F32),
            dma((2,)),
        ],
        compiler_params=pltpu.CompilerParams(vmem_limit_bytes=SETTLE_LIMIT),
        name="settle",
    )(arrived, nest_rows, global_rows)
    shape = energy.shape
    return (global_next.reshape(shape), nest_next.reshape(shape))


def solution(mesh):
    in_specs = (
        P("spec", None, "grid", None),
        P("spec", None, "grid", None),
        P("grid", None),
        P(None, "grid", None),
        P("grid", None),
        P("grid", None),
        P("grid"),
        P("grid", None),
    )
    out_specs = (P("spec", None, "grid", None), P("spec", None, "grid", None))
    return jax.shard_map(
        per_device, mesh=mesh, in_specs=in_specs, out_specs=out_specs, check_vma=False
    )
```

```python
import jax
import jax.numpy as jnp
import numpy as np
from jax import lax
from jax.experimental import pallas as pl
from jax.experimental.pallas import tpu as pltpu
from jax.sharding import PartitionSpec as P

FREQS = 36
ANGLES = 36
LON = 4
LAT = 128
RIM = 128
BANDS = 9
REACH = 5
BINS = BANDS * ANGLES
ROWS = BINS * LON
BAND_ROWS = ANGLES * LON
PAIRS = BAND_ROWS // 8
PACKET = 192
FIRST_ROWS = 144
EAST = 336
RING = 8
SETTLE_LIMIT = 16 << 20
WIDTH = 384
ROOM = 8 * -(-BINS // 8) * LON
FACT = BINS - 256
MESH = pl.DeviceIdType.MESH
F32 = jnp.float32
BF16 = jnp.bfloat16

ratio_step = 1.1
speed_coef = 0.054
wind_coef = 0.05
dissip_coef = 0.2
nonlin_coef = 0.12
nest_speedup = 2.0


def tables():
    heading = 2.0 * np.pi * np.arange(ANGLES) / ANGLES
    cosine, sine = np.cos(heading), np.sin(heading)
    cosine[[9, 27]] = 0.0
    sine[[0, 18]] = 0.0

    def spread(x):
        rows = np.repeat(x, LON)
        return np.broadcast_to(rows[:, None], (BAND_ROWS, LAT)).astype(np.float32)

    degrees = -60.0 + 120.0 * (np.arange(LAT) + 0.5) / LAT
    secant = np.broadcast_to(1.0 / np.cos(degrees * np.pi / 180.0), (8, LAT)).astype(np.float32)
    bands = np.arange(-REACH, FREQS + REACH)
    ratio = ratio_step ** (bands - FREQS // 2).astype(np.float64)
    scalars = np.zeros((128,), np.float32)
    scalars[: 2 * ratio.size] = np.concatenate([ratio, 1.0 / ratio])
    return spread(cosine), spread(sine), secant, scalars


RATIO_COUNT = FREQS + 2 * REACH
MEAN_SCALE = float(
    1.0 / (ANGLES * 0.1 * np.sum(ratio_step ** (np.arange(FREQS) - FREQS // 2.0)))
)


def dot_nt(a, b):
    return lax.dot_general(a, b, (((1,), (1,)), ((), ())), preferred_element_type=F32)


def split_16(x):
    high = x.astype(BF16)
    return high, (x - high.astype(F32)).astype(BF16)


def far_first():
    def hops(step):
        z, x, y = step
        return min(z, RING - z) + 2 * x + min(y, RING - y)

    steps = [(z, x, y) for z in range(RING) for x in range(2) for y in range(RING)]
    return sorted(steps[1:], key=lambda step: -hops(step))


def kernel(
    count,
    e_hbm,
    n_hbm,
    mask_hbm,
    wind_hbm,
    cell_hbm,
    dest_hbm,
    target_hbm,
    weight_hbm,
    cos_hbm,
    sin_hbm,
    sec_hbm,
    scalar_hbm,
    g_out,
    nest,
    arrived,
    e_ref,
    n_ref,
    mask_ref,
    wind_ref,
    cell_ref,
    dest_ref,
    target_ref,
    weight_ref,
    cos_ref,
    sin_ref,
    sec_ref,
    scalar_ref,
    rim_rows,
    stage_a,
    stage_b,
    e_send,
    n_send,
    e_recv,
    n_recv,
    halo_e,
    halo_n,
    even,
    odd,
    bands_16,
    low_halo,
    high_halo,
    gain,
    g_buf,
    part,
    parts,
    col_send,
    col_recv,
    share_high,
    share_low,
    facts,
    blocks,
    in_sem,
    lon_send,
    lon_recv,
    band_send,
    band_recv,
    sum_send,
    sum_recv,
    col_ssem,
    col_rsem,
    rim_send,
    rim_recv,
    near_sem,
    ring_sem,
    half_sem,
):
    sources = (
        e_hbm, n_hbm, scalar_hbm, mask_hbm, cos_hbm, sin_hbm, sec_hbm, wind_hbm,
        cell_hbm, dest_hbm, target_hbm, weight_hbm,
    )
    places = (
        e_ref, n_ref, scalar_ref, mask_ref, cos_ref, sin_ref, sec_ref, wind_ref,
        cell_ref, dest_ref, target_ref, weight_ref,
    )
    loads = [
        pltpu.make_async_copy(source, place, in_sem.at[i])
        for i, (source, place) in enumerate(zip(sources, places))
    ]
    loads[0].start()
    loads[1].start()
    me = lax.axis_index("grid")
    spec = lax.axis_index("spec")
    specs = FREQS // BANDS
    first = spec * BANDS
    west = lax.rem(me + count - 1, count)
    east = lax.rem(me + 1, count)
    barrier = pltpu.get_barrier_semaphore()

    def ratio(band):
        return scalar_ref[first + band]

    def inverse(band):
        return scalar_ref[first + band + RATIO_COUNT]

    z_part = me // (2 * RING)
    x_part = lax.rem(me // RING, 2)
    y_part = lax.rem(me, RING)

    def place_of(z, x, y):
        return (z * 2 + x) * RING + y

    def turned_by(part, step, size):
        return lax.rem(part + step, size) if step else part

    def tell(sem, to):
        pl.semaphore_signal(sem, inc=1, device_id=to, device_id_type=MESH)

    tell(barrier, {"grid": west})
    tell(barrier, {"grid": east})
    for i in range(1, specs):
        tell(barrier, {"spec": lax.rem(spec + i, specs)})
    z_peers = [place_of(turned_by(z_part, i, RING), x_part, y_part) for i in range(1, RING)]
    x_peer = place_of(z_part, 1 - x_part, y_part)
    near = (1, RING - 1, 2, RING - 2)
    y_near = [place_of(z_part, x_part, turned_by(y_part, i, RING)) for i in near]
    z_near = [z_peers[i - 1] for i in near]
    for peer in y_near + z_near:
        tell(barrier, {"grid": peer})
    tell(barrier, {"grid": x_peer})
    for load in loads[2:]:
        load.start()

    packet_rows = lax.broadcasted_iota(jnp.int32, (PACKET, LAT), 0)
    angle = lax.rem(packet_rows, ANGLES)
    eastward = (angle < 10) | (angle >= 28)
    stage_a[...] = jnp.zeros_like(stage_a)
    stage_b[...] = jnp.zeros_like(stage_b)
    direct = 5 * ANGLES
    folded = BINS - direct

    def pack(source, send):
        for index, lon, picked in ((0, LON - 1, eastward), (1, 0, ~eastward)):
            stage_a[pl.ds(0, direct), :] = source[pl.ds(lon, direct, stride=LON), :]
            stage_b[pl.ds(18, folded), :] = source[pl.ds(direct * LON + lon, folded, stride=LON), :]
            send[index] = jnp.where(picked, stage_a[...], stage_b[...]).astype(BF16)

    loads[0].wait()
    pack(e_ref, e_send)
    pl.semaphore_wait(barrier, 2 + specs - 1 + 2 * len(near) + 1)

    def lon_copies(send, recv, base):
        return [
            pltpu.make_async_remote_copy(
                src_ref=send.at[index],
                dst_ref=recv.at[index],
                send_sem=lon_send.at[base + index],
                recv_sem=lon_recv.at[base + index],
                device_id={"grid": to},
                device_id_type=MESH,
            )
            for index, to in ((0, east), (1, west))
        ]

    e_lon = lon_copies(e_send, e_recv, 0)
    n_lon = lon_copies(n_send, n_recv, 2)
    for copy in e_lon:
        copy.start()
    for peer in y_near[2:] + z_near[2:]:
        tell(near_sem, {"grid": peer})
    for load in loads[2:]:
        load.wait()
    loads[1].wait()
    pack(n_ref, n_send)

    lane = lax.broadcasted_iota(jnp.int32, (RIM, LAT), 1)
    sub = lax.broadcasted_iota(jnp.int32, (RIM, LAT), 0)
    rim_rows[...] = jnp.zeros_like(rim_rows)
    rim_rows[pl.ds(0, 2), :] = cell_ref[...].astype(F32)
    rim_rows[pl.ds(2, 1), :] = dest_ref[...].astype(F32)
    rim_rows[pl.ds(3, 1), :] = target_ref[...].astype(F32)
    rim_rows[pl.ds(4, 3), :] = weight_ref[...]
    rim_cols = rim_rows[...].T
    local_col = rim_cols[:, 0:1].astype(jnp.int32) - me * LON
    row = rim_cols[:, 1:2].astype(jnp.int32)
    dest_col = rim_cols[:, 2:3]
    target_col = rim_cols[:, 3:4].astype(jnp.int32)
    ex = rim_cols[:, 4:5]
    ny = rim_cols[:, 5:6]
    relax = rim_cols[:, 6:7]
    row_share = jnp.where(lane == row, 1.0 - ny, jnp.where(lane == row + 1, ny, 0.0))
    shares = []
    for lon in range(LON + 1):
        col_share = jnp.where(
            local_col == lon, 1.0 - ex, jnp.where(local_col == lon - 1, ex, 0.0)
        )
        high, low = split_16(col_share * row_share)
        shares.append((high, low))
    dest_row = dest_ref[...].astype(F32)
    same = dest_col == dest_row
    slot_row = jnp.sum(jnp.where(same & (sub < lane), 1.0, 0.0), axis=0, keepdims=True)
    places = lax.broadcasted_iota(jnp.int32, (2 * RIM, LAT), 0)
    named = (dest_row == (places >> 1).astype(F32)) & (slot_row == (places & 1).astype(F32))
    hot = jnp.where(named, 1.0, 0.0).astype(BF16)
    relax_high = relax.astype(BF16).astype(F32)
    fact = jnp.where(lane == FACT, (target_col >> 7).astype(F32), 0.0)
    fact = jnp.where(lane == FACT + 1, (target_col & 127).astype(F32), fact)
    fact = jnp.where(lane == FACT + 2, relax_high, fact)
    fact = jnp.where(lane == FACT + 3, relax - relax_high, fact)
    facts[...] = jnp.dot(hot, fact.astype(BF16), preferred_element_type=F32)
    for lon, (high, low) in enumerate(shares):
        share_high[lon] = jnp.dot(hot, high, preferred_element_type=F32).astype(BF16)
        share_low[lon] = jnp.dot(hot, low, preferred_element_type=F32).astype(BF16)
    pair_shape = (PAIRS, 8, LAT)
    cosine = cos_ref[...].reshape(pair_shape)
    sine = sin_ref[...].reshape(pair_shape)
    wind = wind_ref[...]
    wind_x = jnp.concatenate([wind[0], wind[0]], axis=0)[None]
    wind_y = jnp.concatenate([wind[1], wind[1]], axis=0)[None]
    gain[...] = wind_coef * jnp.maximum(wind_x * cosine + wind_y * sine, 0.0)
    mask_half = mask_ref[...].astype(F32)
    mask = jnp.concatenate([mask_half, mask_half], axis=0)[None]
    secant = sec_ref[...][None]

    vreg_sub = lax.broadcasted_iota(jnp.int32, (1, 8, LAT), 1)
    vreg_lane = lax.broadcasted_iota(jnp.int32, (1, 8, LAT), 2)
    lon_of = vreg_sub & 3

    def upwind(block, halo):
        before = jnp.where(lon_of == 0, halo, pltpu.roll(block, 1, axis=1))
        after = jnp.where(lon_of == LON - 1, halo, pltpu.roll(block, 7, axis=1))
        along_lon = jnp.concatenate([before[:5], after[5:14], before[14:]], axis=0)
        south = jnp.where(vreg_lane == 0, 0.0, pltpu.roll(block, 1, axis=2))
        north = jnp.where(vreg_lane == LAT - 1, 0.0, pltpu.roll(block, LAT - 1, axis=2))
        along_lat = jnp.concatenate([south[:9], north[9:]], axis=0)
        return block - along_lon, block - along_lat

    def rows_of(ref, band):
        return ref[pl.ds(pl.multiple_of(band * BAND_ROWS, 8), BAND_ROWS), :].reshape(pair_shape)

    def cyclic(ref, band, value):
        ref[band, pl.ds(2, PAIRS)] = value
        ref[band, pl.ds(0, 2)] = value[PAIRS - 2 :]
        ref[band, pl.ds(PAIRS + 2, 2)] = value[:2]

    def keep(band, value):
        cyclic(even, band, value)
        turned = pltpu.roll(value, 4, axis=1)
        following = jnp.concatenate([turned[1:], turned[:1]], axis=0)
        cyclic(odd, band, jnp.where(vreg_sub < 4, turned, following))

    def unpack(recv, halo, lower, upper):
        for index, lon, factor in ((0, 0, lower), (1, LON - 1, upper)):
            stage_a[...] = recv[index].astype(F32)
            front = stage_a[pl.ds(0, direct), :]
            rest = stage_a[pl.ds(18, folded), :]
            if factor is not None:
                front, rest = front * factor, rest * factor
            halo[pl.ds(lon, direct, stride=LON), :] = front
            halo[pl.ds(direct * LON + lon, folded, stride=LON), :] = rest

    for copy in e_lon:
        copy.wait_recv()
    unpack(e_recv, halo_e, None, None)
    pl.semaphore_wait(near_sem, 4)
    for peer in z_peers:
        tell(ring_sem, {"grid": peer})

    backward = lax.rem(spec, 2) == 1

    def advect_band(index, total):
        band = jnp.where(backward, BANDS - 1 - index, index)
        block = rows_of(e_ref, band)
        lon_step, lat_step = upwind(block, rows_of(halo_e, band))
        speed = speed_coef * inverse(band + REACH)
        along_x = jnp.abs(rows_of(cos_ref, 0)) * secant
        along_y = jnp.abs(rows_of(sin_ref, 0))
        moved = (block - speed * (along_x * lon_step + along_y * lat_step)) * mask
        keep(band + REACH, moved)
        bands_16[band] = moved.reshape(BAND_ROWS, LAT).astype(BF16)
        return total + 0.1 * ratio(band + REACH) * jnp.sum(moved, axis=0)

    def band_copy(start, recv, index, to):
        return pltpu.make_async_remote_copy(
            src_ref=bands_16.at[pl.ds(start, REACH)],
            dst_ref=recv,
            send_sem=band_send.at[index],
            recv_sem=band_recv.at[index],
            device_id={"spec": to},
            device_id_type=MESH,
        )

    upward = band_copy(BANDS - REACH, low_halo, 0, lax.rem(spec + 1, specs))
    downward = band_copy(0, high_halo, 1, lax.rem(spec + specs - 1, specs))
    total = lax.fori_loop(0, REACH, advect_band, jnp.zeros((8, LAT), F32))

    @pl.when((spec > 0) & ~backward)
    def _():
        downward.start()

    @pl.when((spec < specs - 1) & backward)
    def _():
        upward.start()

    part[...] = lax.fori_loop(REACH, BANDS, advect_band, total)

    @pl.when((spec > 0) & backward)
    def _():
        downward.start()

    @pl.when((spec < specs - 1) & ~backward)
    def _():
        upward.start()

    sums = []
    for i in range(1, specs):
        sums.append(
            pltpu.make_async_remote_copy(
                src_ref=part,
                dst_ref=parts.at[i],
                send_sem=sum_send.at[i],
                recv_sem=sum_recv.at[i],
                device_id={"spec": lax.rem(spec + i, specs)},
                device_id_type=MESH,
            )
        )
    for copy in sums:
        copy.start()


    chunk = 6

    def product(centre, upper, lower):
        return centre * (centre * (upper + lower) - 2.0 * upper * lower)

    def own_terms(here, at, band):
        terms = [product(here, at(odd, 2, (3 * s - 1) // 2), at(odd, -3, (-s - 1) // 2)) for s in (1, -1)]
        return (-2.0 * nonlin_coef * ratio(band + REACH)) * (terms[0] + terms[1])

    def below_terms(here, at, band):
        terms = [product(at(odd, -2, (-3 * s - 1) // 2), here, at(even, -5, -2 * s)) for s in (1, -1)]
        return (nonlin_coef * ratio(band + REACH - 2)) * (terms[0] + terms[1])

    def above_terms(here, at, band):
        terms = [product(at(odd, 3, (s - 1) // 2), at(even, 5, 2 * s), here) for s in (1, -1)]
        return (nonlin_coef * ratio(band + REACH + 3)) * (terms[0] + terms[1])

    def add_terms(begin, end, kinds, opening, damped):
        def step(band, carry):
            if damped:
                loss = ratio(band + REACH)
                inverse_loss = (1.0 / (1.0 + dissip_coef * loss * loss * damped[0]))[None]
            for piece in range(PAIRS // chunk):
                base = 2 + piece * chunk

                def at(ref, offset, turn):
                    return ref[band + REACH + offset, pl.ds(base + turn, chunk)]

                here = at(even, 0, 0)
                rows = pl.ds(pl.multiple_of(band * BAND_ROWS + piece * chunk * 8, 8), chunk * 8)
                if opening:
                    total = here * (1.0 + ratio(band + REACH) * gain[pl.ds(piece * chunk, chunk)])
                else:
                    total = g_buf[rows, :].reshape(chunk, 8, LAT)
                for kind in kinds:
                    total += kind(here, at, band)
                if damped:
                    total *= inverse_loss
                g_buf[rows, :] = total.reshape(chunk * 8, LAT)
            return carry

        lax.fori_loop(begin, end, step, 0)

    add_terms(0, 3, (above_terms,), True, ())
    add_terms(3, 4, (own_terms, above_terms), True, ())
    add_terms(4, 5, (own_terms,), True, ())
    add_terms(5, 7, (own_terms, below_terms), True, ())
    add_terms(7, 9, (below_terms,), True, ())

    for copy in sums:
        copy.wait_recv()
    whole = part[...] + parts[1] + parts[2] + parts[3]
    mean = (whole + pltpu.roll(whole, 4, axis=0)) * MEAN_SCALE

    @pl.when(spec < specs - 1)
    def _():
        downward.wait_recv()

    @pl.when(spec > 0)
    def _():
        upward.wait_recv()

    def halo_bands(band, carry):
        low = low_halo[band].astype(F32).reshape(pair_shape)
        keep(band, jnp.where(spec > 0, low, 0.0))
        high = high_halo[band].astype(F32).reshape(pair_shape)
        keep(band + BANDS + REACH, jnp.where(spec < specs - 1, high, 0.0))
        return carry

    lax.fori_loop(0, REACH, halo_bands, 0)

    def column_copy(start, rows, index):
        return pltpu.make_async_remote_copy(
            src_ref=col_send.at[pl.ds(start, rows)],
            dst_ref=col_recv.at[pl.ds(start, rows)],
            send_sem=col_ssem.at[index],
            recv_sem=col_rsem.at[index],
            device_id={"grid": west},
            device_id_type=MESH,
        )

    columns = [column_copy(0, FIRST_ROWS, 0), column_copy(FIRST_ROWS, EAST - FIRST_ROWS, 1)]
    g_buf[pl.ds(ROWS, WIDTH * LON - ROWS), :] = jnp.zeros((WIDTH * LON - ROWS, LAT), F32)
    col_recv[pl.ds(EAST, WIDTH - EAST), :] = jnp.zeros((WIDTH - EAST, LAT), BF16)
    add_terms(0, 3, (own_terms, below_terms), False, (mean,))
    add_terms(3, 4, (below_terms,), False, (mean,))
    col_send[pl.ds(0, FIRST_ROWS), :] = g_buf[pl.ds(0, FIRST_ROWS, stride=LON), :].astype(BF16)
    columns[0].start()
    add_terms(4, 5, (below_terms, above_terms), False, (mean,))
    add_terms(5, 7, (above_terms,), False, (mean,))
    add_terms(7, 9, (own_terms, above_terms), False, (mean,))
    col_send[pl.ds(FIRST_ROWS, EAST - FIRST_ROWS), :] = g_buf[
        pl.ds(FIRST_ROWS * LON, EAST - FIRST_ROWS, stride=LON), :
    ].astype(BF16)
    columns[1].start()
    for copy in n_lon:
        copy.start()
    pl.semaphore_wait(ring_sem, RING - 1)
    tell(half_sem, {"grid": x_peer})

    packed = jnp.zeros((2 * RIM, WIDTH), F32)
    for lon in range(LON):
        high, low = split_16(g_buf[pl.ds(lon, WIDTH, stride=LON), :])
        packed += dot_nt(share_high[lon], high)
        packed += dot_nt(share_high[lon], low)
        packed += dot_nt(share_low[lon], high)
    for copy in columns:
        copy.wait_recv()
    packed += dot_nt(share_high[LON], col_recv[...])
    packed += dot_nt(share_low[LON], col_recv[...])
    for c in range(3):
        lanes = packed[:, c * LAT : (c + 1) * LAT]
        if c == 2:
            lanes += facts[...]
        lanes = lanes.astype(BF16)
        blocks[c] = lanes.reshape(count, 2, LAT)

    own_block = pltpu.make_async_copy(blocks.at[:, me], arrived.at[:, me], rim_recv)
    own_block.start()

    pl.semaphore_wait(half_sem, 1)
    for z, x, y in far_first():
        dest = place_of(
            turned_by(z_part, z, RING), 1 - x_part if x else x_part, turned_by(y_part, y, RING)
        )
        pltpu.make_async_remote_copy(
            src_ref=blocks.at[:, dest],
            dst_ref=arrived.at[:, me],
            send_sem=rim_send,
            recv_sem=rim_recv,
            device_id={"grid": dest},
            device_id_type=MESH,
        ).start()
    g_out[...] = g_buf[pl.ds(0, ROWS), :]
    quarter = count // 4
    lower_keep = jnp.where((me != quarter) & (me != 3 * quarter), 1.0, 0.0)
    upper_keep = jnp.where((me != quarter - 1) & (me != 3 * quarter - 1), 1.0, 0.0)
    for copy in n_lon:
        copy.wait_recv()
    unpack(n_recv, halo_n, lower_keep, upper_keep)

    def advect_nest(band, carry):
        block = rows_of(n_ref, band)
        lon_step, lat_step = upwind(block, rows_of(halo_n, band))
        speed = nest_speedup * speed_coef * inverse(band + REACH)
        along_x = jnp.abs(rows_of(cos_ref, 0))
        along_y = jnp.abs(rows_of(sin_ref, 0))
        moved = block - speed * (along_x * lon_step + along_y * lat_step)
        nest[pl.ds(pl.multiple_of(band * BAND_ROWS, 8), BAND_ROWS), :] = moved.reshape(BAND_ROWS, LAT)
        return carry

    lax.fori_loop(0, BANDS, advect_nest, 0)

    for copy in e_lon + n_lon + sums + columns:
        copy.wait_send()

    @pl.when(spec < specs - 1)
    def _():
        upward.wait_send()

    @pl.when(spec > 0)
    def _():
        downward.wait_send()

    others = blocks.at[:, pl.ds(0, count - 1)]
    pltpu.make_async_copy(others, others, rim_send).wait()
    pltpu.make_async_copy(arrived, arrived, rim_recv).wait()


def settle(arrived, nest, g_next, g_out, n_out, n_buf, out_sem):
    g_copy = pltpu.make_async_copy(g_next, g_out, out_sem.at[0])
    g_copy.start()
    spectra = jnp.concatenate([arrived[c].reshape(2 * RIM, LAT) for c in range(3)], axis=1)
    told = spectra[:, 256:].astype(F32)
    cell = told[:, FACT : FACT + 1] * float(LAT) + told[:, FACT + 1 : FACT + 2]
    cells = lax.broadcasted_iota(jnp.int32, (2 * RIM, LON * LAT), 1).astype(F32)
    hit = cell == cells
    rate_high = jnp.where(hit, told[:, FACT + 2 : FACT + 3], 0.0)
    rate_low = jnp.where(hit, told[:, FACT + 3 : FACT + 4], 0.0)
    remains = 1.0 - jnp.sum(rate_high + rate_low, axis=0, keepdims=True)
    turned = spectra.T
    gained = jnp.dot(turned, rate_high.astype(BF16), preferred_element_type=F32)
    gained += jnp.dot(turned, rate_low.astype(BF16), preferred_element_type=F32)
    for lon in range(LON):
        lanes = slice(lon * LAT, (lon + 1) * LAT)
        held = nest[pl.ds(lon, BINS, stride=LON), :]
        n_buf[pl.ds(lon, BINS, stride=LON), :] = held * remains[:, lanes] + gained[:BINS, lanes]
    n_copy = pltpu.make_async_copy(n_buf.at[pl.ds(0, ROWS)], n_out, out_sem.at[1])
    n_copy.start()
    g_copy.wait()
    n_copy.wait()


def per_device(
    energy, nest_energy, ocean_mask, wind_field, rim_cell, rim_dest, rim_target, rim_weight
):
    count = lax.axis_size("grid")
    cosine, sine, secant, scalars = tables()
    vmem = pl.BlockSpec(memory_space=pltpu.VMEM)
    flat = jax.ShapeDtypeStruct((ROWS, LAT), F32)
    dma = pltpu.SemaphoreType.DMA

    def body(*refs):
        kernel(count, *refs)

    global_rows, nest_rows, arrived = pl.pallas_call(
        body,
        out_shape=(flat, jax.ShapeDtypeStruct((ROOM, LAT), F32), jax.ShapeDtypeStruct((3, count, 2, LAT), BF16)),
        in_specs=[pl.BlockSpec(memory_space=pltpu.HBM)] * 12,
        out_specs=(vmem, vmem, vmem),
        scratch_shapes=[
            pltpu.VMEM((ROWS, LAT), F32),
            pltpu.VMEM((ROWS, LAT), F32),
            pltpu.VMEM((LON, LAT), jnp.int32),
            pltpu.VMEM((2, LON, LAT), F32),
            pltpu.VMEM((2, RIM), jnp.int32),
            pltpu.VMEM((1, RIM), jnp.int32),
            pltpu.VMEM((1, RIM), jnp.int32),
            pltpu.VMEM((3, RIM), F32),
            pltpu.VMEM((BAND_ROWS, LAT), F32),
            pltpu.VMEM((BAND_ROWS, LAT), F32),
            pltpu.VMEM((8, LAT), F32),
            pltpu.SMEM((128,), F32),
            pltpu.VMEM((RIM, RIM), F32),
            pltpu.VMEM((PACKET, LAT), F32),
            pltpu.VMEM((PACKET, LAT), F32),
            pltpu.VMEM((2, PACKET, LAT), BF16),
            pltpu.VMEM((2, PACKET, LAT), BF16),
            pltpu.VMEM((2, PACKET, LAT), BF16),
            pltpu.VMEM((2, PACKET, LAT), BF16),
            pltpu.VMEM((ROWS, LAT), F32),
            pltpu.VMEM((ROWS, LAT), F32),
            pltpu.VMEM((BANDS + 2 * REACH, PAIRS + 4, 8, LAT), F32),
            pltpu.VMEM((BANDS + 2 * REACH, PAIRS + 4, 8, LAT), F32),
            pltpu.VMEM((BANDS, BAND_ROWS, LAT), BF16),
            pltpu.VMEM((REACH, BAND_ROWS, LAT), BF16),
            pltpu.VMEM((REACH, BAND_ROWS, LAT), BF16),
            pltpu.VMEM((PAIRS, 8, LAT), F32),
            pltpu.VMEM((WIDTH * LON, LAT), F32),
            pltpu.VMEM((8, LAT), F32),
            pltpu.VMEM((4, 8, LAT), F32),
            pltpu.VMEM((WIDTH, LAT), BF16),
            pltpu.VMEM((WIDTH, LAT), BF16),
            pltpu.VMEM((LON + 1, 2 * RIM, LAT), BF16),
            pltpu.VMEM((LON + 1, 2 * RIM, LAT), BF16),
            pltpu.VMEM((2 * RIM, LAT), F32),
            pltpu.VMEM((3, count, 2, LAT), BF16),
            dma((12,)),
            dma((4,)),
            dma((4,)),
            dma((2,)),
            dma((2,)),
            dma((4,)),
            dma((4,)),
            dma((2,)),
            dma((2,)),
            dma,
            dma,
            pltpu.SemaphoreType.REGULAR,
            pltpu.SemaphoreType.REGULAR,
            pltpu.SemaphoreType.REGULAR,
        ],
        compiler_params=pltpu.CompilerParams(
            collective_id=0, has_side_effects=True, vmem_limit_bytes=40 << 20
        ),
        name="wave_step",
    )(
        *(
            pltpu.with_memory_space_constraint(x, pltpu.HBM)
            for x in (
                energy.reshape(ROWS, LAT),
                nest_energy.reshape(ROWS, LAT),
                ocean_mask,
                wind_field,
                rim_cell.T,
                rim_dest.T,
                rim_target.reshape(1, RIM),
                rim_weight.T,
                jnp.asarray(cosine),
                jnp.asarray(sine),
                jnp.asarray(secant),
                jnp.asarray(scalars),
            )
        )
    )
    hbm = pl.BlockSpec(memory_space=pl.ANY)
    global_next, nest_next = pl.pallas_call(
        settle,
        out_shape=(flat, flat),
        in_specs=[vmem] * 3,
        out_specs=(hbm, hbm),
        scratch_shapes=[
            pltpu.VMEM((ROOM, LAT), F32),
            dma((2,)),
        ],
        compiler_params=pltpu.CompilerParams(vmem_limit_bytes=SETTLE_LIMIT),
        name="settle",
    )(arrived, nest_rows, global_rows)
    shape = energy.shape
    return (global_next.reshape(shape), nest_next.reshape(shape))


def solution(mesh):
    in_specs = (
        P("spec", None, "grid", None),
        P("spec", None, "grid", None),
        P("grid", None),
        P(None, "grid", None),
        P("grid", None),
        P("grid", None),
        P("grid"),
        P("grid", None),
    )
    out_specs = (P("spec", None, "grid", None), P("spec", None, "grid", None))
    return jax.shard_map(
        per_device, mesh=mesh, in_specs=in_specs, out_specs=out_specs, check_vma=False
    )
```
